32 devices in a mesh: comp: 2 (over x), row: 4 (over y, core), col: 4 (over z).
Axes of the slice: x: 2, y: 2, z: 4, core: 2. Of those that a mesh axis runs over, the one named last changes fastest.
Arguments:
- model_state: float32 [2, 1280, 32, 512], P('comp', 'row', None, 'col'), may hold values from -6 to 6
- legendre: bfloat16 [32, 1280, 1280], P('row'), may hold values from -0.15625 to 0.15625
- gauss_weight: float32 [1280], P('row'), may hold values from 0.5 to 1.5
- mixing: float32 [32, 32], replicated, may hold values from -1 to 1
- surface: float32 [2, 1280, 512], P('comp', 'row', 'col'), may hold values from -6 to 6
- sea_count: int32 [2, 1280, 4], P('comp', 'row', 'col'), may hold values from 0 to 128, as said below
- remap_source: int32 [2, 1280, 512], P('comp', 'row', 'col'), may hold values from 0 to 40959
Outputs:
- new_state: float32 [2, 1280, 32, 512], P('comp', 'row', None, 'col')
- new_surface: float32 [2, 1280, 512], P('comp', 'row', 'col')
The draws below stay inside these ranges and needn't reach their ends.
Inputs may be any that keep to these rules, and one draw needn't show every extreme that they name: `sea_count`: the sea cells of a tile row are its first ones, of 128. `remap_source`: an entry counts row-major within a tile of 320 rows and 128 columns.
All inputs are finite; a program needn't handle non-finite values.
Results may differ from the reference program's by a relative error of at most 0.0043.
Values may be sent and summed in bfloat16 or wider, within the bound.
No kernel may reach another device: no remote copies, remote signals or barrier semaphores. Data moves between devices by JAX's collectives and lax.ppermute only.
A program may use at most 128 MiB of HBM per device.

```python
import jax
import jax.numpy as jnp
from jax import lax

ROWS = 1280
NWAVE = 1280
WAVES = 32
COL_DEV = 128
LAT_DEV = 320
COLS = 512
N_ROW = 4
N_COL = 4


def draw_sea_count(key, part):
    toss_key = jax.random.fold_in(key, 11)
    count_key = jax.random.fold_in(key, 12)
    coin_toss = jax.random.randint(toss_key, (2, ROWS, N_COL), 0, 16)
    partial_count = jax.random.randint(count_key, (2, ROWS, N_COL), 0, COL_DEV + 1)
    return jnp.where(coin_toss < 15, COL_DEV, partial_count).astype(jnp.int32)


def place_ends(array, key, low, high):
    longest = array.shape.index(max(array.shape))
    spots = []
    for shift in (0, 1):
        where = [jax.random.randint(jax.random.fold_in(key, axis), (), 0, length) for axis, length in enumerate(array.shape)]
        where[longest] = (where[longest] + shift) % array.shape[longest]
        spots.append(tuple(where))
    return array.at[spots[0]].set(low).at[spots[1]].set(high)


def block_levels(rng, dims, shards, least, largest):
    def one(dim, shards_of):
        heights = jax.random.uniform(jax.random.fold_in(jax.random.fold_in(rng, 6), dim), (shards_of,), jnp.float32, least / len(shards), largest / len(shards))
        return jnp.repeat(jnp.exp(heights), dims[dim] // shards_of).reshape((-1,) + (1,) * (len(dims) - dim - 1))

    loudness = one(*shards[0])
    for cut in shards[1:]:
        loudness = loudness * one(*cut)
    return loudness


def gaussian(own_key, shape, width, reach, pieces=(), dtype=jnp.bfloat16):
    drawn = width * jax.random.normal(own_key, shape, jnp.float32)
    if pieces:
        drawn = drawn * block_levels(own_key, shape, pieces, -0.22, 0.18)
    return jnp.clip(drawn, -reach, reach).astype(dtype)


def setup_inputs(seed: int = 0) -> dict:
    splits = jax.random.split(jax.random.key(seed), 8)
    return {
        "model_state": gaussian(splits[0], (2, ROWS, WAVES, COLS), 1.0, 6.0, ((0, 2), (1, 4), (3, 4)), jnp.float32),
        "legendre": gaussian(splits[1], (WAVES, ROWS, NWAVE), ROWS ** -0.5, 0.15625, ((0, 4),)),
        "gauss_weight": jnp.clip(0.5 + 1.0 * jax.random.uniform(splits[2], (ROWS,), jnp.float32) ** block_levels(splits[2], (ROWS,), ((0, 4),), -0.2, 0.2), 0.5, 1.5),
        "mixing": gaussian(splits[3], (WAVES, WAVES), WAVES ** -0.5, 1.0, (), jnp.float32),
        "surface": gaussian(splits[4], (2, ROWS, COLS), 1.0, 6.0, ((0, 2), (1, 4), (2, 4)), jnp.float32),
        "sea_count": draw_sea_count(jax.random.fold_in(splits[7], 71), 0),
        "remap_source": place_ends(jax.random.randint(splits[6], (2, ROWS, COLS), 0, LAT_DEV * COL_DEV), jax.random.fold_in(splits[6], 1), 0, (LAT_DEV * COL_DEV) - 1).astype(jnp.int32),
    }


def damping_rows(wave_count, nwave_count):
    total_wave = (jnp.arange(wave_count)[:, None] + jnp.arange(nwave_count)[None, :]).astype(jnp.float32)
    wave_ratio = total_wave * (total_wave + 1.0) / (1279.0 * 1280.0)
    return 1.0 / (1.0 + 20.0 * wave_ratio * wave_ratio)


def atmosphere(fourier, gauss_weight, legendre):
    weighted = (gauss_weight[:, None, None] * fourier).astype(jnp.bfloat16)
    damping = damping_rows(WAVES, NWAVE)

    def one_wave(spectral_mode):
        legendre_rows = legendre[spectral_mode]
        column = lax.dynamic_index_in_dim(weighted, spectral_mode, 1, keepdims=False)
        spectral = jnp.dot(legendre_rows.T, column, preferred_element_type=jnp.float32)
        filtered = (damping[spectral_mode][:, None] * spectral).astype(jnp.bfloat16)
        return jnp.dot(legendre_rows, filtered, preferred_element_type=jnp.float32).astype(jnp.bfloat16)

    synthesized = lax.map(one_wave, jnp.arange(WAVES).astype(jnp.int32))
    return jnp.transpose(synthesized, (1, 0, 2)).astype(jnp.float32)


def laplace(field):
    padded = jnp.pad(field, ((1, 1), (1, 1)))
    centre = padded[1:-1, 1:-1]
    return padded[2:, 1:-1] + padded[:-2, 1:-1] + padded[1:-1, 2:] + padded[1:-1, :-2] - 4.0 * centre


def diffuse(level_field, water_mask):
    first_step = level_field + 0.2 * water_mask * laplace(water_mask * level_field)
    return first_step + 0.2 * water_mask * laplace(water_mask * first_step)


def advance_ocean(heat_level, mixing, water_mask):
    blended_field = heat_level + water_mask[:, None, :] * jnp.einsum("do,eot->edt", mixing, heat_level, precision=lax.Precision.HIGHEST)

    def one_level(level_index):
        return diffuse(lax.dynamic_index_in_dim(blended_field, level_index, 1, keepdims=False), water_mask)

    levels = lax.map(one_level, jnp.arange(WAVES).astype(jnp.int32))
    return jnp.transpose(levels, (1, 0, 2))


def sea_cells(counts):
    position = jnp.arange(COLS) % COL_DEV
    block_index = jnp.arange(COLS) // COL_DEV
    return (position[None, :] < counts[:, block_index]).astype(jnp.float32)


def split_into_patches(field):
    return field.reshape(N_ROW, LAT_DEV, N_COL, COL_DEV).transpose(0, 2, 1, 3).reshape(N_ROW, N_COL, LAT_DEV * COL_DEV)


def pull_partner(other, source):
    pulled = jnp.take_along_axis(split_into_patches(other), split_into_patches(source), axis=2)
    return pulled.reshape(N_ROW, N_COL, LAT_DEV, COL_DEV).transpose(0, 2, 1, 3).reshape(ROWS, COLS)


def reference(model_state, legendre, gauss_weight, mixing, surface, sea_count, remap_source):
    sea_air = sea_cells(sea_count[0])
    sea_ocean = sea_cells(sea_count[1])
    synthesized = atmosphere(model_state[0], gauss_weight, legendre)
    ocean_state = advance_ocean(model_state[1], mixing, sea_ocean)
    gap_air = sea_air * (pull_partner(surface[1], remap_source[0]) - surface[0])
    gap_ocean = sea_ocean * (pull_partner(surface[0], remap_source[1]) - surface[1])
    new_surface = jnp.stack([surface[0] + 0.5 * gap_air, surface[1] + 0.25 * gap_ocean])
    ocean_state = ocean_state.at[:, 0, :].add(0.3 * gap_ocean)
    new_state = jnp.stack([synthesized, ocean_state])
    return new_state, new_surface
```

```python
import functools

import jax
import jax.numpy as jnp
from jax import lax
from jax.experimental import pallas as pl
from jax.experimental.pallas import tpu as pltpu
from jax.sharding import PartitionSpec as P

diffusion_rate = 0.2
lanes = 128


def row_block(rows):
    return 64 if rows % 64 == 0 else rows


def lane_index(shape=(8, lanes)):
    return lax.broadcasted_iota(jnp.int32, shape, len(shape) - 1)


def cost(flops, bytes_accessed):
    return pl.CostEstimate(flops=flops, bytes_accessed=bytes_accessed, transcendentals=0)


def entry_kernel(ids, counts, field, last, gauss, mix, send, mixed, edge, *, n_row, chunks, block, groups):
    levels = field.shape[0] // block
    width = levels // n_row // chunks
    step = pl.program_id(0)
    wide = groups * levels

    @pl.when(ids[0] == 0)
    def _():
        for wave in range(levels):
            dest, local = divmod(wave, levels // n_row)
            chunk, slot = divmod(local, width)
            values = field[pl.ds(wave, block, stride=levels), :] * gauss[...]
            send[chunk][dest, slot] = values.astype(jnp.bfloat16)

    def mixed_rows(ref, start, first_row):
        heat = ref[pl.ds(start, wide), :]
        blend = jnp.dot(mix[...], heat, precision=lax.Precision.HIGHEST, preferred_element_type=jnp.float32)
        out = []
        for s in range(groups):
            sea = lane_index((levels, lanes)) < counts[first_row + s]
            part = slice(levels * s, levels * (s + 1))
            out.append((heat[part] + jnp.where(sea, blend[part], 0.0), sea))
        return out

    @pl.when(ids[0] != 0)
    def _():
        def body(g, packed):
            start = pl.multiple_of(g * wide, wide)
            for s, (value, sea) in enumerate(mixed_rows(field, start, step * block + g * groups)):
                mixed[pl.ds(pl.multiple_of(start + s * levels, levels), levels), :] = value
                packed = pack_edge(packed, jnp.where(sea, value, 0.0), g * groups + s)
            return packed

        packed = lax.fori_loop(0, block // groups, body, jnp.zeros((levels, lanes), jnp.float32))
        for c in range(edge.shape[0]):
            edge[c, 0] = packed.astype(jnp.bfloat16)

        @pl.when(step == 0)
        def _():
            total = pl.num_programs(0) * block
            top, top_sea = mixed_rows(field, 0, 0)[0]
            low, low_sea = mixed_rows(last, 0, total - groups)[-1]
            top = jnp.where(top_sea, top, 0.0).astype(jnp.bfloat16)
            low = jnp.where(low_sea, low, 0.0).astype(jnp.bfloat16)
            for dest in range(n_row):
                send[0][dest, 0, 0:levels, :] = jnp.where(dest > ids[1], low, top)


def pack_edge(packed, sea_value, y):
    lane = lane_index(packed.shape)
    shift = (2 * y + 1) % lanes
    moved = pltpu.roll(sea_value, shift, 1)
    return jnp.where((lane == 2 * y) | (lane == 2 * y + 1), moved, packed)


def sweep_kernel(ids, counts, field, above, below, halo_up, halo_down, east_in, west_in, *rest,
                 block, n_row, n_col, final):
    if final:
        gap, out = rest
    else:
        out, edge, ends = rest
    levels = field.shape[0] // block
    step = pl.program_id(0)
    steps = pl.num_programs(0)
    rows = steps * block

    @pl.when(ids[0] != 0)
    def _():
        shape = (levels, lanes)
        lane = lane_index(shape)
        first = lane == 0
        final_lane = lane == lanes - 1

        def sea_of(y):
            return lane < counts[jnp.clip(y, 0, rows - 1)]

        west = jnp.where(ids[2] > 0, west_in[0, 0].astype(jnp.float32), 0.0)
        east = jnp.where(ids[2] < n_col - 1, east_in[0, 0].astype(jnp.float32), 0.0)
        sides = jnp.where(lane % 2 == 0, pltpu.roll(east, lanes - 1, 1), pltpu.roll(west, 1, 1))
        base = step * block
        up0 = jnp.where(step > 0, jnp.where(sea_of(base - 1), above[...], 0.0),
                        jnp.where(ids[1] > 0, halo_up[0, 0].astype(jnp.float32), 0.0))
        down_end = jnp.where(step < steps - 1, jnp.where(sea_of(base + block), below[...], 0.0),
                             jnp.where(ids[1] < n_row - 1, halo_down[0, 0].astype(jnp.float32), 0.0))

        def one(y, up, here, value, down, packed):
            turned = pltpu.roll(sides, (lanes - 1 - 2 * y) % lanes, 1)
            left = jnp.where(first, turned, pltpu.roll(here, 1, 1))
            right = jnp.where(final_lane, turned, pltpu.roll(here, lanes - 1, 1))
            sea = sea_of(base + y)
            lap = up + down + left + right - 4.0 * here
            new = value + jnp.where(sea, diffusion_rate * lap, 0.0)
            out[pl.ds(pl.multiple_of(y * levels, levels), levels), :] = new
            if final:
                here_row = out[pl.ds(y * levels, 1), :]
                out[pl.ds(y * levels, 1), :] = here_row + 0.3 * gap[pl.ds(y, 1), :]
                return packed, None
            masked = jnp.where(sea, new, 0.0)
            return pack_edge(packed, masked, y), masked

        def masked_row(y):
            value = field[pl.ds(pl.multiple_of(y * levels, levels), levels), :]
            return value, jnp.where(sea_of(base + y), value, 0.0)

        def body(y, carry):
            up, here, value, packed = carry
            down_value, down = masked_row(y + 1)
            packed, _ = one(y, up, here, value, down, packed)
            return here, down, down_value, packed

        value0, here0 = masked_row(0)
        packed0 = jnp.zeros(shape, jnp.float32)
        up, here, value, packed = lax.fori_loop(0, block - 1, body, (up0, here0, value0, packed0), unroll=3)
        packed, _ = one(block - 1, up, here, value, down_end, packed)
        if not final:
            for c in range(edge.shape[0]):
                edge[c, 0] = packed.astype(jnp.bfloat16)

            @pl.when(step == 0)
            def _():
                ends[0] = jnp.where(sea_of(0), out[0:levels, :], 0.0).astype(jnp.bfloat16)

            @pl.when(step == steps - 1)
            def _():
                ends[1] = jnp.where(
                    sea_of(rows - 1), out[pl.ds((block - 1) * levels, levels), :], 0.0
                ).astype(jnp.bfloat16)


def legendre_kernel(ids, legendre, coeffs, *rest, n_row, wave_dev, first_wave, with_ends):
    if with_ends:
        ends, out = rest
    else:
        (out,) = rest
    index = pl.program_id(0)
    lats = coeffs.shape[2]
    count = legendre.shape[2]

    @pl.when(ids[0] == 0)
    def _():
        table = legendre[0]
        fourier = coeffs[:, 0].reshape(n_row * lats, lanes)
        spectral = lax.dot_general(fourier, table, (((0,), (0,)), ((), ())), preferred_element_type=jnp.float32)
        wave = ids[1] * wave_dev + first_wave + index
        total = (wave + lax.broadcasted_iota(jnp.int32, (1, count), 1)).astype(jnp.float32)
        ratio = total * (total + 1.0) / (1279.0 * 1280.0)
        damping = 1.0 / (1.0 + 20.0 * ratio * ratio)
        filtered = (spectral * damping).astype(jnp.bfloat16)
        result = lax.dot_general(table, filtered, (((1,), (1,)), ((), ())), preferred_element_type=jnp.float32)
        out[:, 0] = result.astype(jnp.bfloat16).reshape(n_row, lats, lanes)

    if with_ends:
        @pl.when((ids[0] != 0) & (index == 0))
        def _():
            levels = ends.shape[1]
            for dest in range(n_row):
                out[dest, 0, 0:levels, :] = jnp.where(dest > ids[1], ends[1], ends[0])


def surface_kernel(ids, counts, partner, own, source, new, gap, *, group):
    rows = partner.shape[0]
    half = rows // 2
    width = 2 * lanes
    table = jnp.concatenate(
        [partner[pl.ds(0, half, stride=2), :], partner[pl.ds(1, half, stride=2), :]], axis=1
    )
    coarse = table.astype(jnp.bfloat16)
    fine = (table - coarse.astype(jnp.float32)).astype(jnp.bfloat16)
    low_index = lax.broadcasted_iota(jnp.int32, (width, lanes), 0)
    high_index = lax.broadcasted_iota(jnp.int32, (half, lanes), 0)
    one = jnp.ones((width, lanes), jnp.bfloat16)
    zero = jnp.zeros((width, lanes), jnp.bfloat16)
    sublane = lax.broadcasted_iota(jnp.int32, (8, lanes), 0)
    rate = jnp.where(ids[0] == 0, 0.5, 0.25).astype(jnp.float32)

    def body(g, carry):
        start = pl.multiple_of(g * 8, 8)
        entries = source[pl.ds(start, 8), :]
        low = entries & (width - 1)
        high = entries >> 8
        found = []
        for p in range(0, 8, group):
            pick = jnp.concatenate(
                [jnp.where(low_index == low[s:s + 1, :], one, zero) for s in range(p, p + group)], axis=1
            )
            picked = jnp.dot(coarse, pick, preferred_element_type=jnp.float32)
            picked = picked + jnp.dot(fine, pick, preferred_element_type=jnp.float32)
            for s in range(group):
                part = picked[:, lanes * s:lanes * (s + 1)]
                match = high_index == high[p + s:p + s + 1, :]
                found.append(jnp.sum(jnp.where(match, part, 0.0), axis=0, keepdims=True))
        pulled = jnp.concatenate(found, axis=0)
        limit = jnp.zeros((8, lanes), jnp.int32)
        for s in range(8):
            limit = jnp.where(sublane == s, counts[start + s], limit)
        here = own[pl.ds(start, 8), :]
        difference = jnp.where(lane_index() < limit, pulled - here, 0.0)
        new[pl.ds(start, 8), :] = here + rate * difference
        gap[pl.ds(start, 8), :] = difference
        return carry

    lax.fori_loop(0, rows // 8, body, 0)


def exit_kernel(ids, sea, *rest, n_row, chunks, block):
    back, out = rest[:chunks], rest[chunks]
    levels = out.shape[0] // block
    width = levels // n_row // chunks

    @pl.when(ids[0] == 0)
    def _():
        for wave in range(levels):
            origin, local = divmod(wave, levels // n_row)
            chunk, slot = divmod(local, width)
            out[pl.ds(wave, block, stride=levels), :] = back[chunk][origin, slot].astype(jnp.float32)

    @pl.when(ids[0] != 0)
    def _():
        out[...] = sea[...]


def entry_body(*refs, chunks, **kw):
    ids, counts, field, last, gauss, mix = refs[:6]
    send = refs[6:6 + chunks]
    mixed, edge = refs[6 + chunks:]
    entry_kernel(ids, counts, field, last, gauss, mix, send, mixed, edge, chunks=chunks, **kw)


def shards(model_state, legendre, gauss_weight, mixing, surface, sea_count, remap_source):
    n_row, n_col = lax.axis_size("row"), lax.axis_size("col")
    rows, levels = model_state.shape[1], model_state.shape[2]
    wave_dev = levels // n_row
    chunks = 2 if wave_dev % 2 == 0 else 1
    width = wave_dev // chunks
    block = row_block(rows)
    steps = rows // block
    groups = 8
    f32, bf16 = jnp.float32, jnp.bfloat16
    sds = jax.ShapeDtypeStruct

    fields = model_state.reshape(rows * levels, lanes)
    counts = sea_count.reshape(rows)
    ids = jnp.stack([lax.axis_index("comp"), lax.axis_index("row"), lax.axis_index("col")]).astype(jnp.int32)
    own = surface[0]
    comp_size = lax.axis_size("comp")
    partner = lax.ppermute(own, "comp", [(i, comp_size - 1 - i) for i in range(comp_size)])

    gauss = jnp.broadcast_to(gauss_weight[:, None], (rows, lanes))
    stacked = jnp.kron(jnp.eye(groups, dtype=f32), mixing)

    def on(comp, i, s):
        return jnp.where(s[0] == comp, i, 0)

    *send, mixed, edge = pl.pallas_call(
        functools.partial(entry_body, n_row=n_row, chunks=chunks, block=block, groups=groups),
        out_shape=[sds((n_row, width, rows, lanes), bf16)] * chunks
        + [sds((rows * levels, lanes), f32), sds((n_col, steps, levels, lanes), bf16)],
        grid_spec=pltpu.PrefetchScalarGridSpec(
            num_scalar_prefetch=2, grid=(steps,),
            in_specs=[
                pl.BlockSpec((block * levels, lanes), lambda i, s, c: (i, 0)),
                pl.BlockSpec((groups * levels, lanes), lambda i, s, c: (rows // groups - 1, 0)),
                pl.BlockSpec((block, lanes), lambda i, s, c: (i, 0)),
                pl.BlockSpec((groups * levels, groups * levels), lambda i, s, c: (0, 0)),
            ],
            out_specs=[pl.BlockSpec((n_row, width, block, lanes), lambda i, s, c: (0, 0, i, 0))] * chunks
            + [
                pl.BlockSpec((block * levels, lanes), lambda i, s, c: (on(1, i, s), 0)),
                pl.BlockSpec((n_col, 1, levels, lanes), lambda i, s, c: (0, i, 0, 0)),
            ],
        ),
        name="entry",
        cost_estimate=cost(10**7, 4 * rows * levels * lanes * 2),
    )(ids, counts, fields, fields, gauss, stacked)

    def to_waves(x):
        return lax.all_to_all(x, "row", split_axis=0, concat_axis=0, tiled=True)

    def to_columns(x):
        return lax.all_to_all(x, "col", split_axis=0, concat_axis=0, tiled=True)

    coeffs = [to_waves(x) for x in send]
    sides = to_columns(edge)

    new_surface, gap = pl.pallas_call(
        functools.partial(surface_kernel, group=2),
        out_shape=[sds((rows, lanes), f32)] * 2,
        grid_spec=pltpu.PrefetchScalarGridSpec(
            num_scalar_prefetch=2, grid=(1,),
            in_specs=[pl.BlockSpec((rows, lanes), lambda i, s, c: (0, 0))] * 3,
            out_specs=[pl.BlockSpec((rows, lanes), lambda i, s, c: (0, 0))] * 2,
        ),
        name="surface",
        cost_estimate=cost(10**10, 5 * 4 * rows * lanes),
    )(ids, counts, partner, own, remap_source[0])

    def sweep(field, rows_in, cols_in, final, extra=()):
        out_shape = [sds((rows * levels, lanes), f32)]
        out_specs = [pl.BlockSpec((block * levels, lanes), lambda i, s, c: (on(1, i, s), 0))]
        if not final:
            out_shape += [sds((n_col, steps, levels, lanes), bf16), sds((2, levels, lanes), bf16)]
            out_specs += [
                pl.BlockSpec((n_col, 1, levels, lanes), lambda i, s, c: (0, i, 0, 0)),
                pl.BlockSpec((2, levels, lanes), lambda i, s, c: (0, 0, 0)),
            ]
        return pl.pallas_call(
            functools.partial(sweep_kernel, block=block, n_row=n_row, n_col=n_col, final=final),
            out_shape=out_shape,
            grid_spec=pltpu.PrefetchScalarGridSpec(
                num_scalar_prefetch=2, grid=(steps,),
                in_specs=[
                    pl.BlockSpec((block * levels, lanes), lambda i, s, c: (on(1, i, s), 0)),
                    pl.BlockSpec((levels, lanes), lambda i, s, c: (jnp.maximum(on(1, i, s) * block - 1, 0), 0)),
                    pl.BlockSpec((levels, lanes),
                                 lambda i, s, c: (jnp.minimum((on(1, i, s) + 1) * block, rows - 1), 0)),
                    pl.BlockSpec((1, 1, levels, lanes), lambda i, s, c: (jnp.maximum(s[1] - 1, 0), 0, 0, 0)),
                    pl.BlockSpec((1, 1, levels, lanes), lambda i, s, c: (jnp.minimum(s[1] + 1, n_row - 1), 0, 0, 0)),
                    pl.BlockSpec((1, 1, levels, lanes),
                                 lambda i, s, c: (jnp.minimum(s[2] + 1, n_col - 1), i, 0, 0)),
                    pl.BlockSpec((1, 1, levels, lanes), lambda i, s, c: (jnp.maximum(s[2] - 1, 0), i, 0, 0)),
                ] + ([pl.BlockSpec((block, lanes), lambda i, s, c: (i, 0))] if final else []),
                out_specs=out_specs,
            ),
            name="sweep_last" if final else "sweep",
            cost_estimate=cost(10**7, 4 * rows * levels * lanes * 2),
        )(ids, counts, field, field, field, rows_in, rows_in, cols_in, cols_in, *extra)

    first_step, edge, ends = sweep(mixed, coeffs[0], sides, False)
    sides = to_columns(edge)

    returned = []
    for chunk in range(chunks):
        with_ends = chunk == 0
        part = pl.pallas_call(
            functools.partial(legendre_kernel, n_row=n_row, wave_dev=wave_dev, first_wave=chunk * width,
                              with_ends=with_ends),
            out_shape=sds((n_row, width, rows, lanes), bf16),
            grid_spec=pltpu.PrefetchScalarGridSpec(
                num_scalar_prefetch=1, grid=(width,),
                in_specs=[
                    pl.BlockSpec((1,) + legendre.shape[1:],
                                 lambda i, s, chunk=chunk: (chunk * width + on(0, i, s), 0, 0)),
                    pl.BlockSpec((n_row, 1, rows, lanes), lambda i, s: (0, i, 0, 0)),
                ] + ([pl.BlockSpec((2, levels, lanes), lambda i, s: (0, 0, 0))] if with_ends else []),
                out_specs=pl.BlockSpec((n_row, 1, rows, lanes), lambda i, s: (0, i, 0, 0)),
            ),
            name=f"legendre_{chunk}",
            cost_estimate=cost(4 * width * legendre.shape[1] * legendre.shape[2] * lanes,
                               2 * width * legendre.shape[1] * legendre.shape[2]),
        )(ids, legendre, coeffs[chunk], *([ends] if with_ends else []))
        returned.append(to_waves(part))

    (sea,) = sweep(first_step, returned[0], sides, True, (gap,))

    state = pl.pallas_call(
        functools.partial(exit_body, n_row=n_row, chunks=chunks, block=block),
        out_shape=sds((rows * levels, lanes), f32),
        grid_spec=pltpu.PrefetchScalarGridSpec(
            num_scalar_prefetch=1, grid=(steps,),
            in_specs=[pl.BlockSpec((block * levels, lanes), lambda i, s: (on(1, i, s), 0))]
            + [pl.BlockSpec((n_row, width, block, lanes), lambda i, s: (0, 0, on(0, i, s), 0))] * chunks,
            out_specs=pl.BlockSpec((block * levels, lanes), lambda i, s: (i, 0)),
        ),
        name="exit",
        cost_estimate=cost(10**6, 6 * rows * levels * lanes),
    )(ids, sea, *returned)
    return state.reshape(model_state.shape), new_surface[None]


def exit_body(*refs, **kw):
    exit_kernel(*refs, **kw)


def solution(mesh):
    in_specs = (
        P("comp", "row", None, "col"),
        P("row", None, None),
        P("row"),
        P(),
        P("comp", "row", "col"),
        P("comp", "row", "col"),
        P("comp", "row", "col"),
    )
    out_specs = (P("comp", "row", None, "col"), P("comp", "row", "col"))
    return jax.shard_map(shards, mesh=mesh, in_specs=in_specs, out_specs=out_specs, check_vma=False)
```

```python
import functools

import jax
import jax.numpy as jnp
from jax import lax
from jax.experimental import pallas as pl
from jax.experimental.pallas import tpu as pltpu
from jax.sharding import PartitionSpec as P

diffusion_rate = 0.2
lanes = 128


def row_block(rows):
    return 64 if rows % 64 == 0 else rows


def cost(flops, bytes_accessed):
    return pl.CostEstimate(flops=flops, bytes_accessed=bytes_accessed, transcendentals=0)


def where_am_i(place, n_row, n_col):
    flat = place[0]
    return (
        lax.div(flat, n_row * n_col),
        lax.rem(lax.div(flat, n_col), n_row),
        lax.rem(flat, n_col),
    )


def iota(shape, dim):
    return lax.broadcasted_iota(jnp.int32, shape, dim)


def as_bf16(mask):
    return jnp.where(mask, 1.0, 0.0).astype(jnp.bfloat16)


def swap_matrix():
    row, column = iota((256, 256), 0), iota((256, 256), 1)
    return as_bf16(column == ((row & 15) << 4 | row >> 4))


def spread_matrix():
    row, column = iota((lanes, lanes), 0), iota((lanes, lanes), 1)
    odd = column & 1
    return as_bf16(((row == lanes - 1) & (odd == 0)) | ((row == 0) & (odd == 1)))


def beside_matrix():
    row, column = iota((lanes, lanes), 0), iota((lanes, lanes), 1)
    return as_bf16((row == column + 1) | (row + 1 == column))


def side_matrix():
    row, column = iota((lanes, lanes), 0), iota((lanes, lanes), 1)
    odd = row & 1
    return as_bf16(((column == 0) & (odd == 1)) | ((column == lanes - 1) & (odd == 0)))


def split(value):
    high = value.astype(jnp.bfloat16)
    return high, (value - high.astype(jnp.float32)).astype(jnp.bfloat16)


def product(a, b):
    return jnp.dot(a, b, preferred_element_type=jnp.float32)


def entry_kernel(place, counts, field, last, gauss, mix, *rest, n_row, n_col, chunks, block):
    send = rest[:chunks]
    mixed, edge, table = rest[chunks:]
    comp, row, _ = where_am_i(place, n_row, n_col)
    levels = field.shape[0] // block
    wave_dev = levels // n_row
    width = wave_dev // chunks
    step = pl.program_id(0)

    def target(wave):
        dest, local = divmod(wave, wave_dev)
        chunk, slot = divmod(local, width)
        return send[chunk], dest, slot

    @pl.when(comp == 0)
    def _():
        @pl.when(step == 0)
        def _():
            table[...] = swap_matrix()

        for lat in range(0, block - 15, 16):
            halves = []
            for half in range(0, levels, 16):
                halves.append(jnp.concatenate([
                    (field[(lat + s) * levels + half:(lat + s) * levels + half + 16, :]
                     * gauss[step * block + lat + s]).astype(jnp.bfloat16)
                    for s in range(16)
                ], axis=0))
            turned = product(table[...], jnp.concatenate(halves, axis=1)).astype(jnp.bfloat16)
            for wave in range(levels):
                out, dest, slot = target(wave)
                part = lanes * (wave // 16)
                out[dest, slot, lat:lat + 16, :] = turned[16 * (wave % 16):16 * (wave % 16) + 16, part:part + lanes]
        for lat in range(block - block % 16, block, 8):
            weight = jnp.zeros((8, lanes), jnp.float32)
            for s in range(8):
                weight = jnp.where(iota((8, lanes), 0) == s, gauss[step * block + lat + s], weight)
            for wave in range(levels):
                out, dest, slot = target(wave)
                values = field[pl.ds(lat * levels + wave, 8, stride=levels), :] * weight
                out[dest, slot, lat:lat + 8, :] = values.astype(jnp.bfloat16)

    def mixed_rows(ref, start, first_row):
        values = []
        for quarter in range(2):
            parts = []
            for pair in range(2):
                part = ref[pl.ds(start + (2 * quarter + pair) * 2 * levels, 2 * levels), :]
                values.append(part)
                parts.append(split(part))
            high = jnp.concatenate([p[0] for p in parts], axis=1)
            low = jnp.concatenate([p[1] for p in parts], axis=1)
            blend = product(table[0:2 * levels, :], jnp.concatenate([high, low, high, low], axis=0))
            values += [blend[:, :lanes], blend[:, lanes:]]
        out = []
        for s in range(8):
            quarter, pair, place_in = s // 4, s // 2 % 2, slice(levels * (s % 2), levels * (s % 2) + levels)
            heat = values[4 * quarter + pair][place_in]
            blend = values[4 * quarter + 2 + pair][place_in]
            sea = iota((levels, lanes), 1) < counts[0, first_row + s]
            value = heat + jnp.where(sea, blend, 0.0)
            out.append((value, jnp.where(sea, value, 0.0).astype(jnp.bfloat16)))
        return out

    @pl.when(comp != 0)
    def _():
        @pl.when(step == 0)
        def _():
            high, low = split(mix[...])
            repeat = as_bf16((iota((levels, 256), 1) & (levels - 1)) == iota((levels, 256), 0))
            wide = jnp.where(iota((levels, 256), 1) < 4 * levels, product(high, repeat), product(low, repeat))
            wide = jnp.concatenate([wide, wide], axis=0)
            shape = (2 * levels, 256)
            own = (iota(shape, 1) // levels & 1) == iota(shape, 0) // levels
            table[0:2 * levels, :] = jnp.where(own, wide, 0.0).astype(jnp.bfloat16)

        spread = spread_matrix()
        pair_of = iota((levels, lanes), 1) >> 1

        def body(g, packed):
            start = pl.multiple_of(g * 8 * levels, 8 * levels)
            rows = mixed_rows(field, start, step * block + g * 8)
            for s, (value, _) in enumerate(rows):
                mixed[pl.ds(pl.multiple_of(start + s * levels, levels), levels), :] = value
            ends = product(jnp.concatenate([r[1] for r in rows], axis=0), spread)
            for s in range(8):
                packed = jnp.where(pair_of == g * 8 + s, ends[s * levels:(s + 1) * levels], packed)
            return packed

        packed = lax.fori_loop(0, block // 8, body, jnp.zeros((levels, lanes), jnp.float32))
        edge[0] = packed.astype(jnp.bfloat16)

        @pl.when(step == 0)
        def _():
            total = pl.num_programs(0) * block
            top = mixed_rows(field, 0, 0)[0][1]
            low = mixed_rows(last, 0, total - 8)[-1][1]
            for dest in range(n_row):
                send[0][dest, 0, 0:levels, :] = jnp.where(dest > row, low, top)


def sweep_kernel(place, counts, field, above, below, halo_up, halo_down, east_in, west_in, *rest,
                 block, n_row, n_col, final):
    if final:
        gap, out, masked = rest
    else:
        out, edge, ends, masked = rest
    comp, row, col = where_am_i(place, n_row, n_col)
    levels = field.shape[0] // block
    step = pl.program_id(0)
    steps = pl.num_programs(0)
    rows = steps * block
    base = step * block
    shape = (levels, lanes)

    @pl.when(comp != 0)
    def _():
        lane = iota(shape, 1)
        pair_of = lane >> 1

        def sea_of(y):
            return lane < counts[0, jnp.clip(y, 0, rows - 1)]

        def at(y):
            return pl.ds(pl.multiple_of(y * levels, levels), levels)

        west = jnp.where(col > 0, west_in[0].astype(jnp.float32), 0.0)
        east = jnp.where(col < n_col - 1, east_in[0].astype(jnp.float32), 0.0)
        sides = jnp.where((lane & 1) == 0, pltpu.roll(east, lanes - 1, 1), pltpu.roll(west, 1, 1))
        masked[0:levels, :] = jnp.where(
            step > 0, jnp.where(sea_of(base - 1), above[...], 0.0),
            jnp.where(row > 0, halo_up[0, 0].astype(jnp.float32), 0.0))
        masked[(block + 1) * levels:(block + 2) * levels, :] = jnp.where(
            step < steps - 1, jnp.where(sea_of(base + block), below[...], 0.0),
            jnp.where(row < n_row - 1, halo_down[0, 0].astype(jnp.float32), 0.0))

        def fill(g, carry):
            for s in range(8):
                y = g * 8 + s
                masked[at(y + 1), :] = jnp.where(sea_of(base + y), field[at(y), :], 0.0)
            return carry

        lax.fori_loop(0, block // 8, fill, 0)
        beside = beside_matrix()
        if final:
            weights = jnp.concatenate([beside, side_matrix()], axis=0)
        else:
            spread = spread_matrix()

        def body(g, packed):
            here = masked[pl.ds(pl.multiple_of((g * 8 + 1) * levels, levels), 8 * levels), :]
            high, low = split(here)
            turned = jnp.concatenate(
                [jnp.where(pair_of == g * 8 + s, sides, 0.0).astype(jnp.bfloat16) for s in range(8)], axis=0)
            both = jnp.concatenate([beside, side_matrix()], axis=0) if not final else weights
            near = product(jnp.concatenate([high, turned], axis=1), both) + product(low, beside)
            new_rows = []
            for s in range(8):
                y = g * 8 + s
                part = slice(s * levels, (s + 1) * levels)
                lap = masked[at(y), :] + masked[at(y + 2), :] + near[part] - 4.0 * here[part]
                sea = sea_of(base + y)
                new = field[at(y), :] + jnp.where(sea, diffusion_rate * lap, 0.0)
                out[at(y), :] = new
                if final:
                    start = y * levels
                    out[pl.ds(start, 1), :] = new[0:1, :] + 0.3 * gap[pl.ds(y, 1), :]
                else:
                    new_rows.append(jnp.where(sea, new, 0.0).astype(jnp.bfloat16))
            if not final:
                spreads = product(jnp.concatenate(new_rows, axis=0), spread)
                for s in range(8):
                    packed = jnp.where(pair_of == g * 8 + s, spreads[s * levels:(s + 1) * levels], packed)
            return packed

        packed = lax.fori_loop(0, block // 8, body, jnp.zeros(shape, jnp.float32))
        if not final:
            edge[0] = packed.astype(jnp.bfloat16)

            @pl.when(step == 0)
            def _():
                ends[0] = jnp.where(sea_of(0), out[0:levels, :], 0.0).astype(jnp.bfloat16)

            @pl.when(step == steps - 1)
            def _():
                ends[1] = jnp.where(
                    sea_of(rows - 1), out[(block - 1) * levels:block * levels, :], 0.0
                ).astype(jnp.bfloat16)


def legendre_kernel(place, legendre, coeffs, *rest, n_row, n_col, wave_dev, first_wave, with_ends):
    if with_ends:
        ends, _, out = rest
    else:
        (out,) = rest
    comp, row, _ = where_am_i(place, n_row, n_col)
    index = pl.program_id(0)
    lats = coeffs.shape[2]
    count = legendre.shape[2]

    @pl.when(comp == 0)
    def _():
        table = legendre[0]
        fourier = coeffs[:, 0].reshape(n_row * lats, lanes)
        spectral = lax.dot_general(fourier, table, (((0,), (0,)), ((), ())), preferred_element_type=jnp.float32)
        wave = row * wave_dev + first_wave + index
        total = (wave + iota((1, count), 1)).astype(jnp.float32)
        ratio = total * (total + 1.0) / (1279.0 * 1280.0)
        damping = 1.0 / (1.0 + 20.0 * ratio * ratio)
        filtered = (spectral * damping).astype(jnp.bfloat16)
        result = lax.dot_general(table, filtered, (((1,), (1,)), ((), ())), preferred_element_type=jnp.float32)
        out[:, 0] = result.astype(jnp.bfloat16).reshape(n_row, lats, lanes)

    if with_ends:
        @pl.when((comp != 0) & (index == 0))
        def _():
            levels = ends.shape[1]
            for dest in range(n_row):
                out[dest, 0, 0:levels, :] = jnp.where(dest > row, ends[1], ends[0])


def surface_kernel(place, counts, partner, own, source, _, new, gap, *, group, n_row, n_col):
    rows = partner.shape[0]
    half = rows // 2
    width = 2 * lanes
    table = jnp.concatenate(
        [partner[pl.ds(0, half, stride=2), :], partner[pl.ds(1, half, stride=2), :]], axis=1
    )
    coarse = table.astype(jnp.bfloat16)
    fine = (table - coarse.astype(jnp.float32)).astype(jnp.bfloat16)
    low_index = lax.broadcasted_iota(jnp.int32, (width, lanes), 0)
    high_index = lax.broadcasted_iota(jnp.int32, (half, lanes), 0)
    one = jnp.ones((width, lanes), jnp.bfloat16)
    zero = jnp.zeros((width, lanes), jnp.bfloat16)
    sublane = lax.broadcasted_iota(jnp.int32, (8, lanes), 0)
    rate = jnp.where(where_am_i(place, n_row, n_col)[0] == 0, 0.5, 0.25).astype(jnp.float32)

    def body(g, carry):
        start = pl.multiple_of(g * 8, 8)
        entries = source[pl.ds(start, 8), :]
        low = entries & (width - 1)
        high = entries >> 8
        found = []
        for p in range(0, 8, group):
            pick = jnp.concatenate(
                [jnp.where(low_index == low[s:s + 1, :], one, zero) for s in range(p, p + group)], axis=1
            )
            picked = jnp.dot(coarse, pick, preferred_element_type=jnp.float32)
            picked = picked + jnp.dot(fine, pick, preferred_element_type=jnp.float32)
            for s in range(group):
                part = picked[:, lanes * s:lanes * (s + 1)]
                match = high_index == high[p + s:p + s + 1, :]
                found.append(jnp.sum(jnp.where(match, part, 0.0), axis=0, keepdims=True))
        pulled = jnp.concatenate(found, axis=0)
        limit = jnp.zeros((8, lanes), jnp.int32)
        for s in range(8):
            limit = jnp.where(sublane == s, counts[0, start + s], limit)
        here = own[pl.ds(start, 8), :]
        difference = jnp.where(iota((8, lanes), 1) < limit, pulled - here, 0.0)
        new[pl.ds(start, 8), :] = here + rate * difference
        gap[pl.ds(start, 8), :] = difference
        return carry

    lax.fori_loop(0, rows // 8, body, 0)


def exit_kernel(place, sea, *rest, n_row, n_col, chunks, block):
    back, out, table = rest[:chunks], rest[chunks], rest[chunks + 1]
    comp, _, _ = where_am_i(place, n_row, n_col)
    levels = out.shape[0] // block
    wave_dev = levels // n_row
    width = wave_dev // chunks

    def source(wave, lat, count):
        origin, local = divmod(wave, wave_dev)
        chunk, slot = divmod(local, width)
        return back[chunk][origin, slot, lat:lat + count, :]

    @pl.when(comp == 0)
    def _():
        @pl.when(pl.program_id(0) == 0)
        def _():
            table[...] = swap_matrix()

        for lat in range(0, block - 15, 16):
            halves = [
                jnp.concatenate([source(half + wave, lat, 16) for wave in range(16)], axis=0)
                for half in range(0, levels, 16)
            ]
            turned = product(table[...], jnp.concatenate(halves, axis=1))
            for s in range(16):
                for half in range(0, levels, 16):
                    start = (lat + s) * levels + half
                    part = lanes * (half // 16)
                    out[start:start + 16, :] = turned[16 * s:16 * s + 16, part:part + lanes]
        for lat in range(block - block % 16, block, 8):
            for wave in range(levels):
                out[pl.ds(lat * levels + wave, 8, stride=levels), :] = source(wave, lat, 8).astype(jnp.float32)

    @pl.when(comp != 0)
    def _():
        out[...] = sea[...]


def shards(model_state, legendre, gauss_weight, mixing, surface, sea_count, remap_source):
    n_row, n_col = lax.axis_size("row"), lax.axis_size("col")
    rows, levels = model_state.shape[1], model_state.shape[2]
    wave_dev = levels // n_row
    chunks = 2 if wave_dev % 2 == 0 else 1
    width = wave_dev // chunks
    block = row_block(rows)
    steps = rows // block
    f32, bf16 = jnp.float32, jnp.bfloat16
    sds = jax.ShapeDtypeStruct
    mib = 1 << 20

    fields = model_state.reshape(rows * levels, lanes)
    counts = sea_count.reshape(1, rows)
    place = lax.axis_index(("comp", "row", "col")).astype(jnp.int32).reshape(1)
    own = surface[0]
    comp_size = lax.axis_size("comp")
    partner = lax.ppermute(own, "comp", [(i, comp_size - 1 - i) for i in range(comp_size)])

    def on(comp, i, s):
        return jnp.where(lax.div(s[0], n_row * n_col) == comp, i, 0)

    def row_of(s):
        return lax.rem(lax.div(s[0], n_col), n_row)

    def call(kernel, name, grid, in_specs, out_specs, out_shape, args, scratch=(), vmem=59, flops=10**7, size=0):
        return pl.pallas_call(
            functools.partial(kernel, n_row=n_row, n_col=n_col),
            out_shape=out_shape,
            grid_spec=pltpu.PrefetchScalarGridSpec(
                num_scalar_prefetch=1, grid=grid, in_specs=in_specs, out_specs=out_specs, scratch_shapes=scratch),
            compiler_params=pltpu.CompilerParams(vmem_limit_bytes=vmem * mib),
            name=name,
            cost_estimate=cost(flops, size),
        )(place, *args)

    smem = pl.BlockSpec(memory_space=pltpu.SMEM)
    anywhere = pl.BlockSpec(memory_space=pl.ANY)
    state_bytes = 4 * rows * levels * lanes
    tall = block * levels

    *send, mixed, edge = call(
        functools.partial(entry_kernel, chunks=chunks, block=block), "entry", (steps,),
        [
            smem,
            pl.BlockSpec((tall, lanes), lambda i, s: (i, 0)),
            pl.BlockSpec((8 * levels, lanes), lambda i, s: (rows // 8 - 1, 0)),
            smem,
            pl.BlockSpec((levels, levels), lambda i, s: (0, 0)),
        ],
        [pl.BlockSpec((n_row, width, block, lanes), lambda i, s: (0, 0, i, 0))] * chunks
        + [
            pl.BlockSpec((tall, lanes), lambda i, s: (on(1, i, s), 0)),
            pl.BlockSpec((1, levels, lanes), lambda i, s: (on(1, i, s), 0, 0)),
        ],
        [sds((n_row, width, rows, lanes), bf16)] * chunks
        + [sds((rows * levels, lanes), f32), sds((steps, levels, lanes), bf16)],
        (counts, fields, fields, gauss_weight, mixing),
        scratch=[pltpu.VMEM((256, 256), bf16)], vmem=63, size=2 * state_bytes,
    )

    def to_waves(x):
        return lax.all_to_all(x, "row", split_axis=0, concat_axis=0, tiled=True)

    ahead = [(i, i + 1) for i in range(n_col - 1)]

    def to_columns(x):
        return [lax.ppermute(x, "col", [(b, a) for a, b in ahead]), lax.ppermute(x, "col", ahead)]

    coeffs = [to_waves(x) for x in send]
    sides = to_columns(edge)

    whole = pl.BlockSpec((rows, lanes), lambda i, s: (0, 0))
    new_surface, gap = call(
        functools.partial(surface_kernel, group=2), "surface", (1,),
        [smem, whole, whole, whole, anywhere], [whole] * 2, [sds((rows, lanes), f32)] * 2,
        (counts, partner, own, remap_source[0], edge), flops=2 * 10**10, size=5 * 4 * rows * lanes,
    )

    def sweep(field, rows_in, cols_in, final, extra=()):
        out_shape = [sds((rows * levels, lanes), f32)]
        out_specs = [pl.BlockSpec((tall, lanes), lambda i, s: (on(1, i, s), 0))]
        if not final:
            out_shape += [sds((steps, levels, lanes), bf16), sds((2, levels, lanes), bf16)]
            out_specs += [
                pl.BlockSpec((1, levels, lanes), lambda i, s: (on(1, i, s), 0, 0)),
                pl.BlockSpec((2, levels, lanes), lambda i, s: (0, 0, 0)),
            ]
        side = (1, 1, levels, lanes)
        in_specs = [
            smem,
            pl.BlockSpec((tall, lanes), lambda i, s: (on(1, i, s), 0)),
            pl.BlockSpec((levels, lanes), lambda i, s: (jnp.maximum(on(1, i, s) * block - 1, 0), 0)),
            pl.BlockSpec((levels, lanes), lambda i, s: (jnp.minimum((on(1, i, s) + 1) * block, rows - 1), 0)),
            pl.BlockSpec(side, lambda i, s: (jnp.maximum(row_of(s) - 1, 0), 0, 0, 0)),
            pl.BlockSpec(side, lambda i, s: (jnp.minimum(row_of(s) + 1, n_row - 1), 0, 0, 0)),
            pl.BlockSpec((1, levels, lanes), lambda i, s: (on(1, i, s), 0, 0)),
            pl.BlockSpec((1, levels, lanes), lambda i, s: (on(1, i, s), 0, 0)),
        ] + ([pl.BlockSpec((block, lanes), lambda i, s: (on(1, i, s), 0))] if final else [])
        return call(
            functools.partial(sweep_kernel, block=block, final=final), "sweep_last" if final else "sweep", (steps,),
            in_specs, out_specs, out_shape,
            (counts, field, field, field, rows_in, rows_in, *cols_in, *extra),
            scratch=[pltpu.VMEM(((block + 2) * levels, lanes), f32)], size=2 * state_bytes,
        )

    first_step, edge, ends = sweep(mixed, coeffs[0], sides, False)
    sides = to_columns(edge)

    returned = []
    for chunk in range(chunks):
        with_ends = chunk == 0
        part = call(
            functools.partial(legendre_kernel, wave_dev=wave_dev, first_wave=chunk * width, with_ends=with_ends),
            f"legendre_{chunk}", (width,),
            [
                pl.BlockSpec((1,) + legendre.shape[1:],
                             lambda i, s, chunk=chunk: (chunk * width + on(0, i, s), 0, 0)),
                pl.BlockSpec((n_row, 1, rows, lanes), lambda i, s: (0, on(0, i, s), 0, 0)),
            ] + ([pl.BlockSpec((2, levels, lanes), lambda i, s: (0, 0, 0)), anywhere] if with_ends else []),
            pl.BlockSpec((n_row, 1, rows, lanes), lambda i, s: (0, on(0, i, s), 0, 0)),
            sds((n_row, width, rows, lanes), bf16),
            (legendre, coeffs[chunk], *([ends, gap] if with_ends else [])),
            vmem=63, flops=4 * width * legendre.shape[1] * legendre.shape[2] * lanes,
            size=2 * width * legendre.shape[1] * legendre.shape[2],
        )
        returned.append(to_waves(part))

    (sea,) = sweep(first_step, returned[0], sides, True, (gap,))

    state = call(
        functools.partial(exit_kernel, chunks=chunks, block=block), "exit", (steps,),
        [pl.BlockSpec((tall, lanes), lambda i, s: (on(1, i, s), 0))]
        + [pl.BlockSpec((n_row, width, block, lanes), lambda i, s: (0, 0, on(0, i, s), 0))] * chunks,
        pl.BlockSpec((tall, lanes), lambda i, s: (i, 0)),
        sds((rows * levels, lanes), f32),
        (sea, *returned), scratch=[pltpu.VMEM((256, 256), bf16)], size=2 * state_bytes,
    )
    return state.reshape(model_state.shape), new_surface[None]


def solution(mesh):
    in_specs = (
        P("comp", "row", None, "col"),
        P("row", None, None),
        P("row"),
        P(),
        P("comp", "row", "col"),
        P("comp", "row", "col"),
        P("comp", "row", "col"),
    )
    out_specs = (P("comp", "row", None, "col"), P("comp", "row", "col"))
    return jax.shard_map(shards, mesh=mesh, in_specs=in_specs, out_specs=out_specs, check_vma=False)
```

```python
import functools

import jax
import jax.numpy as jnp
from jax import lax
from jax.experimental import pallas as pl
from jax.experimental.pallas import tpu as pltpu
from jax.sharding import PartitionSpec as P


diffusion_rate = 0.2
lanes = 128


def chunk_count(wave_dev):
    return 2 if wave_dev % 2 == 0 else 1


def row_block(rows):
    return 64 if rows % 64 == 0 else rows


def cost(flops, bytes_accessed):
    return pl.CostEstimate(flops=flops, bytes_accessed=bytes_accessed, transcendentals=0)


def where_am_i(place, n_row, n_col):
    flat = place[0]
    return (
        lax.div(flat, n_row * n_col),
        lax.rem(lax.div(flat, n_col), n_row),
        lax.rem(flat, n_col),
    )


def iota(shape, dim):
    return lax.broadcasted_iota(jnp.int32, shape, dim)


def as_bf16(mask):
    return jnp.where(mask, 1.0, 0.0).astype(jnp.bfloat16)


def swap_matrix(flip_high, flip_low):
    row, column = iota((256, 256), 0), iota((256, 256), 1)
    return as_bf16(column == (((row & 15) ^ flip_low) << 4 | ((row >> 4) ^ flip_high)))


def spread_matrix():
    row, column = iota((lanes, lanes), 0), iota((lanes, lanes), 1)
    odd = column & 1
    return as_bf16(((row == lanes - 1) & (odd == 0)) | ((row == 0) & (odd == 1)))


def beside_matrix():
    row, column = iota((lanes, lanes), 0), iota((lanes, lanes), 1)
    return as_bf16((row == column + 1) | (row + 1 == column))


def side_matrix():
    row, column = iota((lanes, lanes), 0), iota((lanes, lanes), 1)
    odd = row & 1
    return as_bf16(((column == 0) & (odd == 1)) | ((column == lanes - 1) & (odd == 0)))


def split(value):
    high = value.astype(jnp.bfloat16)
    return high, (value - high.astype(jnp.float32)).astype(jnp.bfloat16)


def product(a, b):
    return jnp.dot(a, b, preferred_element_type=jnp.float32)


def entry_kernel(place, counts, field, last, gauss, mix, *rest, n_row, n_col, chunks, block):
    send = [rest[n_row * c:n_row * (c + 1)] for c in range(chunks)]
    mixed, edge, table = rest[n_row * chunks:]
    comp, row, _ = where_am_i(place, n_row, n_col)
    levels = field.shape[0] // block
    wave_dev = levels // n_row
    width = wave_dev // chunks
    step = pl.program_id(0)

    flip = row * wave_dev

    def target(wave):
        part, local = divmod(wave, wave_dev)
        chunk, slot = divmod(local, width)
        return send[chunk][part], slot

    @pl.when(comp == 0)
    def _():
        @pl.when(step == 0)
        def _():
            table[...] = swap_matrix(flip & 15, 0)

        for lat in range(0, block - 15, 16):
            halves = []
            for half in range(0, levels, 16):
                halves.append(jnp.concatenate([
                    (field[pl.ds(pl.multiple_of((lat + s) * levels + (half ^ (flip & ~15)), 16), 16), :]
                     * gauss[step * block + lat + s]).astype(jnp.bfloat16)
                    for s in range(16)
                ], axis=0))
            turned = product(table[...], jnp.concatenate(halves, axis=1)).astype(jnp.bfloat16)
            for wave in range(levels):
                out, slot = target(wave)
                part = lanes * (wave // 16)
                out[slot, lat:lat + 16, :] = turned[16 * (wave % 16):16 * (wave % 16) + 16, part:part + lanes]
        for lat in range(block - block % 16, block, 8):
            weight = jnp.zeros((8, lanes), jnp.float32)
            for s in range(8):
                weight = jnp.where(iota((8, lanes), 0) == s, gauss[step * block + lat + s], weight)
            for wave in range(levels):
                out, slot = target(wave)
                values = field[pl.ds(lat * levels + (wave ^ flip), 8, stride=levels), :] * weight
                out[slot, lat:lat + 8, :] = values.astype(jnp.bfloat16)

    def mixed_rows(ref, start, first_row):
        values = []
        for quarter in range(2):
            parts = []
            for pair in range(2):
                part = ref[pl.ds(start + (2 * quarter + pair) * 2 * levels, 2 * levels), :]
                values.append(part)
                parts.append(split(part))
            high = jnp.concatenate([p[0] for p in parts], axis=1)
            low = jnp.concatenate([p[1] for p in parts], axis=1)
            blend = product(table[0:2 * levels, :], jnp.concatenate([high, low, high, low], axis=0))
            values += [blend[:, :lanes], blend[:, lanes:]]
        out = []
        for s in range(8):
            quarter, pair, place_in = s // 4, s // 2 % 2, slice(levels * (s % 2), levels * (s % 2) + levels)
            heat = values[4 * quarter + pair][place_in]
            blend = values[4 * quarter + 2 + pair][place_in]
            sea = iota((levels, lanes), 1) < counts[0, first_row + s]
            value = heat + jnp.where(sea, blend, 0.0)
            out.append((value, jnp.where(sea, value, 0.0).astype(jnp.bfloat16)))
        return out

    @pl.when(comp != 0)
    def _():
        @pl.when(step == 0)
        def _():
            high, low = split(mix[...])
            repeat = as_bf16((iota((levels, 256), 1) & (levels - 1)) == iota((levels, 256), 0))
            wide = jnp.where(iota((levels, 256), 1) < 4 * levels, product(high, repeat), product(low, repeat))
            wide = jnp.concatenate([wide, wide], axis=0)
            shape = (2 * levels, 256)
            own = (iota(shape, 1) // levels & 1) == iota(shape, 0) // levels
            table[0:2 * levels, :] = jnp.where(own, wide, 0.0).astype(jnp.bfloat16)

        spread = spread_matrix()
        pair_of = iota((levels, lanes), 1) >> 1

        batch = 32 if block % 32 == 0 else 8

        def body(g, packed):
            rows = []
            for first in range(0, batch, 8):
                start = pl.multiple_of((g * batch + first) * levels, 8 * levels)
                some = mixed_rows(field, start, step * block + g * batch + first)
                for s, (value, _) in enumerate(some):
                    mixed[pl.ds(pl.multiple_of(start + s * levels, levels), levels), :] = value
                rows += some
            ends = product(jnp.concatenate([r[1] for r in rows], axis=0), spread)
            for s in range(batch):
                packed = jnp.where(pair_of == g * batch + s, ends[s * levels:(s + 1) * levels], packed)
            return packed

        packed = lax.fori_loop(0, block // batch, body, jnp.zeros((levels, lanes), jnp.float32))
        edge[0] = packed.astype(jnp.bfloat16)

        @pl.when(step == 0)
        def _():
            total = pl.num_programs(0) * block
            top = mixed_rows(field, 0, 0)[0][1]
            low = mixed_rows(last, 0, total - 8)[-1][1]
            for part in range(1, n_row):
                send[0][part][0, 0:levels, :] = jnp.where((part ^ row) > row, low, top)


def sweep_kernel(place, counts, field, above, below, east_in, west_in, *rest, block, n_row, n_col, near_parts, final):
    halos, rest = rest[:len(near_parts)], rest[len(near_parts):]
    if final:
        gap, out, masked = rest
    else:
        out, edge, ends, masked = rest
    comp, row, col = where_am_i(place, n_row, n_col)
    levels = field.shape[0] // block
    step = pl.program_id(0)
    steps = pl.num_programs(0)
    rows = steps * block
    base = step * block
    shape = (levels, lanes)
    batch = 32 if block % 32 == 0 else 8

    @pl.when(comp != 0)
    def _():
        lane = iota(shape, 1)
        pair_of = lane >> 1

        def sea_of(y):
            return lane < counts[0, jnp.clip(y, 0, rows - 1)]

        def at(y):
            return pl.ds(pl.multiple_of(y * levels, levels), levels)

        def halo(neighbour):
            found = jnp.zeros(shape, jnp.float32)
            inside = (neighbour >= 0) & (neighbour < n_row)
            for part, ref in zip(near_parts, halos):
                found = jnp.where(inside & ((neighbour ^ row) == part), ref[0].astype(jnp.float32), found)
            return found

        west = jnp.where(col > 0, west_in[0].astype(jnp.float32), 0.0)
        east = jnp.where(col < n_col - 1, east_in[0].astype(jnp.float32), 0.0)
        sides = jnp.where((lane & 1) == 0, pltpu.roll(east, lanes - 1, 1), pltpu.roll(west, 1, 1))
        masked[0:levels, :] = jnp.where(step > 0, jnp.where(sea_of(base - 1), above[...], 0.0), halo(row - 1))
        masked[(block + 1) * levels:(block + 2) * levels, :] = jnp.where(
            step < steps - 1, jnp.where(sea_of(base + block), below[...], 0.0), halo(row + 1))

        def fill(g, carry):
            for s in range(8):
                y = g * 8 + s
                masked[at(y + 1), :] = jnp.where(sea_of(base + y), field[at(y), :], 0.0)
            return carry

        lax.fori_loop(0, block // 8, fill, 0)
        beside = beside_matrix()
        weights = jnp.concatenate([beside, side_matrix(), beside], axis=0)
        spread = spread_matrix()

        def body(g, packed):
            here = masked[pl.ds(pl.multiple_of((g * batch + 1) * levels, levels), batch * levels), :]
            high, low = split(here)
            turned = jnp.concatenate(
                [jnp.where(pair_of == g * batch + s, sides, 0.0).astype(jnp.bfloat16) for s in range(batch)], axis=0)
            near = product(jnp.concatenate([high, turned, low], axis=1), weights)
            new_rows = []
            for s in range(batch):
                y = g * batch + s
                part = slice(s * levels, (s + 1) * levels)
                lap = masked[at(y), :] + masked[at(y + 2), :] + near[part] - 4.0 * masked[at(y + 1), :]
                sea = sea_of(base + y)
                new = field[at(y), :] + jnp.where(sea, diffusion_rate * lap, 0.0)
                out[at(y), :] = new
                if final:
                    out[pl.ds(y * levels, 1), :] = new[0:1, :] + 0.3 * gap[pl.ds(y, 1), :]
                else:
                    new_rows.append(jnp.where(sea, new, 0.0).astype(jnp.bfloat16))
            if not final:
                spreads = product(jnp.concatenate(new_rows, axis=0), spread)
                for s in range(batch):
                    packed = jnp.where(pair_of == g * batch + s, spreads[s * levels:(s + 1) * levels], packed)
            return packed

        packed = lax.fori_loop(0, block // batch, body, jnp.zeros(shape, jnp.float32))
        if not final:
            edge[0] = packed.astype(jnp.bfloat16)

            @pl.when(step == 0)
            def _():
                ends[0] = jnp.where(sea_of(0), out[0:levels, :], 0.0).astype(jnp.bfloat16)

            @pl.when(step == steps - 1)
            def _():
                ends[1] = jnp.where(
                    sea_of(rows - 1), out[(block - 1) * levels:block * levels, :], 0.0
                ).astype(jnp.bfloat16)


def legendre_kernel(place, legendre, *rest, n_row, n_col, wave_dev, first_wave, with_ends):
    coeffs, rest = rest[:n_row], rest[n_row:]
    if with_ends:
        ends, rest = rest[0], rest[2:]
    out, gathered = rest[:n_row], rest[n_row]
    comp, row, _ = where_am_i(place, n_row, n_col)
    index = pl.program_id(0)
    lats = coeffs[0].shape[1]
    count = legendre.shape[2]

    @pl.when(comp == 0)
    def _():
        table = legendre[0]
        for part in range(n_row):
            gathered[part ^ row] = coeffs[part][0]
        fourier = gathered[...].reshape(n_row * lats, lanes)
        spectral = lax.dot_general(fourier, table, (((0,), (0,)), ((), ())), preferred_element_type=jnp.float32)
        wave = row * wave_dev + first_wave + index
        total = (wave + iota((1, count), 1)).astype(jnp.float32)
        ratio = total * (total + 1.0) / (1279.0 * 1280.0)
        damping = 1.0 / (1.0 + 20.0 * ratio * ratio)
        filtered = (spectral * damping).astype(jnp.bfloat16)
        result = lax.dot_general(table, filtered, (((1,), (1,)), ((), ())), preferred_element_type=jnp.float32)
        gathered[...] = result.astype(jnp.bfloat16).reshape(n_row, lats, lanes)
        for part in range(n_row):
            out[part][0] = gathered[part ^ row]

    if with_ends:
        @pl.when((comp != 0) & (index == 0))
        def _():
            levels = ends.shape[1]
            for part in range(1, n_row):
                out[part][0, 0:levels, :] = jnp.where((part ^ row) > row, ends[1], ends[0])


def surface_kernel(place, counts, partner, own, source, _, new, gap, *, group, n_row, n_col):
    rows = partner.shape[0]
    half = rows // 2
    width = 2 * lanes
    table = jnp.concatenate(
        [partner[pl.ds(0, half, stride=2), :], partner[pl.ds(1, half, stride=2), :]], axis=1
    )
    coarse = table.astype(jnp.bfloat16)
    fine = (table - coarse.astype(jnp.float32)).astype(jnp.bfloat16)
    low_index = lax.broadcasted_iota(jnp.int32, (width, lanes), 0)
    high_index = lax.broadcasted_iota(jnp.int32, (half, lanes), 0)
    one = jnp.ones((width, lanes), jnp.bfloat16)
    zero = jnp.zeros((width, lanes), jnp.bfloat16)
    sublane = lax.broadcasted_iota(jnp.int32, (8, lanes), 0)
    rate = jnp.where(where_am_i(place, n_row, n_col)[0] == 0, 0.5, 0.25).astype(jnp.float32)

    def body(g, carry):
        start = pl.multiple_of(g * 8, 8)
        entries = source[pl.ds(start, 8), :]
        low = entries & (width - 1)
        high = entries >> 8
        found = []
        for p in range(0, 8, group):
            pick = jnp.concatenate(
                [jnp.where(low_index == low[s:s + 1, :], one, zero) for s in range(p, p + group)], axis=1
            )
            picked = jnp.dot(coarse, pick, preferred_element_type=jnp.float32)
            picked = picked + jnp.dot(fine, pick, preferred_element_type=jnp.float32)
            for s in range(group):
                part = picked[:, lanes * s:lanes * (s + 1)]
                match = high_index == high[p + s:p + s + 1, :]
                found.append(jnp.sum(jnp.where(match, part, 0.0), axis=0, keepdims=True))
        pulled = jnp.concatenate(found, axis=0)
        limit = jnp.zeros((8, lanes), jnp.int32)
        for s in range(8):
            limit = jnp.where(sublane == s, counts[0, start + s], limit)
        here = own[pl.ds(start, 8), :]
        difference = jnp.where(iota((8, lanes), 1) < limit, pulled - here, 0.0)
        new[pl.ds(start, 8), :] = here + rate * difference
        gap[pl.ds(start, 8), :] = difference
        return carry

    lax.fori_loop(0, rows // 8, body, 0)


def exit_kernel(place, sea, *rest, n_row, n_col, chunks, block):
    back = [rest[n_row * c:n_row * (c + 1)] for c in range(chunks)]
    out, table = rest[n_row * chunks:]
    comp, row, _ = where_am_i(place, n_row, n_col)
    levels = out.shape[0] // block
    wave_dev = levels // n_row
    width = wave_dev // chunks

    flip = row * wave_dev

    def source(wave, lat, count):
        part, local = divmod(wave, wave_dev)
        chunk, slot = divmod(local, width)
        return back[chunk][part][slot, lat:lat + count, :]

    @pl.when(comp == 0)
    def _():
        @pl.when(pl.program_id(0) == 0)
        def _():
            table[...] = swap_matrix(0, flip & 15)

        for lat in range(0, block - 15, 16):
            halves = [
                jnp.concatenate([source(half + wave, lat, 16) for wave in range(16)], axis=0)
                for half in range(0, levels, 16)
            ]
            turned = product(table[...], jnp.concatenate(halves, axis=1))
            for s in range(16):
                for half in range(0, levels, 16):
                    start = pl.multiple_of((lat + s) * levels + (half ^ (flip & ~15)), 16)
                    part = lanes * (half // 16)
                    out[pl.ds(start, 16), :] = turned[16 * s:16 * s + 16, part:part + lanes]
        for lat in range(block - block % 16, block, 8):
            for wave in range(levels):
                out[pl.ds(lat * levels + (wave ^ flip), 8, stride=levels), :] = source(wave, lat, 8).astype(jnp.float32)

    @pl.when(comp != 0)
    def _():
        out[...] = sea[...]


def shards(model_state, legendre, gauss_weight, mixing, surface, sea_count, remap_source):
    n_row, n_col = lax.axis_size("row"), lax.axis_size("col")
    rows, levels = model_state.shape[1], model_state.shape[2]
    wave_dev = levels // n_row
    chunks = chunk_count(wave_dev)
    width = wave_dev // chunks
    block = row_block(rows)
    steps = rows // block
    f32, bf16 = jnp.float32, jnp.bfloat16
    sds = jax.ShapeDtypeStruct
    mib = 1 << 20

    fields = model_state.reshape(rows * levels, lanes)
    counts = sea_count.reshape(1, rows)
    place = lax.axis_index(("comp", "row", "col")).astype(jnp.int32).reshape(1)
    own = surface[0]
    comp_size = lax.axis_size("comp")
    partner = lax.ppermute(own, "comp", [(i, comp_size - 1 - i) for i in range(comp_size)])

    def on(comp, i, s):
        return jnp.where(lax.div(s[0], n_row * n_col) == comp, i, 0)

    def call(kernel, grid, in_specs, out_specs, out_shape, args, scratch=(), vmem=59, flops=10**7, size=0):
        return pl.pallas_call(
            functools.partial(kernel, n_row=n_row, n_col=n_col),
            out_shape=out_shape,
            grid_spec=pltpu.PrefetchScalarGridSpec(
                num_scalar_prefetch=1, grid=grid, in_specs=in_specs, out_specs=out_specs, scratch_shapes=scratch),
            compiler_params=pltpu.CompilerParams(vmem_limit_bytes=vmem * mib),
            cost_estimate=cost(flops, size),
        )(place, *args)

    smem = pl.BlockSpec(memory_space=pltpu.SMEM)
    anywhere = pl.BlockSpec(memory_space=pl.ANY)
    state_bytes = 4 * rows * levels * lanes
    tall = block * levels

    *send, mixed, edge = call(
        functools.partial(entry_kernel, chunks=chunks, block=block), (steps,),
        [
            smem,
            pl.BlockSpec((tall, lanes), lambda i, s: (i, 0)),
            pl.BlockSpec((8 * levels, lanes), lambda i, s: (rows // 8 - 1, 0)),
            smem,
            pl.BlockSpec((levels, levels), lambda i, s: (0, 0)),
        ],
        [pl.BlockSpec((width, block, lanes), lambda i, s: (0, i, 0))] * (chunks * n_row)
        + [
            pl.BlockSpec((tall, lanes), lambda i, s: (on(1, i, s), 0)),
            pl.BlockSpec((1, levels, lanes), lambda i, s: (on(1, i, s), 0, 0)),
        ],
        [sds((width, rows, lanes), bf16)] * (chunks * n_row)
        + [sds((rows * levels, lanes), f32), sds((steps, levels, lanes), bf16)],
        (counts, fields, fields, gauss_weight, mixing),
        scratch=[pltpu.VMEM((256, 256), bf16)], vmem=63, size=2 * state_bytes,
    )

    def traded(parts):
        got = [parts[0]]
        for k in range(1, n_row):
            got.append(lax.ppermute(parts[k], "row", [(r, r ^ k) for r in range(n_row)]))
        return got

    chain = [n_col + i for i in range(n_col - 1)]

    def to_columns(x):
        return [
            lax.ppermute(x, ("comp", "col"), [(i + 1, i) for i in chain]),
            lax.ppermute(x, ("comp", "col"), [(i, i + 1) for i in chain]),
        ]

    coeffs = [traded(send[n_row * c:n_row * (c + 1)]) for c in range(chunks)]
    sides = to_columns(edge)

    whole = pl.BlockSpec((rows, lanes), lambda i, s: (0, 0))
    new_surface, gap = call(
        functools.partial(surface_kernel, group=2), (1,),
        [smem, whole, whole, whole, anywhere], [whole] * 2, [sds((rows, lanes), f32)] * 2,
        (counts, partner, own, remap_source[0], edge), flops=2 * 10**10, size=5 * 4 * rows * lanes,
    )

    near_parts = [k for k in range(1, n_row) if k & (k + 1) == 0]

    def sweep(field, rows_in, cols_in, final, extra=()):
        out_shape = [sds((rows * levels, lanes), f32)]
        out_specs = [pl.BlockSpec((tall, lanes), lambda i, s: (on(1, i, s), 0))]
        if not final:
            out_shape += [sds((steps, levels, lanes), bf16), sds((2, levels, lanes), bf16)]
            out_specs += [
                pl.BlockSpec((1, levels, lanes), lambda i, s: (on(1, i, s), 0, 0)),
                pl.BlockSpec((2, levels, lanes), lambda i, s: (0, 0, 0)),
            ]
        in_specs = [
            smem,
            pl.BlockSpec((tall, lanes), lambda i, s: (on(1, i, s), 0)),
            pl.BlockSpec((levels, lanes), lambda i, s: (jnp.maximum(on(1, i, s) * block - 1, 0), 0)),
            pl.BlockSpec((levels, lanes), lambda i, s: (jnp.minimum((on(1, i, s) + 1) * block, rows - 1), 0)),
            pl.BlockSpec((1, levels, lanes), lambda i, s: (on(1, i, s), 0, 0)),
            pl.BlockSpec((1, levels, lanes), lambda i, s: (on(1, i, s), 0, 0)),
        ] + [pl.BlockSpec((1, levels, lanes), lambda i, s: (0, 0, 0))] * len(near_parts) + ([pl.BlockSpec((block, lanes), lambda i, s: (on(1, i, s), 0))] if final else [])
        return call(
            functools.partial(sweep_kernel, block=block, near_parts=near_parts, final=final), (steps,),
            in_specs, out_specs, out_shape,
            (counts, field, field, field, *cols_in, *(rows_in[k] for k in near_parts), *extra),
            scratch=[pltpu.VMEM(((block + 2) * levels, lanes), f32)], size=2 * state_bytes,
        )

    first_step, edge, ends = sweep(mixed, coeffs[0], sides, False)
    sides = to_columns(edge)

    returned = []
    for chunk in range(chunks):
        with_ends = chunk == 0
        part = call(
            functools.partial(legendre_kernel, wave_dev=wave_dev, first_wave=chunk * width, with_ends=with_ends),
            (width,),
            [
                pl.BlockSpec((1,) + legendre.shape[1:],
                             lambda i, s, chunk=chunk: (chunk * width + on(0, i, s), 0, 0)),
            ] + [pl.BlockSpec((1, rows, lanes), lambda i, s: (on(0, i, s), 0, 0))] * n_row + ([pl.BlockSpec((2, levels, lanes), lambda i, s: (0, 0, 0)), anywhere] if with_ends else []),
            [pl.BlockSpec((1, rows, lanes), lambda i, s: (on(0, i, s), 0, 0))] * n_row,
            [sds((width, rows, lanes), bf16)] * n_row,
            (legendre, *coeffs[chunk], *([ends, gap] if with_ends else [])),
            scratch=[pltpu.VMEM((n_row, rows, lanes), bf16)], vmem=63, flops=4 * width * legendre.shape[1] * legendre.shape[2] * lanes,
            size=2 * width * legendre.shape[1] * legendre.shape[2],
        )
        returned.append(traded(part))

    (sea,) = sweep(first_step, returned[0], sides, True, (gap,))

    state = call(
        functools.partial(exit_kernel, chunks=chunks, block=block), (steps,),
        [pl.BlockSpec((tall, lanes), lambda i, s: (on(1, i, s), 0))]
        + [pl.BlockSpec((width, block, lanes), lambda i, s: (0, on(0, i, s), 0))] * (chunks * n_row),
        pl.BlockSpec((tall, lanes), lambda i, s: (i, 0)),
        sds((rows * levels, lanes), f32),
        (sea, *sum(returned, [])), scratch=[pltpu.VMEM((256, 256), bf16)], size=2 * state_bytes,
    )
    return state.reshape(model_state.shape), new_surface[None]


def solution(mesh):
    in_specs = (
        P("comp", "row", None, "col"),
        P("row", None, None),
        P("row"),
        P(),
        P("comp", "row", "col"),
        P("comp", "row", "col"),
        P("comp", "row", "col"),
    )
    out_specs = (P("comp", "row", None, "col"), P("comp", "row", "col"))

    return jax.shard_map(shards, mesh=mesh, in_specs=in_specs, out_specs=out_specs, check_vma=False)
```

```python
import functools

import jax
import jax.numpy as jnp
from jax import lax
from jax.experimental import pallas as pl
from jax.experimental.pallas import tpu as pltpu
from jax.sharding import PartitionSpec as P


diffusion_rate = 0.2
lanes = 128


def chunk_widths(wave_dev):
    outer = 3 * wave_dev // 8
    return (outer, wave_dev - 2 * outer, outer) if outer else (wave_dev,)


def chunk_of(local, widths):
    chunk = 0
    while local >= widths[chunk]:
        local -= widths[chunk]
        chunk += 1
    return chunk, local


def row_block(rows):
    return 64 if rows % 64 == 0 else rows


def cost(flops, bytes_accessed):
    return pl.CostEstimate(flops=flops, bytes_accessed=bytes_accessed, transcendentals=0)


def where_am_i(place, n_row, n_col):
    flat = place[0]
    return (
        lax.div(flat, n_row * n_col),
        lax.rem(lax.div(flat, n_col), n_row),
        lax.rem(flat, n_col),
    )


def iota(shape, dim):
    return lax.broadcasted_iota(jnp.int32, shape, dim)


def as_bf16(mask):
    return jnp.where(mask, 1.0, 0.0).astype(jnp.bfloat16)


def swap_matrix(flip_high, flip_low):
    row, column = iota((256, 256), 0), iota((256, 256), 1)
    return as_bf16(column == (((row & 15) ^ flip_low) << 4 | ((row >> 4) ^ flip_high)))


def spread_matrix():
    row, column = iota((lanes, lanes), 0), iota((lanes, lanes), 1)
    odd = column & 1
    return as_bf16(((row == lanes - 1) & (odd == 0)) | ((row == 0) & (odd == 1)))


def beside_matrix():
    row, column = iota((lanes, lanes), 0), iota((lanes, lanes), 1)
    return as_bf16((row == column + 1) | (row + 1 == column))


def side_matrix():
    row, column = iota((lanes, lanes), 0), iota((lanes, lanes), 1)
    odd = row & 1
    return as_bf16(((column == 0) & (odd == 1)) | ((column == lanes - 1) & (odd == 0)))


def split(value):
    high = value.astype(jnp.bfloat16)
    return high, (value - high.astype(jnp.float32)).astype(jnp.bfloat16)


def product(a, b):
    return jnp.dot(a, b, preferred_element_type=jnp.float32)


def entry_kernel(place, counts, field, last, gauss, mix, *rest, n_row, n_col, widths, block):
    chunks = len(widths)
    send = [rest[n_row * c:n_row * (c + 1)] for c in range(chunks)]
    mixed, edge, table = rest[n_row * chunks:]
    comp, row, _ = where_am_i(place, n_row, n_col)
    levels = field.shape[0] // block
    wave_dev = levels // n_row
    step = pl.program_id(0)

    flip = row * wave_dev

    def target(wave):
        part, local = divmod(wave, wave_dev)
        chunk, slot = chunk_of(local, widths)
        return send[chunk][part], slot

    @pl.when(comp == 0)
    def _():
        @pl.when(step == 0)
        def _():
            table[...] = swap_matrix(flip & 15, 0)

        for lat in range(0, block - 15, 16):
            halves = []
            for half in range(0, levels, 16):
                halves.append(jnp.concatenate([
                    (field[pl.ds(pl.multiple_of((lat + s) * levels + (half ^ (flip & ~15)), 16), 16), :]
                     * gauss[step * block + lat + s]).astype(jnp.bfloat16)
                    for s in range(16)
                ], axis=0))
            turned = product(table[...], jnp.concatenate(halves, axis=1)).astype(jnp.bfloat16)
            for wave in range(levels):
                out, slot = target(wave)
                part = lanes * (wave // 16)
                out[slot, lat:lat + 16, :] = turned[16 * (wave % 16):16 * (wave % 16) + 16, part:part + lanes]
        for lat in range(block - block % 16, block, 8):
            weight = jnp.zeros((8, lanes), jnp.float32)
            for s in range(8):
                weight = jnp.where(iota((8, lanes), 0) == s, gauss[step * block + lat + s], weight)
            for wave in range(levels):
                out, slot = target(wave)
                values = field[pl.ds(lat * levels + (wave ^ flip), 8, stride=levels), :] * weight
                out[slot, lat:lat + 8, :] = values.astype(jnp.bfloat16)

    def mixed_rows(ref, start, first_row):
        values = []
        for quarter in range(2):
            parts = []
            for pair in range(2):
                part = ref[pl.ds(start + (2 * quarter + pair) * 2 * levels, 2 * levels), :]
                values.append(part)
                parts.append(split(part))
            high = jnp.concatenate([p[0] for p in parts], axis=1)
            low = jnp.concatenate([p[1] for p in parts], axis=1)
            blend = product(table[0:2 * levels, :], jnp.concatenate([high, low, high, low], axis=0))
            values += [blend[:, :lanes], blend[:, lanes:]]
        out = []
        for s in range(8):
            quarter, pair, place_in = s // 4, s // 2 % 2, slice(levels * (s % 2), levels * (s % 2) + levels)
            heat = values[4 * quarter + pair][place_in]
            blend = values[4 * quarter + 2 + pair][place_in]
            sea = iota((levels, lanes), 1) < counts[0, first_row + s]
            value = heat + jnp.where(sea, blend, 0.0)
            out.append((value, jnp.where(sea, value, 0.0).astype(jnp.bfloat16)))
        return out

    @pl.when(comp != 0)
    def _():
        @pl.when(step == 0)
        def _():
            high, low = split(mix[...])
            repeat = as_bf16((iota((levels, 256), 1) & (levels - 1)) == iota((levels, 256), 0))
            wide = jnp.where(iota((levels, 256), 1) < 4 * levels, product(high, repeat), product(low, repeat))
            wide = jnp.concatenate([wide, wide], axis=0)
            shape = (2 * levels, 256)
            own = (iota(shape, 1) // levels & 1) == iota(shape, 0) // levels
            table[0:2 * levels, :] = jnp.where(own, wide, 0.0).astype(jnp.bfloat16)

        spread = spread_matrix()
        pair_of = iota((levels, lanes), 1) >> 1

        batch = 32 if block % 32 == 0 else 8

        def body(g, packed):
            rows = []
            for first in range(0, batch, 8):
                start = pl.multiple_of((g * batch + first) * levels, 8 * levels)
                some = mixed_rows(field, start, step * block + g * batch + first)
                for s, (value, _) in enumerate(some):
                    mixed[pl.ds(pl.multiple_of(start + s * levels, levels), levels), :] = value
                rows += some
            ends = product(jnp.concatenate([r[1] for r in rows], axis=0), spread)
            for s in range(batch):
                packed = jnp.where(pair_of == g * batch + s, ends[s * levels:(s + 1) * levels], packed)
            return packed

        packed = lax.fori_loop(0, block // batch, body, jnp.zeros((levels, lanes), jnp.float32))
        edge[0] = packed.astype(jnp.bfloat16)

        @pl.when(step == 0)
        def _():
            total = pl.num_programs(0) * block
            top = mixed_rows(field, 0, 0)[0][1]
            low = mixed_rows(last, 0, total - 8)[-1][1]
            for part in range(1, n_row):
                send[chunks // 2][part][0, 0:levels, :] = jnp.where((part ^ row) > row, low, top)


def sweep_kernel(place, counts, field, above, below, east_in, west_in, *rest, block, n_row, n_col, near_parts, final):
    halos, rest = rest[:len(near_parts)], rest[len(near_parts):]
    if final:
        gap, out, masked = rest
    else:
        out, edge, ends, masked = rest
    comp, row, col = where_am_i(place, n_row, n_col)
    levels = field.shape[0] // block
    step = pl.program_id(0)
    steps = pl.num_programs(0)
    rows = steps * block
    base = step * block
    shape = (levels, lanes)
    batch = 32 if block % 32 == 0 else 8

    @pl.when(comp != 0)
    def _():
        lane = iota(shape, 1)
        pair_of = lane >> 1

        def sea_of(y):
            return lane < counts[0, jnp.clip(y, 0, rows - 1)]

        def at(y):
            return pl.ds(pl.multiple_of(y * levels, levels), levels)

        def halo(neighbour):
            found = jnp.zeros(shape, jnp.float32)
            inside = (neighbour >= 0) & (neighbour < n_row)
            for part, ref in zip(near_parts, halos):
                found = jnp.where(inside & ((neighbour ^ row) == part), ref[0].astype(jnp.float32), found)
            return found

        west = jnp.where(col > 0, west_in[0].astype(jnp.float32), 0.0)
        east = jnp.where(col < n_col - 1, east_in[0].astype(jnp.float32), 0.0)
        sides = jnp.where((lane & 1) == 0, pltpu.roll(east, lanes - 1, 1), pltpu.roll(west, 1, 1))
        masked[0:levels, :] = jnp.where(step > 0, jnp.where(sea_of(base - 1), above[...], 0.0), halo(row - 1))
        masked[(block + 1) * levels:(block + 2) * levels, :] = jnp.where(
            step < steps - 1, jnp.where(sea_of(base + block), below[...], 0.0), halo(row + 1))

        def fill(g, carry):
            for s in range(8):
                y = g * 8 + s
                masked[at(y + 1), :] = jnp.where(sea_of(base + y), field[at(y), :], 0.0)
            return carry

        lax.fori_loop(0, block // 8, fill, 0)
        beside = beside_matrix()
        weights = jnp.concatenate([beside, side_matrix()], axis=0)
        spread = spread_matrix()

        def body(g, packed):
            here = masked[pl.ds(pl.multiple_of((g * batch + 1) * levels, levels), batch * levels), :]
            turned = jnp.concatenate(
                [jnp.where(pair_of == g * batch + s, sides, 0.0).astype(jnp.bfloat16) for s in range(batch)], axis=0)
            near = product(jnp.concatenate([here.astype(jnp.bfloat16), turned], axis=1), weights)
            new_rows = []
            for s in range(batch):
                y = g * batch + s
                part = slice(s * levels, (s + 1) * levels)
                lap = masked[at(y), :] + masked[at(y + 2), :] + near[part] - 4.0 * masked[at(y + 1), :]
                sea = sea_of(base + y)
                new = field[at(y), :] + jnp.where(sea, diffusion_rate * lap, 0.0)
                out[at(y), :] = new
                if final:
                    out[pl.ds(y * levels, 1), :] = new[0:1, :] + 0.3 * gap[pl.ds(y, 1), :]
                else:
                    new_rows.append(jnp.where(sea, new, 0.0).astype(jnp.bfloat16))
            if not final:
                spreads = product(jnp.concatenate(new_rows, axis=0), spread)
                for s in range(batch):
                    packed = jnp.where(pair_of == g * batch + s, spreads[s * levels:(s + 1) * levels], packed)
            return packed

        packed = lax.fori_loop(0, block // batch, body, jnp.zeros(shape, jnp.float32))
        if not final:
            edge[0] = packed.astype(jnp.bfloat16)

            @pl.when(step == 0)
            def _():
                ends[0] = jnp.where(sea_of(0), out[0:levels, :], 0.0).astype(jnp.bfloat16)

            @pl.when(step == steps - 1)
            def _():
                ends[1] = jnp.where(
                    sea_of(rows - 1), out[(block - 1) * levels:block * levels, :], 0.0
                ).astype(jnp.bfloat16)


def legendre_kernel(place, legendre, *rest, n_row, n_col, wave_dev, first_wave, with_ends):
    coeffs, rest = rest[:n_row], rest[n_row:]
    if with_ends:
        ends, rest = rest[0], rest[2:]
    out, gathered = rest[:n_row], rest[n_row]
    comp, row, _ = where_am_i(place, n_row, n_col)
    index = pl.program_id(0)
    lats = coeffs[0].shape[1]
    count = legendre.shape[2]

    @pl.when(comp == 0)
    def _():
        table = legendre[0]
        for part in range(n_row):
            gathered[part ^ row] = coeffs[part][0]
        fourier = gathered[...].reshape(n_row * lats, lanes)
        spectral = lax.dot_general(fourier, table, (((0,), (0,)), ((), ())), preferred_element_type=jnp.float32)
        wave = row * wave_dev + first_wave + index
        total = (wave + iota((1, count), 1)).astype(jnp.float32)
        ratio = total * (total + 1.0) / (1279.0 * 1280.0)
        damping = 1.0 / (1.0 + 20.0 * ratio * ratio)
        filtered = (spectral * damping).astype(jnp.bfloat16)
        result = lax.dot_general(table, filtered, (((1,), (1,)), ((), ())), preferred_element_type=jnp.float32)
        gathered[...] = result.astype(jnp.bfloat16).reshape(n_row, lats, lanes)
        for part in range(n_row):
            out[part][0] = gathered[part ^ row]

    if with_ends:
        @pl.when((comp != 0) & (index == 0))
        def _():
            levels = ends.shape[1]
            for part in range(1, n_row):
                out[part][0, 0:levels, :] = jnp.where((part ^ row) > row, ends[1], ends[0])


def surface_kernel(place, counts, partner, own, source, *rest, first, group, n_row, n_col):
    new, gap = rest[-2:]
    half = partner.shape[0] // 2
    width = 2 * lanes
    table = jnp.concatenate(
        [partner[pl.ds(0, half, stride=2), :], partner[pl.ds(1, half, stride=2), :]], axis=1
    ).astype(jnp.bfloat16)
    low_index = iota((width, lanes), 0)
    high_index = iota((half, lanes), 0)
    one = jnp.ones((width, lanes), jnp.bfloat16)
    zero = jnp.zeros((width, lanes), jnp.bfloat16)
    sublane = iota((8, lanes), 0)
    rate = jnp.where(where_am_i(place, n_row, n_col)[0] == 0, 0.5, 0.25).astype(jnp.float32)

    def body(g, carry):
        start = pl.multiple_of(g * 8, 8)
        entries = source[pl.ds(start, 8), :]
        low = entries & (width - 1)
        high = entries >> 8
        found = []
        for p in range(0, 8, group):
            pick = jnp.concatenate(
                [jnp.where(low_index == low[s:s + 1, :], one, zero) for s in range(p, p + group)], axis=1
            )
            picked = product(table, pick)
            for s in range(group):
                part = picked[:, lanes * s:lanes * (s + 1)]
                match = high_index == high[p + s:p + s + 1, :]
                found.append(jnp.sum(jnp.where(match, part, 0.0), axis=0, keepdims=True))
        pulled = jnp.concatenate(found, axis=0)
        limit = jnp.zeros((8, lanes), jnp.int32)
        for s in range(8):
            limit = jnp.where(sublane == s, counts[0, first + start + s], limit)
        here = own[pl.ds(start, 8), :]
        difference = jnp.where(iota((8, lanes), 1) < limit, pulled - here, 0.0)
        new[pl.ds(start, 8), :] = here + rate * difference
        gap[pl.ds(start, 8), :] = difference
        return carry

    lax.fori_loop(0, source.shape[0] // 8, body, 0)


def exit_kernel(place, sea, *rest, n_row, n_col, widths, block):
    chunks = len(widths)
    back = [rest[n_row * c:n_row * (c + 1)] for c in range(chunks)]
    out, table = rest[n_row * chunks:]
    comp, row, _ = where_am_i(place, n_row, n_col)
    levels = out.shape[0] // block
    wave_dev = levels // n_row
    flip = row * wave_dev

    def source(wave, lat, count):
        part, local = divmod(wave, wave_dev)
        chunk, slot = chunk_of(local, widths)
        return back[chunk][part][slot, lat:lat + count, :]

    @pl.when(comp == 0)
    def _():
        @pl.when(pl.program_id(0) == 0)
        def _():
            table[...] = swap_matrix(0, flip & 15)

        for lat in range(0, block - 15, 16):
            halves = [
                jnp.concatenate([source(half + wave, lat, 16) for wave in range(16)], axis=0)
                for half in range(0, levels, 16)
            ]
            turned = product(table[...], jnp.concatenate(halves, axis=1))
            for s in range(16):
                for half in range(0, levels, 16):
                    start = pl.multiple_of((lat + s) * levels + (half ^ (flip & ~15)), 16)
                    part = lanes * (half // 16)
                    out[pl.ds(start, 16), :] = turned[16 * s:16 * s + 16, part:part + lanes]
        for lat in range(block - block % 16, block, 8):
            for wave in range(levels):
                out[pl.ds(lat * levels + (wave ^ flip), 8, stride=levels), :] = source(wave, lat, 8).astype(jnp.float32)

    @pl.when(comp != 0)
    def _():
        out[...] = sea[...]


def shards(model_state, legendre, gauss_weight, mixing, surface, sea_count, remap_source):
    n_row, n_col = lax.axis_size("row"), lax.axis_size("col")
    rows, levels = model_state.shape[1], model_state.shape[2]
    wave_dev = levels // n_row
    widths = chunk_widths(wave_dev)
    chunks = len(widths)
    block = row_block(rows)
    steps = rows // block
    f32, bf16 = jnp.float32, jnp.bfloat16
    sds = jax.ShapeDtypeStruct
    mib = 1 << 20

    fields = model_state.reshape(rows * levels, lanes)
    counts = sea_count.reshape(1, rows)
    place = lax.axis_index(("comp", "row", "col")).astype(jnp.int32).reshape(1)
    own = surface[0]
    comp_size = lax.axis_size("comp")
    partner = lax.ppermute(own, "comp", [(i, comp_size - 1 - i) for i in range(comp_size)])

    def on(comp, i, s):
        return jnp.where(lax.div(s[0], n_row * n_col) == comp, i, 0)

    def call(kernel, grid, in_specs, out_specs, out_shape, args, scratch=(), vmem=59, flops=10**7, size=0, aliases={}):
        return pl.pallas_call(
            functools.partial(kernel, n_row=n_row, n_col=n_col),
            out_shape=out_shape,
            grid_spec=pltpu.PrefetchScalarGridSpec(
                num_scalar_prefetch=1, grid=grid, in_specs=in_specs, out_specs=out_specs, scratch_shapes=scratch),
            compiler_params=pltpu.CompilerParams(vmem_limit_bytes=vmem * mib),
            input_output_aliases=aliases,
            cost_estimate=cost(flops, size),
        )(place, *args)

    smem = pl.BlockSpec(memory_space=pltpu.SMEM)
    anywhere = pl.BlockSpec(memory_space=pl.ANY)
    state_bytes = 4 * rows * levels * lanes
    tall = block * levels

    *send, mixed, edge = call(
        functools.partial(entry_kernel, widths=widths, block=block), (steps,),
        [
            smem,
            pl.BlockSpec((tall, lanes), lambda i, s: (i, 0)),
            pl.BlockSpec((8 * levels, lanes), lambda i, s: (rows // 8 - 1, 0)),
            smem,
            pl.BlockSpec((levels, levels), lambda i, s: (0, 0)),
        ],
        [pl.BlockSpec((w, block, lanes), lambda i, s: (0, i, 0)) for w in widths for _ in range(n_row)]
        + [
            pl.BlockSpec((tall, lanes), lambda i, s: (on(1, i, s), 0)),
            pl.BlockSpec((1, levels, lanes), lambda i, s: (on(1, i, s), 0, 0)),
        ],
        [sds((w, rows, lanes), bf16) for w in widths for _ in range(n_row)]
        + [sds((rows * levels, lanes), f32), sds((steps, levels, lanes), bf16)],
        (counts, fields, fields, gauss_weight, mixing),
        scratch=[pltpu.VMEM((256, 256), bf16)], vmem=63, size=2 * state_bytes,
    )

    near_parts = [k for k in range(1, n_row) if k & (k + 1) == 0]
    both = ("comp", "row")

    def traded(parts, with_edges, relayed):
        got = [parts[0]]
        for k in range(1, n_row):
            route = [(r, r ^ k) for r in range(n_row)]
            if with_edges and k in near_parts:
                route += [(n_row + a, n_row + b) for a, b in route]
            if relayed and k > 1:
                halfway = lax.ppermute(parts[k], both, [(a, n_row + b) for a, b in route])
                got.append(lax.ppermute(halfway, both, [(n_row + r, r) for r in range(n_row)]))
            else:
                got.append(lax.ppermute(parts[k], both, route))
        return got

    chain = [n_col + i for i in range(n_col - 1)]

    def to_columns(x):
        return [
            lax.ppermute(x, ("comp", "col"), [(i + 1, i) for i in chain]),
            lax.ppermute(x, ("comp", "col"), [(i, i + 1) for i in chain]),
        ]

    coeffs = [traded(send[n_row * c:n_row * (c + 1)], c == chunks // 2, c == chunks - 1 > 0)
              for c in range(chunks)]
    sides = to_columns(edge)

    halves = 2 if rows % 16 == 0 else 1
    share = rows // halves
    whole = pl.BlockSpec((rows, lanes), lambda i, s: (0, 0))
    surfaces = []

    def remap(half, after):
        piece = pl.BlockSpec((share, lanes), lambda i, s: (half, 0))
        earlier = surfaces[-1] if surfaces else ()
        surfaces.append(call(
            functools.partial(surface_kernel, first=half * share, group=2), (1,),
            [smem, whole, piece, piece] + [anywhere] * (len(earlier) + len(after)),
            [piece] * 2, [sds((rows, lanes), f32)] * 2,
            (counts, partner, own, remap_source[0], *earlier, *after),
            aliases={5 + i: i for i in range(len(earlier))},
            flops=10**10, size=3 * 4 * rows * lanes,
        ))

    remap(0, (edge,))

    def sweep(field, rows_in, cols_in, final, extra=()):
        out_shape = [sds((rows * levels, lanes), f32)]
        out_specs = [pl.BlockSpec((tall, lanes), lambda i, s: (on(1, i, s), 0))]
        if not final:
            out_shape += [sds((steps, levels, lanes), bf16), sds((2, levels, lanes), bf16)]
            out_specs += [
                pl.BlockSpec((1, levels, lanes), lambda i, s: (on(1, i, s), 0, 0)),
                pl.BlockSpec((2, levels, lanes), lambda i, s: (0, 0, 0)),
            ]
        in_specs = [
            smem,
            pl.BlockSpec((tall, lanes), lambda i, s: (on(1, i, s), 0)),
            pl.BlockSpec((levels, lanes), lambda i, s: (jnp.maximum(on(1, i, s) * block - 1, 0), 0)),
            pl.BlockSpec((levels, lanes), lambda i, s: (jnp.minimum((on(1, i, s) + 1) * block, rows - 1), 0)),
            pl.BlockSpec((1, levels, lanes), lambda i, s: (on(1, i, s), 0, 0)),
            pl.BlockSpec((1, levels, lanes), lambda i, s: (on(1, i, s), 0, 0)),
        ] + [pl.BlockSpec((1, levels, lanes), lambda i, s: (0, 0, 0))] * len(near_parts) + ([pl.BlockSpec((block, lanes), lambda i, s: (on(1, i, s), 0))] if final else [])
        return call(
            functools.partial(sweep_kernel, block=block, near_parts=near_parts, final=final), (steps,),
            in_specs, out_specs, out_shape,
            (counts, field, field, field, *cols_in, *(rows_in[k] for k in near_parts), *extra),
            scratch=[pltpu.VMEM(((block + 2) * levels, lanes), f32)], size=2 * state_bytes,
        )

    first_step, edge, ends = sweep(mixed, coeffs[chunks // 2], sides, False)
    sides = to_columns(edge)

    returned = []
    for chunk, width in enumerate(widths):
        with_ends = chunk == chunks // 2
        first_wave = sum(widths[:chunk])
        part = call(
            functools.partial(legendre_kernel, wave_dev=wave_dev, first_wave=first_wave, with_ends=with_ends),
            (width,),
            [
                pl.BlockSpec((1,) + legendre.shape[1:],
                             lambda i, s, first_wave=first_wave: (first_wave + on(0, i, s), 0, 0)),
            ] + [pl.BlockSpec((1, rows, lanes), lambda i, s: (on(0, i, s), 0, 0))] * n_row + ([pl.BlockSpec((2, levels, lanes), lambda i, s: (0, 0, 0)), anywhere] if with_ends else []),
            [pl.BlockSpec((1, rows, lanes), lambda i, s: (on(0, i, s), 0, 0))] * n_row,
            [sds((width, rows, lanes), bf16)] * n_row,
            (legendre, *coeffs[chunk], *([ends, surfaces[0][1]] if with_ends else [])),
            scratch=[pltpu.VMEM((n_row, rows, lanes), bf16)], vmem=63, flops=4 * width * legendre.shape[1] * legendre.shape[2] * lanes,
            size=2 * width * legendre.shape[1] * legendre.shape[2],
        )
        returned.append(traded(part, with_ends, chunk == 0 < chunks - 1))

    if halves > 1:
        remap(1, (first_step,))
    new_surface, gap = surfaces[-1]
    (sea,) = sweep(first_step, returned[chunks // 2], sides, True, (gap,))

    state = call(
        functools.partial(exit_kernel, widths=widths, block=block), (steps,),
        [pl.BlockSpec((tall, lanes), lambda i, s: (on(1, i, s), 0))]
        + [pl.BlockSpec((w, block, lanes), lambda i, s: (0, on(0, i, s), 0)) for w in widths for _ in range(n_row)],
        pl.BlockSpec((tall, lanes), lambda i, s: (i, 0)),
        sds((rows * levels, lanes), f32),
        (sea, *sum(returned, [])), scratch=[pltpu.VMEM((256, 256), bf16)], size=2 * state_bytes,
    )
    return state.reshape(model_state.shape), new_surface[None]


def solution(mesh):
    in_specs = (
        P("comp", "row", None, "col"),
        P("row", None, None),
        P("row"),
        P(),
        P("comp", "row", "col"),
        P("comp", "row", "col"),
        P("comp", "row", "col"),
    )
    out_specs = (P("comp", "row", None, "col"), P("comp", "row", "col"))

    return jax.shard_map(shards, mesh=mesh, in_specs=in_specs, out_specs=out_specs, check_vma=False)
```

```python
import functools

import jax
import jax.numpy as jnp
from jax import lax
from jax.experimental import pallas as pl
from jax.experimental.pallas import tpu as pltpu
from jax.sharding import PartitionSpec as P


diffusion_rate = 0.2
lanes = 128


def chunk_widths(wave_dev):
    return (wave_dev - wave_dev // 2, wave_dev // 2) if wave_dev > 1 else (wave_dev,)


def chunk_of(local, widths):
    chunk = 0
    while local >= widths[chunk]:
        local -= widths[chunk]
        chunk += 1
    return chunk, local


def row_block(rows):
    return 64 if rows % 64 == 0 else rows


def cost(flops, bytes_accessed):
    return pl.CostEstimate(flops=flops, bytes_accessed=bytes_accessed, transcendentals=0)


def where_am_i(place, n_row, n_col):
    flat = place[0]
    return (
        lax.div(flat, n_row * n_col),
        lax.rem(lax.div(flat, n_col), n_row),
        lax.rem(flat, n_col),
    )


def iota(shape, dim):
    return lax.broadcasted_iota(jnp.int32, shape, dim)


def as_bf16(mask):
    return jnp.where(mask, 1.0, 0.0).astype(jnp.bfloat16)


def swap_matrix(flip_high, flip_low):
    row, column = iota((256, 256), 0), iota((256, 256), 1)
    return as_bf16(column == (((row & 15) ^ flip_low) << 4 | ((row >> 4) ^ flip_high)))


def spread_matrix():
    row, column = iota((lanes, lanes), 0), iota((lanes, lanes), 1)
    odd = column & 1
    return as_bf16(((row == lanes - 1) & (odd == 0)) | ((row == 0) & (odd == 1)))


def beside_matrix():
    row, column = iota((lanes, lanes), 0), iota((lanes, lanes), 1)
    return as_bf16((row == column + 1) | (row + 1 == column))


def side_matrix():
    row, column = iota((lanes, lanes), 0), iota((lanes, lanes), 1)
    odd = row & 1
    return as_bf16(((column == 0) & (odd == 1)) | ((column == lanes - 1) & (odd == 0)))


def split(value):
    high = value.astype(jnp.bfloat16)
    return high, (value - high.astype(jnp.float32)).astype(jnp.bfloat16)


def product(a, b):
    return jnp.dot(a, b, preferred_element_type=jnp.float32)


def entry_kernel(place, counts, field, last, gauss, mix, *rest, n_row, n_col, widths, block):
    chunks = len(widths)
    send = [rest[n_row * c:n_row * (c + 1)] for c in range(chunks)]
    mixed, edge, table = rest[n_row * chunks:]
    comp, row, _ = where_am_i(place, n_row, n_col)
    levels = field.shape[0] // block
    wave_dev = levels // n_row
    step = pl.program_id(0)

    flip = row * wave_dev

    def target(wave):
        part, local = divmod(wave, wave_dev)
        chunk, slot = chunk_of(local, widths)
        return send[chunk][part], slot

    @pl.when(comp == 0)
    def _():
        @pl.when(step == 0)
        def _():
            table[...] = swap_matrix(flip & 15, 0)

        for lat in range(0, block - 15, 16):
            halves = []
            for half in range(0, levels, 16):
                halves.append(jnp.concatenate([
                    (field[pl.ds(pl.multiple_of((lat + s) * levels + (half ^ (flip & ~15)), 16), 16), :]
                     * gauss[step * block + lat + s]).astype(jnp.bfloat16)
                    for s in range(16)
                ], axis=0))
            turned = product(table[...], jnp.concatenate(halves, axis=1)).astype(jnp.bfloat16)
            for wave in range(levels):
                out, slot = target(wave)
                part = lanes * (wave // 16)
                out[slot, lat:lat + 16, :] = turned[16 * (wave % 16):16 * (wave % 16) + 16, part:part + lanes]
        for lat in range(block - block % 16, block, 8):
            weight = jnp.zeros((8, lanes), jnp.float32)
            for s in range(8):
                weight = jnp.where(iota((8, lanes), 0) == s, gauss[step * block + lat + s], weight)
            for wave in range(levels):
                out, slot = target(wave)
                values = field[pl.ds(lat * levels + (wave ^ flip), 8, stride=levels), :] * weight
                out[slot, lat:lat + 8, :] = values.astype(jnp.bfloat16)

    def mixed_rows(ref, start, first_row):
        values = []
        for quarter in range(2):
            parts = []
            for pair in range(2):
                part = ref[pl.ds(start + (2 * quarter + pair) * 2 * levels, 2 * levels), :]
                values.append(part)
                parts.append(split(part))
            high = jnp.concatenate([p[0] for p in parts], axis=1)
            low = jnp.concatenate([p[1] for p in parts], axis=1)
            blend = product(table[0:2 * levels, :], jnp.concatenate([high, low, high, low], axis=0))
            values += [blend[:, :lanes], blend[:, lanes:]]
        out = []
        for s in range(8):
            quarter, pair, place_in = s // 4, s // 2 % 2, slice(levels * (s % 2), levels * (s % 2) + levels)
            heat = values[4 * quarter + pair][place_in]
            blend = values[4 * quarter + 2 + pair][place_in]
            sea = iota((levels, lanes), 1) < counts[0, first_row + s]
            value = heat + jnp.where(sea, blend, 0.0)
            out.append((value, jnp.where(sea, value, 0.0).astype(jnp.bfloat16)))
        return out

    @pl.when(comp != 0)
    def _():
        @pl.when(step == 0)
        def _():
            high, low = split(mix[...])
            repeat = as_bf16((iota((levels, 256), 1) & (levels - 1)) == iota((levels, 256), 0))
            wide = jnp.where(iota((levels, 256), 1) < 4 * levels, product(high, repeat), product(low, repeat))
            wide = jnp.concatenate([wide, wide], axis=0)
            shape = (2 * levels, 256)
            own = (iota(shape, 1) // levels & 1) == iota(shape, 0) // levels
            table[0:2 * levels, :] = jnp.where(own, wide, 0.0).astype(jnp.bfloat16)

        spread = spread_matrix()
        pair_of = iota((levels, lanes), 1) >> 1

        batch = 32 if block % 32 == 0 else 8

        def body(g, packed):
            rows = []
            for first in range(0, batch, 8):
                start = pl.multiple_of((g * batch + first) * levels, 8 * levels)
                some = mixed_rows(field, start, step * block + g * batch + first)
                for s, (value, _) in enumerate(some):
                    mixed[pl.ds(pl.multiple_of(start + s * levels, levels), levels), :] = value
                rows += some
            ends = product(jnp.concatenate([r[1] for r in rows], axis=0), spread)
            for s in range(batch):
                packed = jnp.where(pair_of == g * batch + s, ends[s * levels:(s + 1) * levels], packed)
            return packed

        packed = lax.fori_loop(0, block // batch, body, jnp.zeros((levels, lanes), jnp.float32))
        edge[0] = packed.astype(jnp.bfloat16)

        @pl.when(step == 0)
        def _():
            total = pl.num_programs(0) * block
            top = mixed_rows(field, 0, 0)[0][1]
            low = mixed_rows(last, 0, total - 8)[-1][1]
            for part in range(1, n_row):
                send[0][part][0, 0:levels, :] = jnp.where((part ^ row) > row, low, top)


def sweep_kernel(place, counts, field, above, below, east_in, west_in, *rest, block, n_row, n_col, near_parts, final):
    halos, rest = rest[:len(near_parts)], rest[len(near_parts):]
    if final:
        gap, out, masked = rest
    else:
        out, edge, ends, masked = rest
    comp, row, col = where_am_i(place, n_row, n_col)
    levels = field.shape[0] // block
    step = pl.program_id(0)
    steps = pl.num_programs(0)
    rows = steps * block
    base = step * block
    shape = (levels, lanes)
    batch = 32 if block % 32 == 0 else 8

    @pl.when(comp != 0)
    def _():
        lane = iota(shape, 1)
        pair_of = lane >> 1

        def sea_of(y):
            return lane < counts[0, jnp.clip(y, 0, rows - 1)]

        def at(y):
            return pl.ds(pl.multiple_of(y * levels, levels), levels)

        def halo(neighbour):
            found = jnp.zeros(shape, jnp.float32)
            inside = (neighbour >= 0) & (neighbour < n_row)
            for part, ref in zip(near_parts, halos):
                found = jnp.where(inside & ((neighbour ^ row) == part), ref[0].astype(jnp.float32), found)
            return found

        west = jnp.where(col > 0, west_in[0].astype(jnp.float32), 0.0)
        east = jnp.where(col < n_col - 1, east_in[0].astype(jnp.float32), 0.0)
        sides = jnp.where((lane & 1) == 0, pltpu.roll(east, lanes - 1, 1), pltpu.roll(west, 1, 1))
        masked[0:levels, :] = jnp.where(step > 0, jnp.where(sea_of(base - 1), above[...], 0.0), halo(row - 1))
        masked[(block + 1) * levels:(block + 2) * levels, :] = jnp.where(
            step < steps - 1, jnp.where(sea_of(base + block), below[...], 0.0), halo(row + 1))

        def fill(g, carry):
            for s in range(8):
                y = g * 8 + s
                masked[at(y + 1), :] = jnp.where(sea_of(base + y), field[at(y), :], 0.0)
            return carry

        lax.fori_loop(0, block // 8, fill, 0)
        beside = beside_matrix()
        weights = jnp.concatenate([beside, side_matrix()], axis=0)
        spread = spread_matrix()

        def body(g, packed):
            here = masked[pl.ds(pl.multiple_of((g * batch + 1) * levels, levels), batch * levels), :]
            turned = jnp.concatenate(
                [jnp.where(pair_of == g * batch + s, sides, 0.0).astype(jnp.bfloat16) for s in range(batch)], axis=0)
            near = product(jnp.concatenate([here.astype(jnp.bfloat16), turned], axis=1), weights)
            new_rows = []
            for s in range(batch):
                y = g * batch + s
                part = slice(s * levels, (s + 1) * levels)
                lap = masked[at(y), :] + masked[at(y + 2), :] + near[part] - 4.0 * masked[at(y + 1), :]
                sea = sea_of(base + y)
                new = field[at(y), :] + jnp.where(sea, diffusion_rate * lap, 0.0)
                out[at(y), :] = new
                if final:
                    out[pl.ds(y * levels, 1), :] = new[0:1, :] + 0.3 * gap[pl.ds(y, 1), :]
                else:
                    new_rows.append(jnp.where(sea, new, 0.0).astype(jnp.bfloat16))
            if not final:
                spreads = product(jnp.concatenate(new_rows, axis=0), spread)
                for s in range(batch):
                    packed = jnp.where(pair_of == g * batch + s, spreads[s * levels:(s + 1) * levels], packed)
            return packed

        packed = lax.fori_loop(0, block // batch, body, jnp.zeros(shape, jnp.float32))
        if not final:
            edge[0] = packed.astype(jnp.bfloat16)

            @pl.when(step == 0)
            def _():
                ends[0] = jnp.where(sea_of(0), out[0:levels, :], 0.0).astype(jnp.bfloat16)

            @pl.when(step == steps - 1)
            def _():
                ends[1] = jnp.where(
                    sea_of(rows - 1), out[(block - 1) * levels:block * levels, :], 0.0
                ).astype(jnp.bfloat16)


def legendre_kernel(place, legendre, *rest, n_row, n_col, wave_dev, first_wave, with_ends):
    coeffs, rest = rest[:n_row], rest[n_row:]
    if with_ends:
        ends, rest = rest[0], rest[2:]
    out, gathered = rest[:n_row], rest[n_row]
    comp, row, _ = where_am_i(place, n_row, n_col)
    index = pl.program_id(0)
    lats = coeffs[0].shape[1]
    count = legendre.shape[2]

    @pl.when(comp == 0)
    def _():
        table = legendre[0]
        for part in range(n_row):
            gathered[part ^ row] = coeffs[part][0]
        fourier = gathered[...].reshape(n_row * lats, lanes)
        spectral = lax.dot_general(fourier, table, (((0,), (0,)), ((), ())), preferred_element_type=jnp.float32)
        wave = row * wave_dev + first_wave + index
        total = (wave + iota((1, count), 1)).astype(jnp.float32)
        ratio = total * (total + 1.0) / (1279.0 * 1280.0)
        damping = 1.0 / (1.0 + 20.0 * ratio * ratio)
        filtered = (spectral * damping).astype(jnp.bfloat16)
        result = lax.dot_general(table, filtered, (((1,), (1,)), ((), ())), preferred_element_type=jnp.float32)
        gathered[...] = result.astype(jnp.bfloat16).reshape(n_row, lats, lanes)
        for part in range(n_row):
            out[part][0] = gathered[part ^ row]

    if with_ends:
        @pl.when((comp != 0) & (index == 0))
        def _():
            levels = ends.shape[1]
            for part in range(1, n_row):
                out[part][0, 0:levels, :] = jnp.where((part ^ row) > row, ends[1], ends[0])


def surface_kernel(place, counts, partner, own, source, *rest, first, group, n_row, n_col):
    new, gap = rest[-2:]
    half = partner.shape[0] // 2
    width = 2 * lanes
    table = jnp.concatenate(
        [partner[pl.ds(0, half, stride=2), :], partner[pl.ds(1, half, stride=2), :]], axis=1
    ).astype(jnp.bfloat16)
    low_index = iota((width, lanes), 0)
    high_index = iota((half, lanes), 0)
    one = jnp.ones((width, lanes), jnp.bfloat16)
    zero = jnp.zeros((width, lanes), jnp.bfloat16)
    sublane = iota((8, lanes), 0)
    rate = jnp.where(where_am_i(place, n_row, n_col)[0] == 0, 0.5, 0.25).astype(jnp.float32)

    def body(g, carry):
        start = pl.multiple_of(g * 8, 8)
        entries = source[pl.ds(start, 8), :]
        low = entries & (width - 1)
        high = entries >> 8
        found = []
        for p in range(0, 8, group):
            pick = jnp.concatenate(
                [jnp.where(low_index == low[s:s + 1, :], one, zero) for s in range(p, p + group)], axis=1
            )
            picked = product(table, pick)
            for s in range(group):
                part = picked[:, lanes * s:lanes * (s + 1)]
                match = high_index == high[p + s:p + s + 1, :]
                found.append(jnp.sum(jnp.where(match, part, 0.0), axis=0, keepdims=True))
        pulled = jnp.concatenate(found, axis=0)
        limit = jnp.zeros((8, lanes), jnp.int32)
        for s in range(8):
            limit = jnp.where(sublane == s, counts[0, first + start + s], limit)
        here = own[pl.ds(start, 8), :]
        difference = jnp.where(iota((8, lanes), 1) < limit, pulled - here, 0.0)
        new[pl.ds(start, 8), :] = here + rate * difference
        gap[pl.ds(start, 8), :] = difference
        return carry

    lax.fori_loop(0, source.shape[0] // 8, body, 0)


def exit_kernel(place, sea, *rest, n_row, n_col, widths, block):
    chunks = len(widths)
    back = [rest[n_row * c:n_row * (c + 1)] for c in range(chunks)]
    out, table = rest[n_row * chunks:]
    comp, row, _ = where_am_i(place, n_row, n_col)
    levels = out.shape[0] // block
    wave_dev = levels // n_row
    flip = row * wave_dev

    def source(wave, lat, count):
        part, local = divmod(wave, wave_dev)
        chunk, slot = chunk_of(local, widths)
        return back[chunk][part][slot, lat:lat + count, :]

    @pl.when(comp == 0)
    def _():
        @pl.when(pl.program_id(0) == 0)
        def _():
            table[...] = swap_matrix(0, flip & 15)

        for lat in range(0, block - 15, 16):
            halves = [
                jnp.concatenate([source(half + wave, lat, 16) for wave in range(16)], axis=0)
                for half in range(0, levels, 16)
            ]
            turned = product(table[...], jnp.concatenate(halves, axis=1))
            for s in range(16):
                for half in range(0, levels, 16):
                    start = pl.multiple_of((lat + s) * levels + (half ^ (flip & ~15)), 16)
                    part = lanes * (half // 16)
                    out[pl.ds(start, 16), :] = turned[16 * s:16 * s + 16, part:part + lanes]
        for lat in range(block - block % 16, block, 8):
            for wave in range(levels):
                out[pl.ds(lat * levels + (wave ^ flip), 8, stride=levels), :] = source(wave, lat, 8).astype(jnp.float32)

    @pl.when(comp != 0)
    def _():
        out[...] = sea[...]


def shards(model_state, legendre, gauss_weight, mixing, surface, sea_count, remap_source):
    n_row, n_col = lax.axis_size("row"), lax.axis_size("col")
    rows, levels = model_state.shape[1], model_state.shape[2]
    wave_dev = levels // n_row
    widths = chunk_widths(wave_dev)
    chunks = len(widths)
    block = row_block(rows)
    steps = rows // block
    f32, bf16 = jnp.float32, jnp.bfloat16
    sds = jax.ShapeDtypeStruct
    mib = 1 << 20

    fields = model_state.reshape(rows * levels, lanes)
    counts = sea_count.reshape(1, rows)
    place = lax.axis_index(("comp", "row", "col")).astype(jnp.int32).reshape(1)
    own = surface[0]
    comp_size = lax.axis_size("comp")
    partner = lax.ppermute(own, "comp", [(i, comp_size - 1 - i) for i in range(comp_size)])

    def on(comp, i, s):
        return jnp.where(lax.div(s[0], n_row * n_col) == comp, i, 0)

    def call(kernel, grid, in_specs, out_specs, out_shape, args, scratch=(), vmem=59, flops=10**7, size=0, aliases={}):
        return pl.pallas_call(
            functools.partial(kernel, n_row=n_row, n_col=n_col),
            out_shape=out_shape,
            grid_spec=pltpu.PrefetchScalarGridSpec(
                num_scalar_prefetch=1, grid=grid, in_specs=in_specs, out_specs=out_specs, scratch_shapes=scratch),
            compiler_params=pltpu.CompilerParams(vmem_limit_bytes=vmem * mib),
            input_output_aliases=aliases,
            cost_estimate=cost(flops, size),
        )(place, *args)

    smem = pl.BlockSpec(memory_space=pltpu.SMEM)
    anywhere = pl.BlockSpec(memory_space=pl.ANY)
    state_bytes = 4 * rows * levels * lanes
    tall = block * levels

    *send, mixed, edge = call(
        functools.partial(entry_kernel, widths=widths, block=block), (steps,),
        [
            smem,
            pl.BlockSpec((tall, lanes), lambda i, s: (i, 0)),
            pl.BlockSpec((8 * levels, lanes), lambda i, s: (rows // 8 - 1, 0)),
            smem,
            pl.BlockSpec((levels, levels), lambda i, s: (0, 0)),
        ],
        [pl.BlockSpec((w, block, lanes), lambda i, s: (0, i, 0)) for w in widths for _ in range(n_row)]
        + [
            pl.BlockSpec((tall, lanes), lambda i, s: (on(1, i, s), 0)),
            pl.BlockSpec((1, levels, lanes), lambda i, s: (on(1, i, s), 0, 0)),
        ],
        [sds((w, rows, lanes), bf16) for w in widths for _ in range(n_row)]
        + [sds((rows * levels, lanes), f32), sds((steps, levels, lanes), bf16)],
        (counts, fields, fields, gauss_weight, mixing),
        scratch=[pltpu.VMEM((256, 256), bf16)], vmem=63, size=2 * state_bytes,
    )

    near_parts = [k for k in range(1, n_row) if k & (k + 1) == 0]

    def traded(parts):
        got = [parts[0]]
        for k in range(1, n_row):
            got.append(lax.ppermute(parts[k], "row", [(r, r ^ k) for r in range(n_row)]))
        return got

    chain = [n_col + i for i in range(n_col - 1)]

    def to_columns(x):
        return [
            lax.ppermute(x, ("comp", "col"), [(i + 1, i) for i in chain]),
            lax.ppermute(x, ("comp", "col"), [(i, i + 1) for i in chain]),
        ]

    coeffs = [traded(send[n_row * c:n_row * (c + 1)]) for c in range(chunks)]
    sides = to_columns(edge)

    halves = 2 if rows % 16 == 0 else 1
    share = rows // halves
    whole = pl.BlockSpec((rows, lanes), lambda i, s: (0, 0))
    surfaces = []

    def remap(half, after):
        piece = pl.BlockSpec((share, lanes), lambda i, s: (half, 0))
        earlier = surfaces[-1] if surfaces else ()
        surfaces.append(call(
            functools.partial(surface_kernel, first=half * share, group=2), (1,),
            [smem, whole, piece, piece] + [anywhere] * (len(earlier) + len(after)),
            [piece] * 2, [sds((rows, lanes), f32)] * 2,
            (counts, partner, own, remap_source[0], *earlier, *after),
            aliases={5 + i: i for i in range(len(earlier))},
            flops=10**10, size=3 * 4 * rows * lanes,
        ))

    remap(0, (edge,))

    def sweep(field, rows_in, cols_in, final, extra=()):
        out_shape = [sds((rows * levels, lanes), f32)]
        out_specs = [pl.BlockSpec((tall, lanes), lambda i, s: (on(1, i, s), 0))]
        if not final:
            out_shape += [sds((steps, levels, lanes), bf16), sds((2, levels, lanes), bf16)]
            out_specs += [
                pl.BlockSpec((1, levels, lanes), lambda i, s: (on(1, i, s), 0, 0)),
                pl.BlockSpec((2, levels, lanes), lambda i, s: (0, 0, 0)),
            ]
        in_specs = [
            smem,
            pl.BlockSpec((tall, lanes), lambda i, s: (on(1, i, s), 0)),
            pl.BlockSpec((levels, lanes), lambda i, s: (jnp.maximum(on(1, i, s) * block - 1, 0), 0)),
            pl.BlockSpec((levels, lanes), lambda i, s: (jnp.minimum((on(1, i, s) + 1) * block, rows - 1), 0)),
            pl.BlockSpec((1, levels, lanes), lambda i, s: (on(1, i, s), 0, 0)),
            pl.BlockSpec((1, levels, lanes), lambda i, s: (on(1, i, s), 0, 0)),
        ] + [pl.BlockSpec((1, levels, lanes), lambda i, s: (0, 0, 0))] * len(near_parts) + ([pl.BlockSpec((block, lanes), lambda i, s: (on(1, i, s), 0))] if final else [])
        return call(
            functools.partial(sweep_kernel, block=block, near_parts=near_parts, final=final), (steps,),
            in_specs, out_specs, out_shape,
            (counts, field, field, field, *cols_in, *(rows_in[k] for k in near_parts), *extra),
            scratch=[pltpu.VMEM(((block + 2) * levels, lanes), f32)], size=2 * state_bytes,
        )

    first_step, edge, ends = sweep(mixed, coeffs[0], sides, False)
    sides = to_columns(edge)

    returned = []
    for chunk, width in enumerate(widths):
        with_ends = chunk == 0
        first_wave = sum(widths[:chunk])
        part = call(
            functools.partial(legendre_kernel, wave_dev=wave_dev, first_wave=first_wave, with_ends=with_ends),
            (width,),
            [
                pl.BlockSpec((1,) + legendre.shape[1:],
                             lambda i, s, first_wave=first_wave: (first_wave + on(0, i, s), 0, 0)),
            ] + [pl.BlockSpec((1, rows, lanes), lambda i, s: (on(0, i, s), 0, 0))] * n_row + ([pl.BlockSpec((2, levels, lanes), lambda i, s: (0, 0, 0)), anywhere] if with_ends else []),
            [pl.BlockSpec((1, rows, lanes), lambda i, s: (on(0, i, s), 0, 0))] * n_row,
            [sds((width, rows, lanes), bf16)] * n_row,
            (legendre, *coeffs[chunk], *([ends, surfaces[0][1]] if with_ends else [])),
            scratch=[pltpu.VMEM((n_row, rows, lanes), bf16)], vmem=63, flops=4 * width * legendre.shape[1] * legendre.shape[2] * lanes,
            size=2 * width * legendre.shape[1] * legendre.shape[2],
        )
        returned.append(traded(part))

    if halves > 1:
        remap(1, (first_step,))
    new_surface, gap = surfaces[-1]
    (sea,) = sweep(first_step, returned[0], sides, True, (gap,))

    state = call(
        functools.partial(exit_kernel, widths=widths, block=block), (steps,),
        [pl.BlockSpec((tall, lanes), lambda i, s: (on(1, i, s), 0))]
        + [pl.BlockSpec((w, block, lanes), lambda i, s: (0, on(0, i, s), 0)) for w in widths for _ in range(n_row)],
        pl.BlockSpec((tall, lanes), lambda i, s: (i, 0)),
        sds((rows * levels, lanes), f32),
        (sea, *sum(returned, [])), scratch=[pltpu.VMEM((256, 256), bf16)], size=2 * state_bytes,
    )
    return state.reshape(model_state.shape), new_surface[None]


def solution(mesh):
    in_specs = (
        P("comp", "row", None, "col"),
        P("row", None, None),
        P("row"),
        P(),
        P("comp", "row", "col"),
        P("comp", "row", "col"),
        P("comp", "row", "col"),
    )
    out_specs = (P("comp", "row", None, "col"), P("comp", "row", "col"))

    return jax.shard_map(shards, mesh=mesh, in_specs=in_specs, out_specs=out_specs, check_vma=False)
```

```python
import functools

import jax
import jax.numpy as jnp
from jax import lax
from jax.experimental import pallas as pl
from jax.experimental.pallas import tpu as pltpu
from jax.sharding import PartitionSpec as P


diffusion_rate = 0.2
lanes = 128


def chunk_widths(wave_dev):
    return (wave_dev - wave_dev // 2, wave_dev // 2) if wave_dev > 1 else (wave_dev,)


def chunk_of(local, widths):
    chunk = 0
    while local >= widths[chunk]:
        local -= widths[chunk]
        chunk += 1
    return chunk, local


def row_block(rows):
    return 160 if rows % 160 == 0 else rows


def cost(flops, bytes_accessed):
    return pl.CostEstimate(flops=flops, bytes_accessed=bytes_accessed, transcendentals=0)


def where_am_i(place, n_row, n_col):
    flat = place[0]
    return (
        lax.div(flat, n_row * n_col),
        lax.rem(lax.div(flat, n_col), n_row),
        lax.rem(flat, n_col),
    )


def iota(shape, dim):
    return lax.broadcasted_iota(jnp.int32, shape, dim)


def as_bf16(mask):
    return jnp.where(mask, 1.0, 0.0).astype(jnp.bfloat16)


def swap_matrix(flip_high, flip_low):
    row, column = iota((256, 256), 0), iota((256, 256), 1)
    return as_bf16(column == (((row & 15) ^ flip_low) << 4 | ((row >> 4) ^ flip_high)))


def spread_matrix():
    row, column = iota((lanes, lanes), 0), iota((lanes, lanes), 1)
    odd = column & 1
    return as_bf16(((row == lanes - 1) & (odd == 0)) | ((row == 0) & (odd == 1)))


def beside_matrix():
    row, column = iota((lanes, lanes), 0), iota((lanes, lanes), 1)
    return as_bf16((row == column + 1) | (row + 1 == column))


def side_matrix():
    row, column = iota((lanes, lanes), 0), iota((lanes, lanes), 1)
    odd = row & 1
    return as_bf16(((column == 0) & (odd == 1)) | ((column == lanes - 1) & (odd == 0)))


def split(value):
    high = value.astype(jnp.bfloat16)
    return high, (value - high.astype(jnp.float32)).astype(jnp.bfloat16)


def product(a, b):
    return jnp.dot(a, b, preferred_element_type=jnp.float32)


def entry_kernel(place, counts, field, gauss, mix, *rest, n_row, n_col, widths, block):
    chunks = len(widths)
    send = [rest[n_row * c:n_row * (c + 1)] for c in range(chunks)]
    mixed, edge, table, packed, ends = rest[n_row * chunks:]
    comp, row, _ = where_am_i(place, n_row, n_col)
    levels = mix.shape[0]
    wave_dev = levels // n_row
    tall = block * levels
    steps = field.shape[0] // tall
    state_block = pl.BlockSpec((tall, lanes), lambda i: (i, 0))

    flip = row * wave_dev

    def weigh(field, *parts):
        step = pl.program_id(0)

        def target(wave):
            part, local = divmod(wave, wave_dev)
            chunk, slot = chunk_of(local, widths)
            return parts[n_row * chunk + part], slot

        for lat in range(0, block - 15, 16):
            halves = []
            for half in range(0, levels, 16):
                halves.append(jnp.concatenate([
                    (field[pl.ds(pl.multiple_of((lat + s) * levels + (half ^ (flip & ~15)), 16), 16), :]
                     * gauss[step * block + lat + s]).astype(jnp.bfloat16)
                    for s in range(16)
                ], axis=0))
            turned = product(table[...], jnp.concatenate(halves, axis=1)).astype(jnp.bfloat16)
            for wave in range(levels):
                out, slot = target(wave)
                part = lanes * (wave // 16)
                out[slot, lat:lat + 16, :] = turned[16 * (wave % 16):16 * (wave % 16) + 16, part:part + lanes]
        for lat in range(block - block % 16, block, 8):
            weight = jnp.zeros((8, lanes), jnp.float32)
            for s in range(8):
                weight = jnp.where(iota((8, lanes), 0) == s, gauss[step * block + lat + s], weight)
            for wave in range(levels):
                out, slot = target(wave)
                values = field[pl.ds(lat * levels + (wave ^ flip), 8, stride=levels), :] * weight
                out[slot, lat:lat + 8, :] = values.astype(jnp.bfloat16)

    @pl.when(comp == 0)
    def _():
        table[...] = swap_matrix(flip & 15, 0)
        pltpu.emit_pipeline(
            weigh, grid=(steps,), in_specs=[state_block],
            out_specs=[pl.BlockSpec((w, block, lanes), lambda i: (0, i, 0)) for w in widths for _ in range(n_row)],
        )(field, *sum(send, ()))

    def mixed_rows(ref, start, first_row):
        values = []
        for quarter in range(2):
            parts = []
            for pair in range(2):
                part = ref[pl.ds(start + (2 * quarter + pair) * 2 * levels, 2 * levels), :]
                values.append(part)
                parts.append(split(part))
            high = jnp.concatenate([p[0] for p in parts], axis=1)
            low = jnp.concatenate([p[1] for p in parts], axis=1)
            blend = product(table[0:2 * levels, :], jnp.concatenate([high, low, high, low], axis=0))
            values += [blend[:, :lanes], blend[:, lanes:]]
        out = []
        for s in range(8):
            quarter, pair, place_in = s // 4, s // 2 % 2, slice(levels * (s % 2), levels * (s % 2) + levels)
            heat = values[4 * quarter + pair][place_in]
            blend = values[4 * quarter + 2 + pair][place_in]
            sea = iota((levels, lanes), 1) < counts[0, first_row + s]
            value = heat + jnp.where(sea, blend, 0.0)
            out.append((value, jnp.where(sea, value, 0.0).astype(jnp.bfloat16)))
        return out

    @pl.when(comp != 0)
    def _():
        high, low = split(mix[...])
        repeat = as_bf16((iota((levels, 256), 1) & (levels - 1)) == iota((levels, 256), 0))
        wide = jnp.where(iota((levels, 256), 1) < 4 * levels, product(high, repeat), product(low, repeat))
        wide = jnp.concatenate([wide, wide], axis=0)
        shape = (2 * levels, 256)
        own = (iota(shape, 1) // levels & 1) == iota(shape, 0) // levels
        table[0:2 * levels, :] = jnp.where(own, wide, 0.0).astype(jnp.bfloat16)
        packed[...] = jnp.zeros_like(packed)
        batch = 32 if block % 32 == 0 else 8

        def blend(field, mixed):
            step = pl.program_id(0)
            spread = spread_matrix()

            def body(g, carry):
                base = step * block + g * batch
                rows = []
                for first in range(0, batch, 8):
                    start = pl.multiple_of((g * batch + first) * levels, 8 * levels)
                    some = mixed_rows(field, start, base + first)
                    for s, (value, _) in enumerate(some):
                        mixed[pl.ds(pl.multiple_of(start + s * levels, levels), levels), :] = value
                    rows += some
                pack(packed, base, [r[1] for r in rows], spread)
                return carry

            lax.fori_loop(0, block // batch, body, 0)

            @pl.when(step == 0)
            def _():
                ends[0] = mixed_rows(field, 0, 0)[0][1]

            @pl.when(step == steps - 1)
            def _():
                ends[1] = mixed_rows(field, tall - 8 * levels, steps * block - 8)[-1][1]

        pltpu.emit_pipeline(blend, grid=(steps,), in_specs=[state_block], out_specs=[state_block])(field, mixed)
        edge[...] = packed[...].astype(jnp.bfloat16)
        hand_on(ends, send[0], row)


def hand_on(ends, parts, row):
    levels = ends.shape[1]
    for k in range(1, len(parts)):
        pltpu.sync_copy(ends.at[((k ^ row) > row).astype(jnp.int32)], parts[k].at[0, pl.ds(0, levels)])


def pack(packed, base, rows, spread):
    levels = packed.shape[1]
    ends = product(jnp.concatenate(rows, axis=0), spread)
    pair_of = iota((levels, lanes), 1) >> 1
    slot = base >> 6
    kept = packed[slot]
    for s in range(len(rows)):
        kept = jnp.where(pair_of == (base & 63) + s, ends[s * levels:(s + 1) * levels], kept)
    packed[slot] = kept


def sweep_kernel(place, counts, field, east_in, west_in, *rest, block, n_row, n_col, near_parts, final):
    halos, rest = rest[:len(near_parts)], rest[len(near_parts):]
    if final:
        gap, out, masked, sides = rest
    else:
        out, edge, ends, masked, sides, packed = rest
    comp, row, col = where_am_i(place, n_row, n_col)
    levels = sides.shape[1]
    tall = block * levels
    rows = field.shape[0] // levels
    steps = rows // block
    shape = (levels, lanes)
    batch = 32 if block % 32 == 0 else 8

    @pl.when(comp != 0)
    def _():
        lane = iota(shape, 1)
        pair_of = lane >> 1

        def sea_of(y):
            return lane < counts[0, jnp.clip(y, 0, rows - 1)]

        def at(y):
            return pl.ds(pl.multiple_of(y * levels, levels), levels)

        def halo(neighbour):
            found = jnp.zeros(shape, jnp.float32)
            inside = (neighbour >= 0) & (neighbour < n_row)
            for part, ref in zip(near_parts, halos):
                found = jnp.where(inside & ((neighbour ^ row) == part), ref[0].astype(jnp.float32), found)
            return found

        for slot in range(sides.shape[0]):
            west = jnp.where(col > 0, west_in[slot].astype(jnp.float32), 0.0)
            east = jnp.where(col < n_col - 1, east_in[slot].astype(jnp.float32), 0.0)
            sides[slot] = jnp.where((lane & 1) == 0, pltpu.roll(east, lanes - 1, 1), pltpu.roll(west, 1, 1))
        if not final:
            packed[...] = jnp.zeros_like(packed)

        def advance(field, above, below, out):
            step = pl.program_id(0)
            base = step * block
            masked[0:levels, :] = jnp.where(step > 0, jnp.where(sea_of(base - 1), above[...], 0.0), halo(row - 1))
            masked[(block + 1) * levels:(block + 2) * levels, :] = jnp.where(
                step < steps - 1, jnp.where(sea_of(base + block), below[...], 0.0), halo(row + 1))

            def fill(g, carry):
                for s in range(8):
                    y = g * 8 + s
                    masked[at(y + 1), :] = jnp.where(sea_of(base + y), field[at(y), :], 0.0)
                return carry

            lax.fori_loop(0, block // 8, fill, 0)
            weights = jnp.concatenate([beside_matrix(), side_matrix()], axis=0)
            spread = spread_matrix()

            def body(g, carry):
                first = base + g * batch
                here = masked[pl.ds(pl.multiple_of((g * batch + 1) * levels, levels), batch * levels), :]
                beyond = sides[first >> 6]
                turned = jnp.concatenate(
                    [jnp.where(pair_of == (first & 63) + s, beyond, 0.0).astype(jnp.bfloat16) for s in range(batch)],
                    axis=0)
                near = product(jnp.concatenate([here.astype(jnp.bfloat16), turned], axis=1), weights)
                new_rows = []
                for s in range(batch):
                    y = g * batch + s
                    part = slice(s * levels, (s + 1) * levels)
                    lap = masked[at(y), :] + masked[at(y + 2), :] + near[part] - 4.0 * masked[at(y + 1), :]
                    sea = sea_of(base + y)
                    new = field[at(y), :] + jnp.where(sea, diffusion_rate * lap, 0.0)
                    out[at(y), :] = new
                    if final:
                        out[pl.ds(y * levels, 1), :] = new[0:1, :] + 0.3 * gap[pl.ds(base + y, 1), :]
                    else:
                        new_rows.append(jnp.where(sea, new, 0.0).astype(jnp.bfloat16))
                if not final:
                    pack(packed, first, new_rows, spread)
                return carry

            lax.fori_loop(0, block // batch, body, 0)
            if not final:
                @pl.when(step == 0)
                def _():
                    ends[0] = jnp.where(sea_of(0), out[0:levels, :], 0.0).astype(jnp.bfloat16)

                @pl.when(step == steps - 1)
                def _():
                    ends[1] = jnp.where(
                        sea_of(rows - 1), out[(block - 1) * levels:block * levels, :], 0.0
                    ).astype(jnp.bfloat16)

        state_block = pl.BlockSpec((tall, lanes), lambda i: (i, 0))
        pltpu.emit_pipeline(
            advance, grid=(steps,),
            in_specs=[
                state_block,
                pl.BlockSpec((levels, lanes), lambda i: (jnp.maximum(i * block - 1, 0), 0)),
                pl.BlockSpec((levels, lanes), lambda i: (jnp.minimum((i + 1) * block, rows - 1), 0)),
            ],
            out_specs=[state_block],
        )(field, field, field, out)
        if not final:
            edge[...] = packed[...].astype(jnp.bfloat16)


def legendre_kernel(place, legendre, *rest, n_row, n_col, wave_dev, first_wave, with_ends):
    coeffs, rest = rest[:n_row], rest[n_row:]
    if with_ends:
        ends, rest = rest[0], rest[2:]
    out, gathered = rest[:n_row], rest[n_row]
    comp, row, _ = where_am_i(place, n_row, n_col)
    waves, lats = coeffs[0].shape[:2]
    count = legendre.shape[2]

    def one_wave(legendre, *parts):
        coeffs, out = parts[:n_row], parts[n_row:]
        table = legendre[0]
        for part in range(n_row):
            gathered[part ^ row] = coeffs[part][0]
        fourier = gathered[...].reshape(n_row * lats, lanes)
        spectral = lax.dot_general(fourier, table, (((0,), (0,)), ((), ())), preferred_element_type=jnp.float32)
        wave = row * wave_dev + first_wave + pl.program_id(0)
        total = (wave + iota((1, count), 1)).astype(jnp.float32)
        ratio = total * (total + 1.0) / (1279.0 * 1280.0)
        damping = 1.0 / (1.0 + 20.0 * ratio * ratio)
        filtered = (spectral * damping).astype(jnp.bfloat16)
        result = lax.dot_general(table, filtered, (((1,), (1,)), ((), ())), preferred_element_type=jnp.float32)
        gathered[...] = result.astype(jnp.bfloat16).reshape(n_row, lats, lanes)
        for part in range(n_row):
            out[part][0] = gathered[part ^ row]

    @pl.when(comp == 0)
    def _():
        pieces = [pl.BlockSpec((1, lats, lanes), lambda i: (i, 0, 0))] * n_row
        pltpu.emit_pipeline(
            one_wave, grid=(waves,),
            in_specs=[pl.BlockSpec((1,) + legendre.shape[1:], lambda i: (first_wave + i, 0, 0))] + pieces,
            out_specs=pieces,
        )(legendre, *coeffs, *out)

    if with_ends:
        @pl.when(comp != 0)
        def _():
            hand_on(ends, out, row)


def surface_kernel(place, counts, partner, own, source, *rest, first, group, n_row, n_col):
    new, gap = rest[-2:]
    half = partner.shape[0] // 2
    width = 2 * lanes
    table = jnp.concatenate(
        [partner[pl.ds(0, half, stride=2), :], partner[pl.ds(1, half, stride=2), :]], axis=1
    ).astype(jnp.bfloat16)
    low_index = iota((width, lanes), 0)
    high_index = iota((half, lanes), 0)
    one = jnp.ones((width, lanes), jnp.bfloat16)
    zero = jnp.zeros((width, lanes), jnp.bfloat16)
    sublane = iota((8, lanes), 0)
    rate = jnp.where(where_am_i(place, n_row, n_col)[0] == 0, 0.5, 0.25).astype(jnp.float32)

    def body(g, carry):
        start = pl.multiple_of(g * 8, 8)
        entries = source[pl.ds(start, 8), :]
        low = entries & (width - 1)
        high = entries >> 8
        found = []
        for p in range(0, 8, group):
            pick = jnp.concatenate(
                [jnp.where(low_index == low[s:s + 1, :], one, zero) for s in range(p, p + group)], axis=1
            )
            picked = product(table, pick)
            for s in range(group):
                part = picked[:, lanes * s:lanes * (s + 1)]
                match = high_index == high[p + s:p + s + 1, :]
                found.append(jnp.sum(jnp.where(match, part, 0.0), axis=0, keepdims=True))
        pulled = jnp.concatenate(found, axis=0)
        limit = jnp.zeros((8, lanes), jnp.int32)
        for s in range(8):
            limit = jnp.where(sublane == s, counts[0, first + start + s], limit)
        here = own[pl.ds(start, 8), :]
        difference = jnp.where(iota((8, lanes), 1) < limit, pulled - here, 0.0)
        new[pl.ds(start, 8), :] = here + rate * difference
        gap[pl.ds(start, 8), :] = difference
        return carry

    lax.fori_loop(0, source.shape[0] // 8, body, 0)


def exit_kernel(place, sea, *rest, n_row, n_col, widths, block):
    chunks = len(widths)
    back, (out, table) = rest[:n_row * chunks], rest[n_row * chunks:]
    comp, row, _ = where_am_i(place, n_row, n_col)
    levels = sum(widths) * n_row
    wave_dev = levels // n_row
    flip = row * wave_dev
    tall = block * levels

    def turn(*refs):
        parts, out = refs[:-1], refs[-1]

        def source(wave, lat, count):
            part, local = divmod(wave, wave_dev)
            chunk, slot = chunk_of(local, widths)
            return parts[n_row * chunk + part][slot, lat:lat + count, :]

        for lat in range(0, block - 15, 16):
            halves = [
                jnp.concatenate([source(half + wave, lat, 16) for wave in range(16)], axis=0)
                for half in range(0, levels, 16)
            ]
            turned = product(table[...], jnp.concatenate(halves, axis=1))
            for s in range(16):
                for half in range(0, levels, 16):
                    start = pl.multiple_of((lat + s) * levels + (half ^ (flip & ~15)), 16)
                    part = lanes * (half // 16)
                    out[pl.ds(start, 16), :] = turned[16 * s:16 * s + 16, part:part + lanes]
        for lat in range(block - block % 16, block, 8):
            for wave in range(levels):
                out[pl.ds(lat * levels + (wave ^ flip), 8, stride=levels), :] = source(wave, lat, 8).astype(jnp.float32)

    @pl.when(comp == 0)
    def _():
        table[...] = swap_matrix(0, flip & 15)
        pltpu.emit_pipeline(
            turn, grid=(out.shape[0] // tall,),
            in_specs=[pl.BlockSpec((w, block, lanes), lambda i: (0, i, 0)) for w in widths for _ in range(n_row)],
            out_specs=[pl.BlockSpec((tall, lanes), lambda i: (i, 0))],
        )(*back, out)


def shards(model_state, legendre, gauss_weight, mixing, surface, sea_count, remap_source):
    n_row, n_col = lax.axis_size("row"), lax.axis_size("col")
    rows, levels = model_state.shape[1], model_state.shape[2]
    wave_dev = levels // n_row
    widths = chunk_widths(wave_dev)
    chunks = len(widths)
    block = row_block(rows)
    f32, bf16 = jnp.float32, jnp.bfloat16
    sds = jax.ShapeDtypeStruct
    mib = 1 << 20

    fields = model_state.reshape(rows * levels, lanes)
    counts = sea_count.reshape(1, rows)
    place = lax.axis_index(("comp", "row", "col")).astype(jnp.int32).reshape(1)
    own = surface[0]
    comp_size = lax.axis_size("comp")
    partner = lax.ppermute(own, "comp", [(i, comp_size - 1 - i) for i in range(comp_size)])

    slots = pl.cdiv(rows, 64)

    def call(kernel, grid, in_specs, out_specs, out_shape, args, scratch=(), vmem=59, flops=10**7, size=0, aliases={}):
        return pl.pallas_call(
            functools.partial(kernel, n_row=n_row, n_col=n_col),
            out_shape=out_shape,
            grid_spec=pltpu.PrefetchScalarGridSpec(
                num_scalar_prefetch=1, grid=grid, in_specs=in_specs, out_specs=out_specs, scratch_shapes=scratch),
            compiler_params=pltpu.CompilerParams(vmem_limit_bytes=vmem * mib),
            input_output_aliases=aliases,
            cost_estimate=cost(flops, size),
        )(place, *args)

    smem = pl.BlockSpec(memory_space=pltpu.SMEM)
    anywhere = pl.BlockSpec(memory_space=pl.ANY)
    state_bytes = 4 * rows * levels * lanes
    vmem = pl.BlockSpec(memory_space=pltpu.VMEM)
    edge_shape = (slots, levels, lanes)
    ends_shape = (2, levels, lanes)
    *send, mixed, edge = call(
        functools.partial(entry_kernel, widths=widths, block=block), (),
        [smem, anywhere, smem, vmem],
        [anywhere] * (n_row * chunks + 1) + [vmem],
        [sds((w, rows, lanes), bf16) for w in widths for _ in range(n_row)]
        + [sds((rows * levels, lanes), f32), sds(edge_shape, bf16)],
        (counts, fields, gauss_weight, mixing),
        scratch=[pltpu.VMEM((256, 256), bf16), pltpu.VMEM(edge_shape, f32), pltpu.VMEM(ends_shape, bf16)],
        vmem=63, size=2 * state_bytes,
    )

    near_parts = [k for k in range(1, n_row) if k & (k + 1) == 0]

    def traded(parts, name):
        got = [parts[0]]
        for k in range(1, n_row):
            real = k in near_parts and name[-1] == "0"
            route = [(r, r ^ k) for r in range(n_row)]
            for r in range(n_row, n_row * comp_size):
                route.append((r, r ^ k if real else r ^ 1))
            got.append(lax.ppermute(parts[k], ("comp", "row"), route))
        return got

    chain = [n_col + i for i in range(n_col - 1)]

    def to_columns(x):
        return [
            lax.ppermute(x, ("comp", "col"), [(i + 1, i) for i in chain]),
            lax.ppermute(x, ("comp", "col"), [(i, i + 1) for i in chain]),
        ]

    coeffs = [traded(send[n_row * c:n_row * (c + 1)], f"there{c}") for c in range(chunks)]
    sides = to_columns(edge)

    halves = 2 if rows % 16 == 0 else 1
    share = rows // halves
    whole = pl.BlockSpec((rows, lanes), lambda i, s: (0, 0))
    surfaces = []

    def remap(half, after):
        piece = pl.BlockSpec((share, lanes), lambda i, s: (half, 0))
        earlier = surfaces[-1] if surfaces else ()
        surfaces.append(call(
            functools.partial(surface_kernel, first=half * share, group=2), (1,),
            [smem, whole, piece, piece] + [anywhere] * (len(earlier) + len(after)),
            [piece] * 2, [sds((rows, lanes), f32)] * 2,
            (counts, partner, own, remap_source[0], *earlier, *after),
            aliases={5 + i: i for i in range(len(earlier))},
            flops=10**10, size=3 * 4 * rows * lanes,
        ))

    remap(0, (edge,))

    def sweep(field, rows_in, cols_in, final, extra=()):
        out_shape = [sds((rows * levels, lanes), f32)]
        out_specs = [anywhere]
        scratch = [pltpu.VMEM(((block + 2) * levels, lanes), f32), pltpu.VMEM(edge_shape, f32)]
        if not final:
            out_shape += [sds(edge_shape, bf16), sds(ends_shape, bf16)]
            out_specs += [vmem, vmem]
            scratch += [pltpu.VMEM(edge_shape, f32)]
        return call(
            functools.partial(sweep_kernel, block=block, near_parts=near_parts, final=final),
            (1,),
            [smem, anywhere, pl.BlockSpec(edge_shape, lambda i, s: (0, 0, 0)),
             pl.BlockSpec(edge_shape, lambda i, s: (0, 0, 0))]
            + [pl.BlockSpec((1, levels, lanes), lambda i, s: (0, 0, 0))] * len(near_parts)
            + ([pl.BlockSpec((rows, lanes), lambda i, s: (0, 0))] if final else []),
            out_specs, out_shape,
            (counts, field, *cols_in, *(rows_in[k] for k in near_parts), *extra),
            scratch=scratch, size=2 * state_bytes,
        )

    first_step, edge, ends = sweep(mixed, coeffs[0], sides, False)
    sides = to_columns(edge)

    returned = []
    for chunk, width in enumerate(widths):
        with_ends = chunk == 0
        first_wave = sum(widths[:chunk])
        part = call(
            functools.partial(legendre_kernel, wave_dev=wave_dev, first_wave=first_wave, with_ends=with_ends),
            (),
            [anywhere] * (1 + n_row) + ([vmem, anywhere] if with_ends else []),
            [anywhere] * n_row,
            [sds((width, rows, lanes), bf16)] * n_row,
            (legendre, *coeffs[chunk], *([ends, surfaces[0][1]] if with_ends else [])),
            scratch=[pltpu.VMEM((n_row, rows, lanes), bf16)], vmem=63,
            flops=4 * width * legendre.shape[1] * legendre.shape[2] * lanes,
            size=2 * width * legendre.shape[1] * legendre.shape[2],
        )
        returned.append(traded(part, f"back{chunk}"))

    if halves > 1:
        remap(1, (first_step,))
    new_surface, gap = surfaces[-1]
    (sea,) = sweep(first_step, returned[0], sides, True, (gap,))

    state = call(
        functools.partial(exit_kernel, widths=widths, block=block), (),
        [anywhere] * (1 + n_row * chunks), anywhere, sds((rows * levels, lanes), f32),
        (sea, *sum(returned, [])), scratch=[pltpu.VMEM((256, 256), bf16)], size=2 * state_bytes, aliases={1: 0},
    )
    return state.reshape(model_state.shape), new_surface[None]


def solution(mesh):
    in_specs = (
        P("comp", "row", None, "col"),
        P("row", None, None),
        P("row"),
        P(),
        P("comp", "row", "col"),
        P("comp", "row", "col"),
        P("comp", "row", "col"),
    )
    out_specs = (P("comp", "row", None, "col"), P("comp", "row", "col"))

    return jax.shard_map(shards, mesh=mesh, in_specs=in_specs, out_specs=out_specs, check_vma=False)
```

```python
import functools

import jax
import jax.numpy as jnp
from jax import lax
from jax.experimental import pallas as pl
from jax.experimental.pallas import tpu as pltpu
from jax.sharding import PartitionSpec as P


diffusion_rate = 0.2
lanes = 128


def chunk_widths(wave_dev):
    return (wave_dev - wave_dev // 2, wave_dev // 2) if wave_dev > 1 else (wave_dev,)


def chunk_of(local, widths):
    chunk = 0
    while local >= widths[chunk]:
        local -= widths[chunk]
        chunk += 1
    return chunk, local


def row_block(rows):
    return 160 if rows % 160 == 0 else rows


def cost(flops, bytes_accessed):
    return pl.CostEstimate(flops=flops, bytes_accessed=bytes_accessed, transcendentals=0)


def where_am_i(place, n_row, n_col):
    flat = place[0]
    return (
        lax.div(flat, n_row * n_col),
        lax.rem(lax.div(flat, n_col), n_row),
        lax.rem(flat, n_col),
    )


def iota(shape, dim):
    return lax.broadcasted_iota(jnp.int32, shape, dim)


def as_bf16(mask):
    return jnp.where(mask, 1.0, 0.0).astype(jnp.bfloat16)


def swap_matrix(flip_high, flip_low):
    row, column = iota((256, 256), 0), iota((256, 256), 1)
    return as_bf16(column == (((row & 15) ^ flip_low) << 4 | ((row >> 4) ^ flip_high)))


def spread_matrix():
    row, column = iota((lanes, lanes), 0), iota((lanes, lanes), 1)
    odd = column & 1
    return as_bf16(((row == lanes - 1) & (odd == 0)) | ((row == 0) & (odd == 1)))


def beside_matrix():
    row, column = iota((lanes, lanes), 0), iota((lanes, lanes), 1)
    return as_bf16((row == column + 1) | (row + 1 == column))


def side_matrix():
    row, column = iota((lanes, lanes), 0), iota((lanes, lanes), 1)
    odd = row & 1
    return as_bf16(((column == 0) & (odd == 1)) | ((column == lanes - 1) & (odd == 0)))


def split(value):
    high = value.astype(jnp.bfloat16)
    return high, (value - high.astype(jnp.float32)).astype(jnp.bfloat16)


def product(a, b):
    return jnp.dot(a, b, preferred_element_type=jnp.float32)


def parts_of_half(half, n_row, wave_dev):
    return [k for k in range(n_row) if k * wave_dev // 16 == half]


def entry_kernel(place, counts, field, waves, gauss, mix, *rest, n_row, n_col, widths, block, half):
    levels = mix.shape[0]
    wave_dev = levels // n_row
    mine = parts_of_half(half, n_row, wave_dev)
    chunks = len(widths)
    total = len(mine) * chunks
    if half:
        send, (mixed, edge, ends, table, packed, sems) = rest[:total], rest[total:]
    else:
        ends, send, (table, sems) = rest[0], rest[1:1 + total], rest[1 + total:]
    comp, row, _ = where_am_i(place, n_row, n_col)
    tall = block * levels
    steps = field.shape[0] // tall
    state_block = pl.BlockSpec((tall, lanes), lambda i: (i, 0))
    flip = row * wave_dev
    first_parts = {k: send[n] for n, k in enumerate(mine)}

    def weigh(waves, *parts):
        step = pl.program_id(0)

        def target(wave):
            part, local = divmod(16 * half + wave, wave_dev)
            chunk, slot = chunk_of(local, widths)
            return parts[len(mine) * chunk + mine.index(part)], slot

        for lat in range(0, block, 16):
            size = min(16, block - lat)
            rows = jnp.concatenate([
                (waves[lat + s] * gauss[step * block + lat + s]).astype(jnp.bfloat16) for s in range(size)
            ], axis=0)
            if size == 16:
                swap = table[...]
            else:
                shape = (16 * size, 16 * size)
                line, column = iota(shape, 0), iota(shape, 1)
                swap = as_bf16(column == ((line & (size - 1)) << 4 | ((line // size) ^ (flip & 15))))
            turned = product(swap, rows).astype(jnp.bfloat16)
            for wave in range(16):
                out, slot = target(wave)
                out[slot, lat:lat + size, :] = turned[size * wave:size * (wave + 1), :]

    @pl.when(comp == 0)
    def _():
        table[...] = swap_matrix(flip & 15, 0)
        pltpu.emit_pipeline(
            weigh, grid=(steps,),
            in_specs=[pl.BlockSpec((block, pl.Squeezed(), 16, lanes), lambda i: (i, half ^ (flip >> 4), 0, 0))],
            out_specs=[pl.BlockSpec((w, block, lanes), lambda i: (0, i, 0)) for w in widths for _ in mine],
        )(waves, *send)

    if not half:
        @pl.when(comp != 0)
        def _():
            hand_on(ends, first_parts, row, sems)

        return

    def mixed_rows(ref, start, first_row):
        values = []
        for quarter in range(2):
            parts = []
            for pair in range(2):
                part = ref[pl.ds(start + (2 * quarter + pair) * 2 * levels, 2 * levels), :]
                values.append(part)
                parts.append(split(part))
            high = jnp.concatenate([p[0] for p in parts], axis=1)
            low = jnp.concatenate([p[1] for p in parts], axis=1)
            blend = product(table[0:2 * levels, :], jnp.concatenate([high, low, high, low], axis=0))
            values += [blend[:, :lanes], blend[:, lanes:]]
        out = []
        for s in range(8):
            quarter, pair, place_in = s // 4, s // 2 % 2, slice(levels * (s % 2), levels * (s % 2) + levels)
            heat = values[4 * quarter + pair][place_in]
            blend = values[4 * quarter + 2 + pair][place_in]
            sea = iota((levels, lanes), 1) < counts[0, first_row + s]
            value = heat + jnp.where(sea, blend, 0.0)
            out.append((value, jnp.where(sea, value, 0.0).astype(jnp.bfloat16)))
        return out

    @pl.when(comp != 0)
    def _():
        high, low = split(mix[...])
        repeat = as_bf16((iota((levels, 256), 1) & (levels - 1)) == iota((levels, 256), 0))
        wide = jnp.where(iota((levels, 256), 1) < 4 * levels, product(high, repeat), product(low, repeat))
        wide = jnp.concatenate([wide, wide], axis=0)
        shape = (2 * levels, 256)
        own = (iota(shape, 1) // levels & 1) == iota(shape, 0) // levels
        table[0:2 * levels, :] = jnp.where(own, wide, 0.0).astype(jnp.bfloat16)
        packed[...] = jnp.zeros_like(packed)
        batch = 32 if block % 32 == 0 else 8

        def blend(field, mixed):
            step = pl.program_id(0)
            spread = spread_matrix()

            def body(g, carry):
                base = step * block + g * batch
                rows = []
                for first in range(0, batch, 8):
                    start = pl.multiple_of((g * batch + first) * levels, 8 * levels)
                    some = mixed_rows(field, start, base + first)
                    for s, (value, _) in enumerate(some):
                        mixed[pl.ds(pl.multiple_of(start + s * levels, levels), levels), :] = value
                    rows += some
                pack(packed, base, [r[1] for r in rows], spread)
                return carry

            lax.fori_loop(0, block // batch, body, 0)

            @pl.when(step == 0)
            def _():
                ends[0] = mixed_rows(field, 0, 0)[0][1]

            @pl.when(step == steps - 1)
            def _():
                ends[1] = mixed_rows(field, tall - 8 * levels, steps * block - 8)[-1][1]

        pltpu.emit_pipeline(blend, grid=(steps,), in_specs=[state_block], out_specs=[state_block])(field, mixed)
        edge[...] = packed[...].astype(jnp.bfloat16)
        hand_on(ends, first_parts, row, sems)


def hand_on(ends, parts, row, sems):
    levels = ends.shape[1]
    copies = [
        pltpu.make_async_copy(
            ends.at[((k ^ row) > row).astype(jnp.int32)], part.at[0, pl.ds(0, levels)], sems.at[k])
        for k, part in parts.items() if k
    ]
    for copy in copies:
        copy.start()
    for copy in copies:
        copy.wait()


def pack(packed, base, rows, spread):
    levels = packed.shape[1]
    ends = product(jnp.concatenate(rows, axis=0), spread)
    pair_of = iota((levels, lanes), 1) >> 1
    slot = base >> 6
    kept = packed[slot]
    for s in range(len(rows)):
        kept = jnp.where(pair_of == (base & 63) + s, ends[s * levels:(s + 1) * levels], kept)
    packed[slot] = kept


def sweep_kernel(place, counts, field, near_in, far_in, *rest, block, n_row, n_col, near_parts, final):
    halos, rest = rest[:len(near_parts)], rest[len(near_parts):]
    if final:
        gap, out, masked, sides = rest
    else:
        out, edge, ends, masked, sides, packed = rest
    comp, row, col = where_am_i(place, n_row, n_col)
    levels = sides.shape[1]
    tall = block * levels
    rows = field.shape[0] // levels
    steps = rows // block
    shape = (levels, lanes)
    batch = 32 if block % 32 == 0 else 8

    @pl.when(comp != 0)
    def _():
        lane = iota(shape, 1)
        pair_of = lane >> 1

        def sea_of(y):
            return lane < counts[0, jnp.clip(y, 0, rows - 1)]

        def at(y):
            return pl.ds(pl.multiple_of(y * levels, levels), levels)

        def halo(neighbour):
            found = jnp.zeros(shape, jnp.float32)
            inside = (neighbour >= 0) & (neighbour < n_row)
            for part, ref in zip(near_parts, halos):
                found = jnp.where(inside & ((neighbour ^ row) == part), ref[0].astype(jnp.float32), found)
            return found

        for slot in range(sides.shape[0]):
            near, far = near_in[slot].astype(jnp.float32), far_in[slot].astype(jnp.float32)
            east_is_near = (col & 1) == 0
            west = jnp.where(col > 0, jnp.where(east_is_near, far, near), 0.0)
            east = jnp.where(col < n_col - 1, jnp.where(east_is_near, near, far), 0.0)
            sides[slot] = jnp.where((lane & 1) == 0, pltpu.roll(east, lanes - 1, 1), pltpu.roll(west, 1, 1))
        if not final:
            packed[...] = jnp.zeros_like(packed)

        def advance(field, above, below, out):
            step = pl.program_id(0)
            base = step * block
            masked[0:levels, :] = jnp.where(step > 0, jnp.where(sea_of(base - 1), above[...], 0.0), halo(row - 1))
            masked[(block + 1) * levels:(block + 2) * levels, :] = jnp.where(
                step < steps - 1, jnp.where(sea_of(base + block), below[...], 0.0), halo(row + 1))

            def fill(g, carry):
                for s in range(8):
                    y = g * 8 + s
                    masked[at(y + 1), :] = jnp.where(sea_of(base + y), field[at(y), :], 0.0)
                return carry

            lax.fori_loop(0, block // 8, fill, 0)
            weights = jnp.concatenate([beside_matrix(), side_matrix()], axis=0)
            spread = spread_matrix()

            def body(g, carry):
                first = base + g * batch
                here = masked[pl.ds(pl.multiple_of((g * batch + 1) * levels, levels), batch * levels), :]
                beyond = sides[first >> 6]
                turned = jnp.concatenate(
                    [jnp.where(pair_of == (first & 63) + s, beyond, 0.0).astype(jnp.bfloat16) for s in range(batch)],
                    axis=0)
                near = product(jnp.concatenate([here.astype(jnp.bfloat16), turned], axis=1), weights)
                new_rows = []
                for s in range(batch):
                    y = g * batch + s
                    part = slice(s * levels, (s + 1) * levels)
                    lap = masked[at(y), :] + masked[at(y + 2), :] + near[part] - 4.0 * masked[at(y + 1), :]
                    sea = sea_of(base + y)
                    new = field[at(y), :] + jnp.where(sea, diffusion_rate * lap, 0.0)
                    out[at(y), :] = new
                    if final:
                        out[pl.ds(y * levels, 1), :] = new[0:1, :] + 0.3 * gap[pl.ds(base + y, 1), :]
                    else:
                        new_rows.append(jnp.where(sea, new, 0.0).astype(jnp.bfloat16))
                if not final:
                    pack(packed, first, new_rows, spread)
                return carry

            lax.fori_loop(0, block // batch, body, 0)
            if not final:
                @pl.when(step == 0)
                def _():
                    ends[0] = jnp.where(sea_of(0), out[0:levels, :], 0.0).astype(jnp.bfloat16)

                @pl.when(step == steps - 1)
                def _():
                    ends[1] = jnp.where(
                        sea_of(rows - 1), out[(block - 1) * levels:block * levels, :], 0.0
                    ).astype(jnp.bfloat16)

        state_block = pl.BlockSpec((tall, lanes), lambda i: (i, 0))
        pltpu.emit_pipeline(
            advance, grid=(steps,),
            in_specs=[
                state_block,
                pl.BlockSpec((levels, lanes), lambda i: (jnp.maximum(i * block - 1, 0), 0)),
                pl.BlockSpec((levels, lanes), lambda i: (jnp.minimum((i + 1) * block, rows - 1), 0)),
            ],
            out_specs=[state_block],
        )(field, field, field, out)
        if not final:
            edge[...] = packed[...].astype(jnp.bfloat16)


def legendre_kernel(place, legendre, *rest, n_row, n_col, wave_dev, first_wave, with_ends):
    coeffs, rest = rest[:n_row], rest[n_row:]
    if with_ends:
        ends, rest = rest[0], rest[2:]
    out, (gathered, sems) = rest[:n_row], rest[n_row:]
    comp, row, _ = where_am_i(place, n_row, n_col)
    waves, lats = coeffs[0].shape[:2]
    count = legendre.shape[2]

    def one_wave(legendre, *parts):
        coeffs, out = parts[:n_row], parts[n_row:]
        table = legendre[0]
        for part in range(n_row):
            gathered[part ^ row] = coeffs[part][0]
        fourier = gathered[...].reshape(n_row * lats, lanes)
        spectral = lax.dot_general(fourier, table, (((0,), (0,)), ((), ())), preferred_element_type=jnp.float32)
        wave = row * wave_dev + first_wave + pl.program_id(0)
        total = (wave + iota((1, count), 1)).astype(jnp.float32)
        ratio = total * (total + 1.0) / (1279.0 * 1280.0)
        damping = 1.0 / (1.0 + 20.0 * ratio * ratio)
        filtered = (spectral * damping).astype(jnp.bfloat16)
        result = lax.dot_general(table, filtered, (((1,), (1,)), ((), ())), preferred_element_type=jnp.float32)
        gathered[...] = result.astype(jnp.bfloat16).reshape(n_row, lats, lanes)
        for part in range(n_row):
            out[part][0] = gathered[part ^ row]

    @pl.when(comp == 0)
    def _():
        pieces = [pl.BlockSpec((1, lats, lanes), lambda i: (i, 0, 0))] * n_row
        pltpu.emit_pipeline(
            one_wave, grid=(waves,),
            in_specs=[pl.BlockSpec((1,) + legendre.shape[1:], lambda i: (first_wave + i, 0, 0))] + pieces,
            out_specs=pieces,
        )(legendre, *coeffs, *out)

    if with_ends:
        @pl.when(comp != 0)
        def _():
            hand_on(ends, dict(enumerate(out)), row, sems)


def surface_kernel(place, counts, partner, own, source, *rest, first_piece, group, n_row, n_col):
    new, gap = rest[-2:]
    first = (first_piece + pl.program_id(0)) * source.shape[0]
    half = partner.shape[0] // 2
    width = 2 * lanes
    table = jnp.concatenate(
        [partner[pl.ds(0, half, stride=2), :], partner[pl.ds(1, half, stride=2), :]], axis=1
    ).astype(jnp.bfloat16)
    low_index = iota((width, lanes), 0)
    high_index = iota((half, lanes), 0)
    one = jnp.ones((width, lanes), jnp.bfloat16)
    zero = jnp.zeros((width, lanes), jnp.bfloat16)
    sublane = iota((8, lanes), 0)
    rate = jnp.where(where_am_i(place, n_row, n_col)[0] == 0, 0.5, 0.25).astype(jnp.float32)

    def body(g, carry):
        start = pl.multiple_of(g * 8, 8)
        entries = source[pl.ds(start, 8), :]
        low = entries & (width - 1)
        high = entries >> 8
        found = []
        for p in range(0, 8, group):
            pick = jnp.concatenate(
                [jnp.where(low_index == low[s:s + 1, :], one, zero) for s in range(p, p + group)], axis=1
            )
            picked = product(table, pick)
            for s in range(group):
                part = picked[:, lanes * s:lanes * (s + 1)]
                match = high_index == high[p + s:p + s + 1, :]
                found.append(jnp.sum(jnp.where(match, part, 0.0), axis=0, keepdims=True))
        pulled = jnp.concatenate(found, axis=0)
        limit = jnp.zeros((8, lanes), jnp.int32)
        for s in range(8):
            limit = jnp.where(sublane == s, counts[0, first + start + s], limit)
        here = own[pl.ds(start, 8), :]
        difference = jnp.where(iota((8, lanes), 1) < limit, pulled - here, 0.0)
        new[pl.ds(start, 8), :] = here + rate * difference
        gap[pl.ds(start, 8), :] = difference
        return carry

    lax.fori_loop(0, source.shape[0] // 8, body, 0)


def exit_kernel(place, sea, *rest, n_row, n_col, widths, block):
    chunks = len(widths)
    back, (out, table) = rest[:n_row * chunks], rest[n_row * chunks:]
    comp, row, _ = where_am_i(place, n_row, n_col)
    levels = sum(widths) * n_row
    wave_dev = levels // n_row
    flip = row * wave_dev
    tall = block * levels

    def turn(*refs):
        parts, out = refs[:-1], refs[-1]

        def source(wave, lat, count):
            part, local = divmod(wave, wave_dev)
            chunk, slot = chunk_of(local, widths)
            return parts[n_row * chunk + part][slot, lat:lat + count, :]

        for lat in range(0, block - 15, 16):
            halves = [
                jnp.concatenate([source(half + wave, lat, 16) for wave in range(16)], axis=0)
                for half in range(0, levels, 16)
            ]
            turned = product(table[...], jnp.concatenate(halves, axis=1))
            for s in range(16):
                for half in range(0, levels, 16):
                    start = pl.multiple_of((lat + s) * levels + (half ^ (flip & ~15)), 16)
                    part = lanes * (half // 16)
                    out[pl.ds(start, 16), :] = turned[16 * s:16 * s + 16, part:part + lanes]
        for lat in range(block - block % 16, block, 8):
            for wave in range(levels):
                out[pl.ds(lat * levels + (wave ^ flip), 8, stride=levels), :] = source(wave, lat, 8).astype(jnp.float32)

    @pl.when(comp == 0)
    def _():
        table[...] = swap_matrix(0, flip & 15)
        pltpu.emit_pipeline(
            turn, grid=(out.shape[0] // tall,),
            in_specs=[pl.BlockSpec((w, block, lanes), lambda i: (0, i, 0)) for w in widths for _ in range(n_row)],
            out_specs=[pl.BlockSpec((tall, lanes), lambda i: (i, 0))],
        )(*back, out)


def shards(model_state, legendre, gauss_weight, mixing, surface, sea_count, remap_source):
    n_row, n_col = lax.axis_size("row"), lax.axis_size("col")
    rows, levels = model_state.shape[1], model_state.shape[2]
    wave_dev = levels // n_row
    widths = chunk_widths(wave_dev)
    chunks = len(widths)
    block = row_block(rows)
    f32, bf16 = jnp.float32, jnp.bfloat16
    sds = jax.ShapeDtypeStruct

    fields = model_state.reshape(rows * levels, lanes)
    counts = sea_count.reshape(1, rows)
    place = lax.axis_index(("comp", "row", "col")).astype(jnp.int32).reshape(1)
    own = surface[0]
    comp_size = lax.axis_size("comp")
    partner = lax.ppermute(own, "comp", [(i, comp_size - 1 - i) for i in range(comp_size)])

    slots = pl.cdiv(rows, 64)

    def call(kernel, grid, in_specs, out_specs, out_shape, args, scratch=(), vmem_limit=66700000, flops=10**7, size=0, aliases={}):
        return pl.pallas_call(
            functools.partial(kernel, n_row=n_row, n_col=n_col),
            out_shape=out_shape,
            grid_spec=pltpu.PrefetchScalarGridSpec(
                num_scalar_prefetch=1, grid=grid, in_specs=in_specs, out_specs=out_specs, scratch_shapes=scratch),
            compiler_params=pltpu.CompilerParams(vmem_limit_bytes=vmem_limit),
            input_output_aliases=aliases,
            cost_estimate=cost(flops, size),
        )(place, *args)

    smem = pl.BlockSpec(memory_space=pltpu.SMEM)
    anywhere = pl.BlockSpec(memory_space=pl.ANY)
    state_bytes = 4 * rows * levels * lanes
    vmem = pl.BlockSpec(memory_space=pltpu.VMEM)
    edge_shape = (slots, levels, lanes)
    ends_shape = (2, levels, lanes)
    send = {}
    wave_blocks = model_state.reshape(rows, levels // 16, 16, lanes)

    def enter(half, extra_in, extra_specs, extra_out, scratch):
        mine = parts_of_half(half, n_row, wave_dev)
        keys = [(c, k) for c in range(chunks) for k in mine]
        got = call(
            functools.partial(entry_kernel, widths=widths, block=block, half=half), (),
            [smem, anywhere, anywhere, smem, vmem] + [vmem] * len(extra_in),
            [anywhere] * len(keys) + extra_specs,
            [sds((widths[c], rows, lanes), bf16) for c, _ in keys] + extra_out,
            (counts, fields, wave_blocks, gauss_weight, mixing, *extra_in),
            scratch=[pltpu.VMEM((256, 256), bf16)] + scratch + [pltpu.SemaphoreType.DMA((n_row,))],
            size=state_bytes,
        )
        send.update(zip(keys, got))
        return got[len(keys):]

    mixed, edge, tile_ends = enter(
        1, [], [anywhere, vmem, vmem],
        [sds((rows * levels, lanes), f32), sds(edge_shape, bf16), sds(ends_shape, bf16)],
        [pltpu.VMEM(edge_shape, f32)])
    enter(0, [tile_ends], [], [], [])

    near_parts = [k for k in range(1, n_row) if k & (k + 1) == 0]

    def traded(parts, name):
        got = [parts[0]]
        for k in range(1, n_row):
            real = k in near_parts and name[-1] == "0"
            route = [(r, r ^ k) for r in range(n_row)]
            for r in range(n_row, n_row * comp_size):
                route.append((r, r ^ k if real else r ^ 1))
            got.append(lax.ppermute(parts[k], ("comp", "row"), route))
        return got

    def to_columns(x):
        near = [(i, i ^ 1) for i in range(n_col) if i ^ 1 < n_col]
        far = [(i, j) for i in range(n_col) for j in [((i + 1) ^ 1) - 1] if 0 <= j < n_col]
        ocean = [[(n_col + a, n_col + b) for a, b in pairs] for pairs in (near, far)]
        return [lax.ppermute(x, ("comp", "col"), pairs) for pairs in ocean]

    coeffs = [traded([send[c, k] for k in range(n_row)], f"there{c}") for c in range(chunks)]
    sides = to_columns(edge)

    pieces = (1, 3) if rows % 32 == 0 else (1,)
    share = rows // sum(pieces)
    surfaces = []

    def remap(index, after):
        first = sum(pieces[:index])
        piece = pl.BlockSpec((share, lanes), lambda i, s: (first + i, 0))
        earlier = surfaces[-1] if surfaces else ()
        surfaces.append(call(
            functools.partial(surface_kernel, first_piece=first, group=2), (pieces[index],),
            [smem, vmem, piece, piece] + [anywhere] * (len(earlier) + len(after)),
            [piece] * 2, [sds((rows, lanes), f32)] * 2,
            (counts, partner, own, remap_source[0], *earlier, *after),
            aliases={5 + i: i for i in range(len(earlier))},
            flops=10**10, size=3 * 4 * rows * lanes,
        ))

    remap(0, (edge,))

    def sweep(field, rows_in, cols_in, final, extra=()):
        out_shape = [sds((rows * levels, lanes), f32)]
        out_specs = [anywhere]
        scratch = [pltpu.VMEM(((block + 2) * levels, lanes), f32), pltpu.VMEM(edge_shape, f32)]
        if not final:
            out_shape += [sds(edge_shape, bf16), sds(ends_shape, bf16)]
            out_specs += [vmem, vmem]
            scratch += [pltpu.VMEM(edge_shape, f32)]
        return call(
            functools.partial(sweep_kernel, block=block, near_parts=near_parts, final=final),
            (1,),
            [smem, anywhere, vmem, vmem]
            + [pl.BlockSpec((1, levels, lanes), lambda i, s: (0, 0, 0))] * len(near_parts)
            + ([pl.BlockSpec((rows, lanes), lambda i, s: (0, 0))] if final else []),
            out_specs, out_shape,
            (counts, field, *cols_in, *(rows_in[k] for k in near_parts), *extra),
            scratch=scratch, size=2 * state_bytes,
        )

    first_step, edge, ends = sweep(mixed, coeffs[0], sides, False)
    sides = to_columns(edge)

    returned = []
    for chunk, width in enumerate(widths):
        with_ends = chunk == 0
        first_wave = sum(widths[:chunk])
        part = call(
            functools.partial(legendre_kernel, wave_dev=wave_dev, first_wave=first_wave, with_ends=with_ends),
            (),
            [anywhere] * (1 + n_row) + ([vmem, anywhere] if with_ends else []),
            [anywhere] * n_row,
            [sds((width, rows, lanes), bf16)] * n_row,
            (legendre, *coeffs[chunk], *([ends, surfaces[0][1]] if with_ends else [])),
            scratch=[pltpu.VMEM((n_row, rows, lanes), bf16), pltpu.SemaphoreType.DMA((n_row,))],
            flops=4 * width * legendre.shape[1] * legendre.shape[2] * lanes,
            size=2 * width * legendre.shape[1] * legendre.shape[2],
        )
        returned.append(traded(part, f"back{chunk}"))

    if len(pieces) > 1:
        remap(1, (first_step,))
    new_surface, gap = surfaces[-1]
    (sea,) = sweep(first_step, returned[0], sides, True, (gap,))

    state = call(
        functools.partial(exit_kernel, widths=widths, block=block), (),
        [anywhere] * (1 + n_row * chunks), anywhere, sds((rows * levels, lanes), f32),
        (sea, *sum(returned, [])), scratch=[pltpu.VMEM((256, 256), bf16)], size=2 * state_bytes, aliases={1: 0},
    )
    return state.reshape(model_state.shape), new_surface[None]


def solution(mesh):
    in_specs = (
        P("comp", "row", None, "col"),
        P("row", None, None),
        P("row"),
        P(),
        P("comp", "row", "col"),
        P("comp", "row", "col"),
        P("comp", "row", "col"),
    )
    out_specs = (P("comp", "row", None, "col"), P("comp", "row", "col"))

    return jax.shard_map(shards, mesh=mesh, in_specs=in_specs, out_specs=out_specs, check_vma=False)
```

```python
import functools

import jax
import jax.numpy as jnp
from jax import lax
from jax.experimental import pallas as pl
from jax.experimental.pallas import tpu as pltpu
from jax.sharding import PartitionSpec as P


diffusion_rate = 0.2
lanes = 128


def chunk_widths(wave_dev):
    return (wave_dev - wave_dev // 2, wave_dev // 2) if wave_dev > 1 else (wave_dev,)


def chunk_of(local, widths):
    chunk = 0
    while local >= widths[chunk]:
        local -= widths[chunk]
        chunk += 1
    return chunk, local


def row_block(rows):
    return 160 if rows % 160 == 0 else rows


def cost(flops, bytes_accessed):
    return pl.CostEstimate(flops=flops, bytes_accessed=bytes_accessed, transcendentals=0)


def where_am_i(place, n_row, n_col):
    flat = place[0]
    return (
        lax.div(flat, n_row * n_col),
        lax.rem(lax.div(flat, n_col), n_row),
        lax.rem(flat, n_col),
    )


def iota(shape, dim):
    return lax.broadcasted_iota(jnp.int32, shape, dim)


def as_bf16(mask):
    return jnp.where(mask, 1.0, 0.0).astype(jnp.bfloat16)


def swap_matrix(flip_high, flip_low):
    row, column = iota((256, 256), 0), iota((256, 256), 1)
    return as_bf16(column == (((row & 15) ^ flip_low) << 4 | ((row >> 4) ^ flip_high)))


def spread_matrix():
    row, column = iota((lanes, lanes), 0), iota((lanes, lanes), 1)
    odd = column & 1
    return as_bf16(((row == lanes - 1) & (odd == 0)) | ((row == 0) & (odd == 1)))


def beside_matrix():
    row, column = iota((lanes, lanes), 0), iota((lanes, lanes), 1)
    return as_bf16((row == column + 1) | (row + 1 == column))


def side_matrix():
    row, column = iota((lanes, lanes), 0), iota((lanes, lanes), 1)
    odd = row & 1
    return as_bf16(((column == 0) & (odd == 1)) | ((column == lanes - 1) & (odd == 0)))


def split(value):
    high = value.astype(jnp.bfloat16)
    return high, (value - high.astype(jnp.float32)).astype(jnp.bfloat16)


def product(a, b):
    return jnp.dot(a, b, preferred_element_type=jnp.float32)


def parts_of_half(half, n_row, wave_dev):
    return [k for k in range(n_row) if k * wave_dev // 16 == half]


def entry_kernel(place, counts, field, waves, gauss, mix, *rest, n_row, n_col, widths, block, half):
    levels = mix.shape[0]
    wave_dev = levels // n_row
    mine = parts_of_half(half, n_row, wave_dev)
    chunks = len(widths)
    total = len(mine) * chunks
    if half:
        send, (mixed, edge, ends, table, packed, sems) = rest[:total], rest[total:]
    else:
        ends, send, (table, sems) = rest[0], rest[1:1 + total], rest[1 + total:]
    comp, row, _ = where_am_i(place, n_row, n_col)
    tall = block * levels
    steps = field.shape[0] // tall
    state_block = pl.BlockSpec((tall, lanes), lambda i: (i, 0))
    flip = row * wave_dev
    first_parts = {k: send[n] for n, k in enumerate(mine)}

    def weigh(waves, *parts):
        step = pl.program_id(0)

        def target(wave):
            part, local = divmod(16 * half + wave, wave_dev)
            chunk, slot = chunk_of(local, widths)
            return parts[len(mine) * chunk + mine.index(part)], slot

        for lat in range(0, block, 16):
            size = min(16, block - lat)
            rows = jnp.concatenate([
                (waves[lat + s] * gauss[step * block + lat + s]).astype(jnp.bfloat16) for s in range(size)
            ], axis=0)
            if size == 16:
                swap = table[...]
            else:
                shape = (16 * size, 16 * size)
                line, column = iota(shape, 0), iota(shape, 1)
                swap = as_bf16(column == ((line & (size - 1)) << 4 | ((line // size) ^ (flip & 15))))
            turned = product(swap, rows).astype(jnp.bfloat16)
            for wave in range(16):
                out, slot = target(wave)
                out[slot, lat:lat + size, :] = turned[size * wave:size * (wave + 1), :]

    @pl.when(comp == 0)
    def _():
        table[...] = swap_matrix(flip & 15, 0)
        pltpu.emit_pipeline(
            weigh, grid=(steps,),
            in_specs=[pl.BlockSpec((block, pl.Squeezed(), 16, lanes), lambda i: (i, half ^ (flip >> 4), 0, 0))],
            out_specs=[pl.BlockSpec((w, block, lanes), lambda i: (0, i, 0)) for w in widths for _ in mine],
        )(waves, *send)

    if not half:
        @pl.when(comp != 0)
        def _():
            hand_on(ends, first_parts, row, sems)

        return

    def mixed_rows(ref, start, first_row):
        values = []
        for quarter in range(2):
            parts = []
            for pair in range(2):
                part = ref[pl.ds(start + (2 * quarter + pair) * 2 * levels, 2 * levels), :]
                values.append(part)
                parts.append(split(part))
            high = jnp.concatenate([p[0] for p in parts], axis=1)
            low = jnp.concatenate([p[1] for p in parts], axis=1)
            blend = product(table[0:2 * levels, :], jnp.concatenate([high, low, high, low], axis=0))
            values += [blend[:, :lanes], blend[:, lanes:]]
        out = []
        for s in range(8):
            quarter, pair, place_in = s // 4, s // 2 % 2, slice(levels * (s % 2), levels * (s % 2) + levels)
            heat = values[4 * quarter + pair][place_in]
            blend = values[4 * quarter + 2 + pair][place_in]
            sea = iota((levels, lanes), 1) < counts[0, first_row + s]
            value = heat + jnp.where(sea, blend, 0.0)
            out.append((value, jnp.where(sea, value, 0.0).astype(jnp.bfloat16)))
        return out

    @pl.when(comp != 0)
    def _():
        high, low = split(mix[...])
        repeat = as_bf16((iota((levels, 256), 1) & (levels - 1)) == iota((levels, 256), 0))
        wide = jnp.where(iota((levels, 256), 1) < 4 * levels, product(high, repeat), product(low, repeat))
        wide = jnp.concatenate([wide, wide], axis=0)
        shape = (2 * levels, 256)
        own = (iota(shape, 1) // levels & 1) == iota(shape, 0) // levels
        table[0:2 * levels, :] = jnp.where(own, wide, 0.0).astype(jnp.bfloat16)
        packed[...] = jnp.zeros_like(packed)
        batch = 32 if block % 32 == 0 else 8

        def blend(field, mixed):
            step = pl.program_id(0)
            spread = spread_matrix()

            def body(g, carry):
                base = step * block + g * batch
                rows = []
                for first in range(0, batch, 8):
                    start = pl.multiple_of((g * batch + first) * levels, 8 * levels)
                    some = mixed_rows(field, start, base + first)
                    for s, (value, _) in enumerate(some):
                        mixed[pl.ds(pl.multiple_of(start + s * levels, levels), levels), :] = value
                    rows += some
                pack(packed, base, [r[1] for r in rows], spread)
                return carry

            lax.fori_loop(0, block // batch, body, 0)

            @pl.when(step == 0)
            def _():
                ends[0] = mixed_rows(field, 0, 0)[0][1]

            @pl.when(step == steps - 1)
            def _():
                ends[1] = mixed_rows(field, tall - 8 * levels, steps * block - 8)[-1][1]

        pltpu.emit_pipeline(blend, grid=(steps,), in_specs=[state_block], out_specs=[state_block])(field, mixed)
        edge[...] = packed[...].astype(jnp.bfloat16)
        hand_on(ends, first_parts, row, sems)


def hand_on(ends, parts, row, sems):
    levels = ends.shape[1]
    copies = [
        pltpu.make_async_copy(
            ends.at[((k ^ row) > row).astype(jnp.int32)], part.at[0, pl.ds(0, levels)], sems.at[k])
        for k, part in parts.items() if k
    ]
    for copy in copies:
        copy.start()
    for copy in copies:
        copy.wait()


def pack(packed, base, rows, spread):
    levels = packed.shape[1]
    ends = product(jnp.concatenate(rows, axis=0), spread)
    pair_of = iota((levels, lanes), 1) >> 1
    slot = base >> 6
    kept = packed[slot]
    for s in range(len(rows)):
        kept = jnp.where(pair_of == (base & 63) + s, ends[s * levels:(s + 1) * levels], kept)
    packed[slot] = kept


def sweep_kernel(place, counts, field, east_in, west_in, *rest, block, n_row, n_col, near_parts, final):
    halos, rest = rest[:len(near_parts)], rest[len(near_parts):]
    if final:
        gap, out, masked, sides = rest
    else:
        out, edge, ends, masked, sides, packed = rest
    comp, row, col = where_am_i(place, n_row, n_col)
    levels = sides.shape[1]
    tall = block * levels
    rows = field.shape[0] // levels
    steps = rows // block
    shape = (levels, lanes)
    batch = 32 if block % 32 == 0 else 8

    @pl.when(comp != 0)
    def _():
        lane = iota(shape, 1)
        pair_of = lane >> 1

        def sea_of(y):
            return lane < counts[0, jnp.clip(y, 0, rows - 1)]

        def at(y):
            return pl.ds(pl.multiple_of(y * levels, levels), levels)

        def halo(neighbour):
            found = jnp.zeros(shape, jnp.float32)
            inside = (neighbour >= 0) & (neighbour < n_row)
            for part, ref in zip(near_parts, halos):
                found = jnp.where(inside & ((neighbour ^ row) == part), ref[0].astype(jnp.float32), found)
            return found

        for slot in range(sides.shape[0]):
            west = jnp.where(col > 0, west_in[slot].astype(jnp.float32), 0.0)
            east = jnp.where(col < n_col - 1, east_in[slot].astype(jnp.float32), 0.0)
            sides[slot] = jnp.where((lane & 1) == 0, pltpu.roll(east, lanes - 1, 1), pltpu.roll(west, 1, 1))
        if not final:
            packed[...] = jnp.zeros_like(packed)

        def advance(field, above, below, out):
            step = pl.program_id(0)
            base = step * block
            masked[0:levels, :] = jnp.where(step > 0, jnp.where(sea_of(base - 1), above[...], 0.0), halo(row - 1))
            masked[(block + 1) * levels:(block + 2) * levels, :] = jnp.where(
                step < steps - 1, jnp.where(sea_of(base + block), below[...], 0.0), halo(row + 1))

            def fill(g, carry):
                for s in range(8):
                    y = g * 8 + s
                    masked[at(y + 1), :] = jnp.where(sea_of(base + y), field[at(y), :], 0.0)
                return carry

            lax.fori_loop(0, block // 8, fill, 0)
            weights = jnp.concatenate([beside_matrix(), side_matrix()], axis=0)
            spread = spread_matrix()

            def body(g, carry):
                first = base + g * batch
                here = masked[pl.ds(pl.multiple_of((g * batch + 1) * levels, levels), batch * levels), :]
                beyond = sides[first >> 6]
                turned = jnp.concatenate(
                    [jnp.where(pair_of == (first & 63) + s, beyond, 0.0).astype(jnp.bfloat16) for s in range(batch)],
                    axis=0)
                near = product(jnp.concatenate([here.astype(jnp.bfloat16), turned], axis=1), weights)
                new_rows = []
                for s in range(batch):
                    y = g * batch + s
                    part = slice(s * levels, (s + 1) * levels)
                    lap = masked[at(y), :] + masked[at(y + 2), :] + near[part] - 4.0 * masked[at(y + 1), :]
                    sea = sea_of(base + y)
                    new = field[at(y), :] + jnp.where(sea, diffusion_rate * lap, 0.0)
                    out[at(y), :] = new
                    if final:
                        out[pl.ds(y * levels, 1), :] = new[0:1, :] + 0.3 * gap[pl.ds(base + y, 1), :]
                    else:
                        new_rows.append(jnp.where(sea, new, 0.0).astype(jnp.bfloat16))
                if not final:
                    pack(packed, first, new_rows, spread)
                return carry

            lax.fori_loop(0, block // batch, body, 0)
            if not final:
                @pl.when(step == 0)
                def _():
                    ends[0] = jnp.where(sea_of(0), out[0:levels, :], 0.0).astype(jnp.bfloat16)

                @pl.when(step == steps - 1)
                def _():
                    ends[1] = jnp.where(
                        sea_of(rows - 1), out[(block - 1) * levels:block * levels, :], 0.0
                    ).astype(jnp.bfloat16)

        state_block = pl.BlockSpec((tall, lanes), lambda i: (i, 0))
        pltpu.emit_pipeline(
            advance, grid=(steps,),
            in_specs=[
                state_block,
                pl.BlockSpec((levels, lanes), lambda i: (jnp.maximum(i * block - 1, 0), 0)),
                pl.BlockSpec((levels, lanes), lambda i: (jnp.minimum((i + 1) * block, rows - 1), 0)),
            ],
            out_specs=[state_block],
        )(field, field, field, out)
        if not final:
            edge[...] = packed[...].astype(jnp.bfloat16)


def legendre_kernel(place, legendre, *rest, n_row, n_col, wave_dev, first_wave, with_ends):
    coeffs, rest = rest[:n_row], rest[n_row:]
    if with_ends:
        ends, rest = rest[0], rest[2:]
    out, (gathered, sems) = rest[:n_row], rest[n_row:]
    comp, row, _ = where_am_i(place, n_row, n_col)
    waves, lats = coeffs[0].shape[:2]
    count = legendre.shape[2]

    def one_wave(legendre, *parts):
        coeffs, out = parts[:n_row], parts[n_row:]
        table = legendre[0]
        for part in range(n_row):
            gathered[part ^ row] = coeffs[part][0]
        fourier = gathered[...].reshape(n_row * lats, lanes)
        spectral = lax.dot_general(fourier, table, (((0,), (0,)), ((), ())), preferred_element_type=jnp.float32)
        wave = row * wave_dev + first_wave + pl.program_id(0)
        total = (wave + iota((1, count), 1)).astype(jnp.float32)
        ratio = total * (total + 1.0) / (1279.0 * 1280.0)
        damping = 1.0 / (1.0 + 20.0 * ratio * ratio)
        filtered = (spectral * damping).astype(jnp.bfloat16)
        result = lax.dot_general(table, filtered, (((1,), (1,)), ((), ())), preferred_element_type=jnp.float32)
        gathered[...] = result.astype(jnp.bfloat16).reshape(n_row, lats, lanes)
        for part in range(n_row):
            out[part][0] = gathered[part ^ row]

    @pl.when(comp == 0)
    def _():
        pieces = [pl.BlockSpec((1, lats, lanes), lambda i: (i, 0, 0))] * n_row
        pltpu.emit_pipeline(
            one_wave, grid=(waves,),
            in_specs=[pl.BlockSpec((1,) + legendre.shape[1:], lambda i: (first_wave + i, 0, 0))] + pieces,
            out_specs=pieces,
        )(legendre, *coeffs, *out)

    if with_ends:
        @pl.when(comp != 0)
        def _():
            hand_on(ends, dict(enumerate(out)), row, sems)


def surface_kernel(place, counts, partner, own, source, *rest, first_piece, group, n_row, n_col):
    new, gap = rest[-2:]
    first = (first_piece + pl.program_id(0)) * source.shape[0]
    half = partner.shape[0] // 2
    width = 2 * lanes
    table = jnp.concatenate(
        [partner[pl.ds(0, half, stride=2), :], partner[pl.ds(1, half, stride=2), :]], axis=1
    ).astype(jnp.bfloat16)
    low_index = iota((width, lanes), 0)
    high_index = iota((half, lanes), 0)
    one = jnp.ones((width, lanes), jnp.bfloat16)
    zero = jnp.zeros((width, lanes), jnp.bfloat16)
    sublane = iota((8, lanes), 0)
    rate = jnp.where(where_am_i(place, n_row, n_col)[0] == 0, 0.5, 0.25).astype(jnp.float32)

    def body(g, carry):
        start = pl.multiple_of(g * 8, 8)
        entries = source[pl.ds(start, 8), :]
        low = entries & (width - 1)
        high = entries >> 8
        found = []
        for p in range(0, 8, group):
            pick = jnp.concatenate(
                [jnp.where(low_index == low[s:s + 1, :], one, zero) for s in range(p, p + group)], axis=1
            )
            picked = product(table, pick)
            for s in range(group):
                part = picked[:, lanes * s:lanes * (s + 1)]
                match = high_index == high[p + s:p + s + 1, :]
                found.append(jnp.sum(jnp.where(match, part, 0.0), axis=0, keepdims=True))
        pulled = jnp.concatenate(found, axis=0)
        limit = jnp.zeros((8, lanes), jnp.int32)
        for s in range(8):
            limit = jnp.where(sublane == s, counts[0, first + start + s], limit)
        here = own[pl.ds(start, 8), :]
        difference = jnp.where(iota((8, lanes), 1) < limit, pulled - here, 0.0)
        new[pl.ds(start, 8), :] = here + rate * difference
        gap[pl.ds(start, 8), :] = difference
        return carry

    lax.fori_loop(0, source.shape[0] // 8, body, 0)


def exit_kernel(place, state, *rest, n_row, n_col, widths, block, half):
    chunks = len(widths)
    wave_dev = sum(widths)
    mine = parts_of_half(half, n_row, wave_dev)
    back, (out, table) = rest[:len(mine) * chunks], rest[len(mine) * chunks:]
    comp, row, _ = where_am_i(place, n_row, n_col)
    flip = row * wave_dev

    def turn(*refs):
        parts, out = refs[:-1], refs[-1]

        def source(wave, lat, size):
            part, local = divmod(16 * half + wave, wave_dev)
            chunk, slot = chunk_of(local, widths)
            return parts[len(mine) * chunk + mine.index(part)][slot, lat:lat + size, :]

        for lat in range(0, block, 16):
            size = min(16, block - lat)
            rows = [source(wave, lat, size) for wave in range(16)]
            if size == 16:
                swap, rows = table[...], jnp.concatenate(rows, axis=0)
            else:
                shape = (16 * size, 16 * size)
                line, column = iota(shape, 0), iota(shape, 1)
                swap = as_bf16(column == ((line & 15) ^ (flip & 15)) * size + (line >> 4))
                rows = jnp.concatenate([r.astype(jnp.float32) for r in rows], axis=0).astype(jnp.bfloat16)
            turned = product(swap, rows)
            for s in range(size):
                out[lat + s] = turned[16 * s:16 * s + 16, :]

    @pl.when(comp == 0)
    def _():
        table[...] = swap_matrix(0, flip & 15)
        pltpu.emit_pipeline(
            turn, grid=(out.shape[0] // block,),
            in_specs=[pl.BlockSpec((w, block, lanes), lambda i: (0, i, 0)) for w in widths for _ in mine],
            out_specs=[pl.BlockSpec((block, pl.Squeezed(), 16, lanes), lambda i: (i, half ^ (flip >> 4), 0, 0))],
        )(*back, out)


def shards(model_state, legendre, gauss_weight, mixing, surface, sea_count, remap_source):
    n_row, n_col = lax.axis_size("row"), lax.axis_size("col")
    rows, levels = model_state.shape[1], model_state.shape[2]
    wave_dev = levels // n_row
    widths = chunk_widths(wave_dev)
    chunks = len(widths)
    block = row_block(rows)
    f32, bf16 = jnp.float32, jnp.bfloat16
    sds = jax.ShapeDtypeStruct

    fields = model_state.reshape(rows * levels, lanes)
    counts = sea_count.reshape(1, rows)
    place = lax.axis_index(("comp", "row", "col")).astype(jnp.int32).reshape(1)
    own = surface[0]
    comp_size = lax.axis_size("comp")
    partner = lax.ppermute(own, "comp", [(i, comp_size - 1 - i) for i in range(comp_size)])

    slots = pl.cdiv(rows, 64)

    def call(kernel, grid, in_specs, out_specs, out_shape, args, scratch=(), vmem_limit=66800000, flops=10**7, size=0, aliases={}):
        return pl.pallas_call(
            functools.partial(kernel, n_row=n_row, n_col=n_col),
            out_shape=out_shape,
            grid_spec=pltpu.PrefetchScalarGridSpec(
                num_scalar_prefetch=1, grid=grid, in_specs=in_specs, out_specs=out_specs, scratch_shapes=scratch),
            compiler_params=pltpu.CompilerParams(vmem_limit_bytes=vmem_limit),
            input_output_aliases=aliases,
            cost_estimate=cost(flops, size),
        )(place, *args)

    smem = pl.BlockSpec(memory_space=pltpu.SMEM)
    anywhere = pl.BlockSpec(memory_space=pl.ANY)
    state_bytes = 4 * rows * levels * lanes
    vmem = pl.BlockSpec(memory_space=pltpu.VMEM)
    edge_shape = (slots, levels, lanes)
    ends_shape = (2, levels, lanes)
    send = {}
    wave_blocks = model_state.reshape(rows, levels // 16, 16, lanes)

    def enter(half, extra_in, extra_specs, extra_out, scratch):
        mine = parts_of_half(half, n_row, wave_dev)
        keys = [(c, k) for c in range(chunks) for k in mine]
        got = call(
            functools.partial(entry_kernel, widths=widths, block=block, half=half), (),
            [smem, anywhere, anywhere, smem, vmem] + [vmem] * len(extra_in),
            [anywhere] * len(keys) + extra_specs,
            [sds((widths[c], rows, lanes), bf16) for c, _ in keys] + extra_out,
            (counts, fields, wave_blocks, gauss_weight, mixing, *extra_in),
            scratch=[pltpu.VMEM((256, 256), bf16)] + scratch + [pltpu.SemaphoreType.DMA((n_row,))],
            size=state_bytes,
        )
        send.update(zip(keys, got))
        return got[len(keys):]

    mixed, edge, tile_ends = enter(
        1, [], [anywhere, vmem, vmem],
        [sds((rows * levels, lanes), f32), sds(edge_shape, bf16), sds(ends_shape, bf16)],
        [pltpu.VMEM(edge_shape, f32)])
    enter(0, [tile_ends], [], [], [])

    near_parts = [k for k in range(1, n_row) if k & (k + 1) == 0]

    def traded(parts, name):
        got = [parts[0]]
        for k in range(1, n_row):
            real = k in near_parts and name[-1] == "0"
            route = [(r, r ^ k) for r in range(n_row)]
            for r in range(n_row, n_row * comp_size):
                route.append((r, r ^ k if real else r ^ 1))
            got.append(lax.ppermute(parts[k], ("comp", "row"), route))
        return got

    chain = [n_col + i for i in range(n_col - 1)]

    def to_columns(x):
        return [
            lax.ppermute(x, ("comp", "col"), [(i + 1, i) for i in chain]),
            lax.ppermute(x, ("comp", "col"), [(i, i + 1) for i in chain]),
        ]

    coeffs = [traded([send[c, k] for k in range(n_row)], f"there{c}") for c in range(chunks)]
    sides = to_columns(edge)

    pieces = (1, 3) if rows % 32 == 0 else (1,)
    share = rows // sum(pieces)
    surfaces = []

    def remap(index, after):
        first = sum(pieces[:index])
        piece = pl.BlockSpec((share, lanes), lambda i, s: (first + i, 0))
        earlier = surfaces[-1] if surfaces else ()
        surfaces.append(call(
            functools.partial(surface_kernel, first_piece=first, group=2), (pieces[index],),
            [smem, vmem, piece, piece] + [anywhere] * (len(earlier) + len(after)),
            [piece] * 2, [sds((rows, lanes), f32)] * 2,
            (counts, partner, own, remap_source[0], *earlier, *after),
            aliases={5 + i: i for i in range(len(earlier))},
            flops=10**10, size=3 * 4 * rows * lanes,
        ))

    remap(0, (edge,))

    def sweep(field, rows_in, cols_in, final, extra=()):
        out_shape = [sds((rows * levels, lanes), f32)]
        out_specs = [anywhere]
        scratch = [pltpu.VMEM(((block + 2) * levels, lanes), f32), pltpu.VMEM(edge_shape, f32)]
        if not final:
            out_shape += [sds(edge_shape, bf16), sds(ends_shape, bf16)]
            out_specs += [vmem, vmem]
            scratch += [pltpu.VMEM(edge_shape, f32)]
        return call(
            functools.partial(sweep_kernel, block=block, near_parts=near_parts, final=final),
            (1,),
            [smem, anywhere, vmem, vmem]
            + [pl.BlockSpec((1, levels, lanes), lambda i, s: (0, 0, 0))] * len(near_parts)
            + ([pl.BlockSpec((rows, lanes), lambda i, s: (0, 0))] if final else []),
            out_specs, out_shape,
            (counts, field, *cols_in, *(rows_in[k] for k in near_parts), *extra),
            scratch=scratch, size=2 * state_bytes,
        )

    first_step, edge, ends = sweep(mixed, coeffs[0], sides, False)
    sides = to_columns(edge)

    returned = []
    for chunk, width in enumerate(widths):
        with_ends = chunk == 0
        first_wave = sum(widths[:chunk])
        part = call(
            functools.partial(legendre_kernel, wave_dev=wave_dev, first_wave=first_wave, with_ends=with_ends),
            (),
            [anywhere] * (1 + n_row) + ([vmem, anywhere] if with_ends else []),
            [anywhere] * n_row,
            [sds((width, rows, lanes), bf16)] * n_row,
            (legendre, *coeffs[chunk], *([ends, surfaces[0][1]] if with_ends else [])),
            scratch=[pltpu.VMEM((n_row, rows, lanes), bf16), pltpu.SemaphoreType.DMA((n_row,))],
            flops=4 * width * legendre.shape[1] * legendre.shape[2] * lanes,
            size=2 * width * legendre.shape[1] * legendre.shape[2],
        )
        returned.append(traded(part, f"back{chunk}"))

    if len(pieces) > 1:
        remap(1, (first_step,))
    new_surface, gap = surfaces[-1]
    (sea,) = sweep(first_step, returned[0], sides, True, (gap,))

    state = sea.reshape(rows, levels // 16, 16, lanes)
    for half in range(2):
        mine = parts_of_half(half, n_row, wave_dev)
        state = call(
            functools.partial(exit_kernel, widths=widths, block=block, half=half), (),
            [anywhere] * (1 + len(mine) * chunks), anywhere, sds(state.shape, f32),
            (state, *(returned[c][k] for c in range(chunks) for k in mine)),
            scratch=[pltpu.VMEM((256, 256), bf16)], size=state_bytes, aliases={1: 0},
        )
    return state.reshape(model_state.shape), new_surface[None]


def solution(mesh):
    in_specs = (
        P("comp", "row", None, "col"),
        P("row", None, None),
        P("row"),
        P(),
        P("comp", "row", "col"),
        P("comp", "row", "col"),
        P("comp", "row", "col"),
    )
    out_specs = (P("comp", "row", None, "col"), P("comp", "row", "col"))

    return jax.shard_map(shards, mesh=mesh, in_specs=in_specs, out_specs=out_specs, check_vma=False)
```
